32 devices in a mesh: grp: 4 (over x, core), dev: 8 (over z, y).
Axes of the slice: x: 2, y: 2, z: 4, core: 2. Of those that a mesh axis runs over, the one named last changes fastest.
Arguments:
- positions: float32 [3, 32768], P(None, ('grp', 'dev')), may hold values from -6 to 6
- rotations: float32 [9, 32768], P(None, ('grp', 'dev')), may hold values from -1 to 1, as said below
- clump_kind: int32 [32768], P(('grp', 'dev')), may hold values from 0 to 7
- sub_offsets: int32 [8, 3, 64], replicated, may hold values from -8 to 8
- pair_blocks: int32 [2, 32768], P(None, ('grp', 'dev')), may hold values from 0 to 16383, as said below
- pair_count: int32 [32], P(('grp', 'dev')), may hold values from 1 to 1024, as said below
Outputs:
- clump_force: float32 [3, 32768], P(None, ('grp', 'dev'))
- clump_torque: float32 [3, 32768], P(None, ('grp', 'dev'))
The draws below stay inside these ranges and needn't reach their ends.
Inputs may be any that keep to these rules, and one draw needn't show every extreme that they name: `rotations`: each column is a proper rotation matrix in row-major order. `pair_blocks`: the two blocks of a slot differ. A slot on a device of group g names as its first block one of group g's blocks (g * 4096 to (g + 1) * 4096 - 1) and as its second one of group g's blocks or of the 128 nearest blocks of groups g - 1 and g + 1, that is a block from g * 4096 - 128 to (g + 1) * 4096 + 127. `pair_count`: each device has at least one live slot.
All inputs are finite; a program needn't handle non-finite values.
Results may differ from the reference program's by a relative error of at most 0.0003.
Values sent between devices are 32-bit elements; how exact they have to be, the bound alone decides.
No kernel may reach another device: no remote copies, remote signals or barrier semaphores. Data moves between devices by JAX's collectives and lax.ppermute only.
A program may use at most 128 MiB of HBM per device.

```python
import jax
import jax.numpy as jnp
from jax import lax

SUBS = 64
NTYPES = 8
RIM = 128
PAIR_CAP = 1024
GROUPS = 4
MEMBERS = 8
GRP_BLOCKS = 4096
BLOCKS = 16384
CLUMPS = 32768
PAIRS = 32768


def draw_rotations(key, part):
    quats = jax.random.normal(key, (4, CLUMPS), jnp.float32)
    quats = quats / jnp.sqrt(jnp.sum(quats * quats, 0, keepdims=True) + 1e-12)
    real_part = quats[0]
    along_first = quats[1]
    along_second = quats[2]
    along_third = quats[3]
    rows_list = [1.0 - 2.0 * (along_second * along_second + along_third * along_third), 2.0 * (along_first * along_second - real_part * along_third), 2.0 * (along_first * along_third + real_part * along_second), 2.0 * (along_first * along_second + real_part * along_third), 1.0 - 2.0 * (along_first * along_first + along_third * along_third), 2.0 * (along_second * along_third - real_part * along_first), 2.0 * (along_first * along_third - real_part * along_second), 2.0 * (along_second * along_third + real_part * along_first), 1.0 - 2.0 * (along_first * along_first + along_second * along_second)]
    return jnp.stack(rows_list, 0).astype(jnp.float32)


def draw_pair_blocks(key, part):
    key_start, key_side, key_rim, key_step = jax.random.split(jax.random.fold_in(key, 11), 4)
    slot_ids = jnp.arange(PAIRS, dtype=jnp.int32)
    device_of = slot_ids // PAIR_CAP
    group_of = device_of // MEMBERS
    own_start = jax.random.randint(key_start, (PAIRS,), 0, GRP_BLOCKS, jnp.int32)
    side_pick = jax.random.randint(key_side, (PAIRS,), 0, 3, jnp.int32)
    rim_pick = jax.random.randint(key_rim, (PAIRS,), 0, RIM, jnp.int32)
    step_pick = jax.random.randint(key_step, (PAIRS,), 1, GRP_BLOCKS, jnp.int32)
    first_block = group_of * GRP_BLOCKS + own_start
    same_group = group_of * GRP_BLOCKS + (own_start + step_pick) % GRP_BLOCKS
    lower_rim = group_of * GRP_BLOCKS - 1 - rim_pick
    upper_rim = (group_of + 1) * GRP_BLOCKS + rim_pick
    go_lower = (side_pick == 0) & (group_of > 0)
    go_upper = (side_pick == 2) & (group_of < GROUPS - 1)
    second_block = jnp.where(go_lower, lower_rim, jnp.where(go_upper, upper_rim, same_group))
    first_block = first_block.at[0].set(0)
    second_block = second_block.at[0].set(1)
    last_slot = PAIRS - PAIR_CAP
    first_block = first_block.at[last_slot].set(BLOCKS - 2)
    second_block = second_block.at[last_slot].set(BLOCKS - 1)
    return jnp.stack([first_block, second_block], 0).astype(jnp.int32)


def draw_pair_count(key, part):
    key_base, key_hot = jax.random.split(jax.random.fold_in(key, 23), 2)
    device_total = GROUPS * MEMBERS
    base_count = jax.random.randint(key_base, (device_total,), max(PAIR_CAP // 8, 1), PAIR_CAP // 2 + 1, jnp.int32)
    hot_member = jax.random.randint(key_hot, (GROUPS,), 0, MEMBERS, jnp.int32)
    device_ids = jnp.arange(device_total, dtype=jnp.int32)
    is_hot = device_ids % MEMBERS == hot_member[device_ids // MEMBERS]
    return jnp.where(is_hot, PAIR_CAP, base_count).astype(jnp.int32)


def plant(entries, rng, low, high):
    index_at = [jax.random.randint(jax.random.fold_in(rng, axis), (), 0, length) for axis, length in enumerate(entries.shape)]
    main_axis = entries.shape.index(max(entries.shape))
    beside = index_at[:main_axis] + [(index_at[main_axis] + 1) % entries.shape[main_axis]] + index_at[main_axis + 1:]
    return entries.at[tuple(index_at)].set(low).at[tuple(beside)].set(high)


def block_levels(stream_key, extent, pieces, smallest, largest):
    def one(dim, shards_of):
        steps = jax.random.uniform(jax.random.fold_in(jax.random.fold_in(stream_key, 6), dim), (shards_of,), jnp.float32, smallest / len(pieces), largest / len(pieces))
        return jnp.repeat(jnp.exp(steps), extent[dim] // shards_of).reshape((-1,) + (1,) * (len(extent) - dim - 1))

    factor_of = one(*pieces[0])
    for cut in pieces[1:]:
        factor_of = factor_of * one(*cut)
    return factor_of


def centred(own_key, extent, width, limit, pieces=(), held_as=jnp.bfloat16):
    values = jax.random.normal(own_key, extent, jnp.float32) * width
    if len(pieces) > 0:
        values = block_levels(own_key, extent, pieces, -0.22, 0.18) * values
    return jnp.clip(values, min=-limit, max=limit).astype(held_as)


def setup_inputs(seed: int = 0) -> dict:
    key_list = jax.random.split(jax.random.key(seed), 7)
    return {
        "positions": centred(key_list[0], (3, CLUMPS), 1.0, 6.0, ((1, 32),), jnp.float32),
        "rotations": draw_rotations(jax.random.fold_in(key_list[6], 71), 0),
        "clump_kind": plant(jax.random.randint(key_list[2], (CLUMPS,), 0, NTYPES), jax.random.fold_in(key_list[2], 1), 0, NTYPES - 1).astype(jnp.int32),
        "sub_offsets": plant(jax.random.randint(key_list[3], (NTYPES, 3, SUBS), -8, 9), jax.random.fold_in(key_list[3], 1), -8, 8).astype(jnp.int32),
        "pair_blocks": draw_pair_blocks(jax.random.fold_in(key_list[6], 71), 0),
        "pair_count": draw_pair_count(jax.random.fold_in(key_list[6], 71), 0),
    }


OFFSET_UNIT = 0.125
REACH_SQUARED = 4.0
STIFFNESS = 1.0 / 256.0


def cross_axis(left_vec, right_vec):
    return jnp.stack([left_vec[1] * right_vec[2] - left_vec[2] * right_vec[1],
                      left_vec[2] * right_vec[0] - left_vec[0] * right_vec[2],
                      left_vec[0] * right_vec[1] - left_vec[1] * right_vec[0]], 0)


def place_blocks(centers, rotation_rows, onehot, offset_table):
    sub_count = offset_table.shape[1] // 3
    offsets = jnp.dot(onehot, offset_table, precision=lax.Precision.HIGHEST).reshape(-1, 3, sub_count)
    rotation_mats = rotation_rows.T.reshape(-1, 3, 3)
    world_pos = centers.T[:, :, None] + jnp.einsum("ckm,cms->cks", rotation_mats, offsets, precision=lax.Precision.HIGHEST)
    block_count = world_pos.shape[0] // 2
    return world_pos.reshape(block_count, 2, 3, sub_count).transpose(0, 2, 1, 3).reshape(block_count, 3, 2 * sub_count)


def contact(near_pos, far_pos):
    separation = near_pos[:, :, None] - far_pos[:, None, :]
    squared = jnp.sum(separation * separation, 0)
    weights = STIFFNESS * jnp.maximum(REACH_SQUARED - squared, 0.0)
    pushes = weights[None] * separation
    return jnp.sum(pushes, 2), -jnp.sum(pushes, 1)


def clump_moments(sphere_blocks, force_blocks, centers):
    block_count = sphere_blocks.shape[0]
    sub_count = sphere_blocks.shape[2] // 2
    spots = sphere_blocks.reshape(block_count, 3, 2, sub_count).transpose(1, 0, 2, 3)
    pushes = force_blocks.reshape(block_count, 3, 2, sub_count).transpose(1, 0, 2, 3)
    middle = centers.reshape(3, block_count, 2)[:, :, :, None]
    torque = jnp.sum(cross_axis(spots - middle, pushes), -1).reshape(3, 2 * block_count)
    total = jnp.sum(pushes, -1).reshape(3, 2 * block_count)
    return total, torque


def reference(positions, rotations, clump_kind, sub_offsets, pair_blocks, pair_count):
    kind_count = sub_offsets.shape[0]
    sub_count = sub_offsets.shape[2]
    offset_table = sub_offsets.astype(jnp.float32).reshape(kind_count, 3 * sub_count) * OFFSET_UNIT
    onehot = (clump_kind[:, None] == jnp.arange(kind_count, dtype=jnp.int32)[None, :]).astype(jnp.float32)
    spheres = place_blocks(positions, rotations, onehot, offset_table)
    slot_count = pair_blocks.shape[1]
    capacity = slot_count // pair_count.shape[0]
    slot_ids = jnp.arange(slot_count, dtype=jnp.int32)
    live_rows = ((slot_ids % capacity) < pair_count[slot_ids // capacity]).astype(jnp.float32)

    def visit_block(totals, packet):
        first_block, second_block, live_part = packet
        push_first, push_second = jax.vmap(contact)(spheres[first_block], spheres[second_block])
        weight_live = live_part[:, None, None]
        totals = totals.at[first_block].add(push_first * weight_live)
        totals = totals.at[second_block].add(push_second * weight_live)
        return totals, None

    packets = (pair_blocks[0].reshape(-1, 16), pair_blocks[1].reshape(-1, 16), live_rows.reshape(-1, 16))
    zero_table = jnp.zeros(spheres.shape, jnp.float32)
    sphere_force = lax.scan(visit_block, zero_table, packets)[0]
    clump_force, clump_torque = clump_moments(spheres, sphere_force, positions)
    return clump_force, clump_torque
```

```python
import functools

import jax
import jax.numpy as jnp
from jax import lax
from jax.experimental import pallas as pl
from jax.experimental.pallas import tpu as pltpu
from jax.sharding import PartitionSpec as P

RIM = 128
LANES = 128
OFFSET_UNIT = 0.125
REACH_SQUARED = 4.0
STIFFNESS = 1.0 / 256.0
CHUNK = 64
UNROLL = 4
FORM = 32
COMPS = 12


def cross_axis(left_vec, right_vec):
    return jnp.stack(
        [
            left_vec[1] * right_vec[2] - left_vec[2] * right_vec[1],
            left_vec[2] * right_vec[0] - left_vec[0] * right_vec[2],
            left_vec[0] * right_vec[1] - left_vec[1] * right_vec[0],
        ],
        0,
    )


def split3(value):
    high = value.astype(jnp.bfloat16).astype(jnp.float32)
    rest = value - high
    middle = rest.astype(jnp.bfloat16).astype(jnp.float32)
    return high, middle, rest - middle


def pair_kernel(
    members, slots, head_row,
    place_ref, *refs,
):
    piece_count = members // 2
    pieces = refs[:piece_count]
    (rim_ref, off_ref, inner_ref, edge_ref, table, lists, gathered, form_a, form_b, form_c,
     form_v, spots, acc, sems) = refs[piece_count:]
    along_z, along_y, group = place_ref[0], place_ref[1], place_ref[2]
    own_rows = pieces[0].shape[1] - head_row
    inner_blocks = members * own_rows * 4
    slot_rows = slots // LANES
    spots_of = LANES // 4

    copies = []
    owners = []
    for k in range(piece_count):
        for side in range(2):
            member = lax.rem(along_z - k + piece_count, piece_count) * 2 + (
                along_y if side == 0 else 1 - along_y
            )
            owners.append(member)
            copy = pltpu.make_async_copy(
                pieces[k].at[side, pl.ds(0, head_row + 8)], lists.at[member], sems.at[2 * k + side]
            )
            copy.start()
            copies.append(copy)

    def unpack(source, row, first):
        rows = source[pl.ds(row, 32), :]
        for sub in range(4):
            shifted = rows if sub == 0 else pltpu.roll(rows, LANES - 32 * sub, axis=1)
            table[pl.ds(pl.multiple_of(first + sub * 32, 32), 32), :] = shifted

    for k in range(piece_count):
        for side in range(2):
            base = owners[2 * k + side] * (own_rows * 4)

            def take(part, carry, k=k, side=side, base=base):
                unpack(
                    pieces[k].at[side],
                    pl.multiple_of(head_row + part * 32, 8),
                    base + part * LANES,
                )
                return carry

            lax.fori_loop(0, own_rows // 32, take, 0)
    for end in range(2):
        unpack(rim_ref, end * 32, inner_blocks + end * LANES)

    acc[...] = jnp.zeros_like(acc)
    form_a[...] = jnp.zeros_like(form_a)
    form_b[...] = jnp.zeros_like(form_b)
    form_c[...] = jnp.zeros_like(form_c)
    form_v[...] = jnp.zeros_like(form_v)
    ones = jnp.ones((CHUNK, LANES), jnp.float32)
    lane_wide = lax.broadcasted_iota(jnp.int32, (CHUNK, LANES), 1)
    low_half = (lane_wide < LANES // 2).astype(jnp.float32)
    high_half = 1.0 - low_half
    for row in range(3):
        form_a[pl.ds(21 + row, CHUNK, stride=FORM), :] = ones
        form_b[pl.ds(18 + row, CHUNK, stride=FORM), :] = ones
        form_c[pl.ds(24 + row, CHUNK, stride=FORM), :] = low_half
        form_c[pl.ds(28 + row, CHUNK, stride=FORM), :] = high_half

    for copy in copies:
        copy.wait()
    cumulative = [jnp.int32(0)]
    for member in range(members):
        count = lists[member, head_row, 15].astype(jnp.int32)
        cumulative.append(cumulative[-1] + count)
    total = cumulative[-1]
    me = along_z * 2 + along_y
    begin = (total * me) // members
    finish = (total * (me + 1)) // members

    group_base = group * inner_blocks
    lane = lax.broadcasted_iota(jnp.int32, (2 * CHUNK, LANES), 1)
    lane8 = lax.broadcasted_iota(jnp.int32, (24, LANES), 1)
    row_sum = lax.broadcasted_iota(jnp.int32, (3 * LANES, 2 * LANES), 0)
    col_sum = lax.broadcasted_iota(jnp.int32, (3 * LANES, 2 * LANES), 1)
    halves = (((row_sum & (LANES - 1)) >= LANES // 2) == (col_sum >= LANES)).astype(jnp.bfloat16)

    def local_block(value):
        block = value.astype(jnp.int32) - group_base
        block = jnp.where(
            block < 0,
            block + inner_blocks + LANES,
            jnp.where(block >= inner_blocks, block + LANES, block),
        )
        return block

    def table_row(block):
        return (block & ~(LANES - 1)) | ((block & 3) << 5) | ((block >> 2) & (spots_of - 1))

    def fetch(first):
        def step(turn, carry):
            for sub in range(4):
                index = turn * 4 + sub
                at = jnp.minimum(first + index, finish - 1)
                member = jnp.int32(0)
                before = jnp.int32(0)
                for other in range(1, members):
                    past = at >= cumulative[other]
                    member = member + past.astype(jnp.int32)
                    before = jnp.where(past, cumulative[other], before)
                slot = at - before
                near = local_block(lists[member, slot >> 7, slot & (LANES - 1)])
                far = local_block(lists[member, slot_rows + (slot >> 7), slot & (LANES - 1)])
                gathered[pl.ds(index, 1), :] = table[pl.ds(table_row(near), 1), :]
                gathered[pl.ds(CHUNK + index, 1), :] = table[pl.ds(table_row(far), 1), :]
                spots[0, index] = near
                spots[1, index] = far
            return carry

        lax.fori_loop(0, CHUNK // 4, step, 0)

    def arrange():
        packed = gathered[...]

        def both(column):
            even = jnp.broadcast_to(packed[:, column : column + 1], packed.shape)
            odd = jnp.broadcast_to(packed[:, 16 + column : 17 + column], packed.shape)
            return even, odd

        def spread(column):
            even, odd = both(column)
            return jnp.where(lane < LANES // 2, even, odd)

        kind_even, kind_odd = both(12)
        lane_f = lane.astype(jnp.float32)
        pick = jnp.where(
            ((lane < 8) & (kind_even == lane_f)) | ((lane >= 8) & (kind_odd == lane_f - 8.0)),
            1.0,
            0.0,
        ).astype(jnp.bfloat16)
        offsets = jnp.dot(pick, off_ref[...], preferred_element_type=jnp.float32)
        where_at = []
        for axis in range(3):
            value = spread(axis)
            for mode in range(3):
                value = value + spread(3 + 3 * axis + mode) * offsets[:, mode * LANES : (mode + 1) * LANES]
            where_at.append(value)
        near = [value[:CHUNK] for value in where_at]
        far = [value[CHUNK:] for value in where_at]
        near_sq = near[0] * near[0] + near[1] * near[1] + near[2] * near[2]
        far_sq = far[0] * far[0] + far[1] * far[1] + far[2] * far[2]

        def put(form, row, value):
            form[pl.ds(row, CHUNK, stride=FORM), :] = value

        for axis in range(3):
            parts = split3(near[axis])
            for place, part in enumerate((0, 0, 1, 1, 0, 2)):
                put(form_a, 3 * place + axis, parts[part] * 2.0)
            for part in range(3):
                put(form_c, 8 * part + axis, parts[part] * low_half)
                put(form_c, 8 * part + 4 + axis, parts[part] * high_half)
            parts = split3(far[axis])
            for place, part in enumerate((0, 1, 0, 1, 2, 0)):
                put(form_b, 3 * place + axis, parts[part])
            for turn in range(3):
                spot = (axis - turn + 3) % 3
                put(form_v, 8 * turn + spot, far[axis])
                put(form_v, 8 * turn + 4 + spot, far[axis])
        for part, value in enumerate(split3(REACH_SQUARED - near_sq)):
            put(form_a, 18 + part, value)
        for part, value in enumerate(split3(-far_sq)):
            put(form_b, 21 + part, value)

    def meet(index, first):
        at = pl.ds(pl.multiple_of(index * FORM, FORM), FORM)
        near = form_a[at, :].astype(jnp.bfloat16)
        far = form_b[at, :].astype(jnp.bfloat16)
        reach = lax.dot_general(
            near, far, (((0,), (0,)), ((), ())), preferred_element_type=jnp.float32
        )
        weight = jnp.maximum(reach, 0.0)
        weight_high = weight.astype(jnp.bfloat16)
        weight_low = (weight - weight_high.astype(jnp.float32)).astype(jnp.bfloat16)
        side = form_c[at, :].astype(jnp.bfloat16)
        sums = jnp.dot(
            jnp.concatenate([side, side], 1),
            jnp.concatenate([weight_high, weight_low], 0),
            preferred_element_type=jnp.float32,
        )
        spot = form_v[at, :]
        force = sums[24:32] * spot[0:8] - (sums[0:8] + sums[8:16] + sums[16:24])
        terms = jnp.concatenate([force, force * spot[8:16], force * spot[16:24]], 0)
        parts = split3(terms)
        joined = jnp.concatenate([part.astype(jnp.bfloat16) for part in parts], 1)
        folded = jnp.dot(joined, halves, preferred_element_type=jnp.float32)
        lower = folded[:, :LANES]
        upper = folded[:, LANES:]
        live = first + index < finish
        block = spots[0, index]
        own = jnp.where(live, block & (LANES - 1), -1)
        here = lane8 == own
        base = pl.multiple_of((block >> 7) * 72, 8)
        acc[pl.ds(base, 24), :] += jnp.where(here, lower + upper, 0.0)
        block = spots[1, index]
        own = jnp.where(live, block & (LANES - 1), -1)
        here = lane8 == own
        base = pl.multiple_of((block >> 7) * 72 + 24, 8)
        acc[pl.ds(base, 24), :] += jnp.where(here, lower, 0.0)
        base = pl.multiple_of((block >> 7) * 72 + 48, 8)
        acc[pl.ds(base, 24), :] += jnp.where(here, upper, 0.0)

    def chunk(turn, carry):
        first = begin + turn * CHUNK
        fetch(first)
        arrange()
        todo = jnp.minimum(finish - first, CHUNK)

        def step(turn, carry):
            for sub in range(UNROLL):
                meet(turn * UNROLL + sub, first)
            return carry

        lax.fori_loop(0, (todo + UNROLL - 1) // UNROLL, step, 0)
        return carry

    lax.fori_loop(0, (finish - begin + CHUNK - 1) // CHUNK, chunk, 0)

    def total_of(row, half, tiles, start):
        def get(which, line):
            return acc[pl.ds(start * 72 + which * 24 + line, tiles, stride=72), :]

        line = (row // 3) * 8 + row % 3
        mine = get(0, line + 4 * half)
        other = get(1 + half, line) + get(1 + half, line + 4)
        return (other - mine) * STIFFNESS

    for tiles, start, out in ((inner_blocks // LANES, 0, inner_ref), (2, inner_blocks // LANES, edge_ref)):
        for half in range(2):
            rows = [total_of(row, half, tiles, start) for row in range(9)]
            results = rows[0:3] + [rows[6 + (axis + 2) % 3] - rows[3 + (axis + 1) % 3] for axis in range(3)]
            for axis in range(6):
                out[pl.ds(6 * half + axis, tiles, stride=COMPS), :] = results[axis]


def neighbour_swap(rows_low, rows_high, axis):
    count = lax.axis_size(axis)
    index = lax.axis_index(axis)
    even = index % 2 == 0
    inside = [(i, i ^ 1) for i in range(count)]
    across = [(i, (i + 1) % count if i % 2 else (i - 1) % count) for i in range(count)]
    got_across = lax.ppermute(jnp.where(even, rows_low, rows_high), axis, across)
    got_inside = lax.ppermute(jnp.where(even, rows_high, rows_low), axis, inside)
    from_below = jnp.where(even, got_across, got_inside)
    from_above = jnp.where(even, got_inside, got_across)
    return from_below, from_above


def shards(positions, rotations, clump_kind, sub_offsets, pair_blocks, pair_count):
    members = lax.axis_size("dev")
    groups = lax.axis_size("grp")
    group = lax.axis_index("grp")
    me = lax.axis_index("dev")
    along_z, along_y = me // 2, me % 2
    rings = members // 2
    clumps = positions.shape[1]
    slots = pair_blocks.shape[1]
    own_blocks = clumps // 2
    kinds, _, subs = sub_offsets.shape
    head_row = 2 * slots // LANES

    values = jnp.concatenate(
        [
            positions,
            rotations,
            clump_kind.astype(jnp.float32)[None],
            jnp.zeros((3, clumps), jnp.float32),
        ],
        0,
    )
    values = values.T.reshape(own_blocks, 32)
    lane = lax.broadcasted_iota(jnp.int32, values.shape, 1)
    values = jnp.where(lane == 15, pair_count[0].astype(jnp.float32), values)
    packed = values.reshape(own_blocks // 4, LANES)
    payload = jnp.concatenate(
        [pair_blocks.astype(jnp.float32).reshape(head_row, LANES), packed], 0
    )

    pair_y = [(i, i ^ 1) for i in range(members)]
    both = jnp.stack([payload, lax.ppermute(payload, "dev", pair_y)])
    pieces = [both]
    for k in range(1, rings):
        pieces.append(
            lax.ppermute(both, "dev", [(i, (i + 2 * k) % members) for i in range(members)])
        )

    def piece_rows(member, start, count):
        z, y = member // 2, member % 2
        found = None
        for k in range(rings):
            rows = lax.dynamic_slice_in_dim(pieces[k], start, count, 1)
            side = jnp.where(along_y == y, rows[0], rows[1])
            hit = (along_z - k + rings) % rings == z
            found = side if found is None else jnp.where(hit, side, found)
        return found

    rim_rows = RIM // 4
    first_rows = piece_rows(0, head_row, rim_rows)
    last_rows = piece_rows(members - 1, head_row + packed.shape[0] - rim_rows, rim_rows)
    from_below, from_above = neighbour_swap(first_rows, last_rows, "grp")
    rims = jnp.concatenate([from_below, from_above], 0)

    offset_table = sub_offsets.astype(jnp.float32) * OFFSET_UNIT
    blank = jnp.zeros_like(offset_table)
    offset_rows = jnp.concatenate(
        [
            jnp.concatenate([offset_table, blank], 2).reshape(kinds, -1),
            jnp.concatenate([blank, offset_table], 2).reshape(kinds, -1),
        ],
        0,
    )
    offset_rows = jnp.concatenate(
        [offset_rows, jnp.zeros((LANES - 2 * kinds, offset_rows.shape[1]), jnp.float32)], 0
    ).astype(jnp.bfloat16)

    place = jnp.stack([along_z, along_y, group]).astype(jnp.int32)
    inner_blocks = own_blocks * members
    tiles = inner_blocks // LANES
    vmem = pl.BlockSpec(memory_space=pltpu.VMEM)
    inner, edge = pl.pallas_call(
        functools.partial(pair_kernel, members, slots, head_row),
        out_shape=(
            jax.ShapeDtypeStruct((tiles * COMPS, LANES), jnp.float32),
            jax.ShapeDtypeStruct((2 * COMPS, LANES), jnp.float32),
        ),
        in_specs=[pl.BlockSpec(memory_space=pltpu.SMEM)] + [vmem] * (rings + 2),
        out_specs=(vmem, vmem),
        scratch_shapes=[
            pltpu.VMEM((inner_blocks + 2 * RIM, LANES), jnp.float32),
            pltpu.SMEM((members, head_row + 8, LANES), jnp.float32),
            pltpu.VMEM((2 * CHUNK, LANES), jnp.float32),
            pltpu.VMEM((CHUNK * FORM, LANES), jnp.float32),
            pltpu.VMEM((CHUNK * FORM, LANES), jnp.float32),
            pltpu.VMEM((CHUNK * FORM, LANES), jnp.float32),
            pltpu.VMEM((CHUNK * FORM, LANES), jnp.float32),
            pltpu.SMEM((2, CHUNK), jnp.int32),
            pltpu.VMEM(((tiles + 2) * 72, LANES), jnp.float32),
            pltpu.SemaphoreType.DMA((members,)),
        ],
        name="pair_kernel",
    )(place, *pieces, rims, offset_rows)

    below, above = neighbour_swap(edge[:COMPS], edge[COMPS:], "grp")
    below = jnp.where(group > 0, below, 0.0)
    above = jnp.where(group < groups - 1, above, 0.0)
    inner = inner.at[:COMPS].add(below)
    inner = inner.at[(tiles - 1) * COMPS :].add(above)

    own_rows = tiles * COMPS // members
    ranks = inner.reshape(rings, 2, own_rows, LANES)
    mine = lax.dynamic_index_in_dim(ranks, along_y, 1, False)
    other = lax.dynamic_index_in_dim(ranks, 1 - along_y, 1, False)
    column = mine + lax.ppermute(other, "dev", pair_y)
    summed = lax.dynamic_index_in_dim(column, along_z, 0, False)
    for k in range(1, rings):
        part = lax.dynamic_index_in_dim(column, (along_z + k) % rings, 0, False)
        summed = summed + lax.ppermute(
            part, "dev", [(i, (i + 2 * k) % members) for i in range(members)]
        )
    summed = summed.reshape(own_blocks // LANES, 2, 6, LANES).transpose(2, 0, 3, 1).reshape(6, clumps)
    clump_force = summed[0:3]
    clump_torque = summed[3:6] - cross_axis(positions, clump_force)
    return (clump_force, clump_torque)


def solution(mesh):
    placed = (
        P(None, ("grp", "dev")),
        P(None, ("grp", "dev")),
        P(("grp", "dev")),
        P(),
        P(None, ("grp", "dev")),
        P(("grp", "dev")),
    )
    return jax.shard_map(
        shards,
        mesh=mesh,
        in_specs=placed,
        out_specs=(P(None, ("grp", "dev")), P(None, ("grp", "dev"))),
        check_vma=False,
    )
```

```python
import functools

import jax
import jax.numpy as jnp
from jax import lax
from jax.experimental import pallas as pl
from jax.experimental.pallas import tpu as pltpu
from jax.sharding import PartitionSpec as P

RIM = 128
LANES = 128
OFFSET_UNIT = 0.125
REACH_SQUARED = 4.0
STIFFNESS = 1.0 / 256.0
CHUNK = 64
UNROLL = 1
COMPS = 12


def cross_axis(left_vec, right_vec):
    return jnp.stack(
        [
            left_vec[1] * right_vec[2] - left_vec[2] * right_vec[1],
            left_vec[2] * right_vec[0] - left_vec[0] * right_vec[2],
            left_vec[0] * right_vec[1] - left_vec[1] * right_vec[0],
        ],
        0,
    )


def split3(value):
    high = value.astype(jnp.bfloat16).astype(jnp.float32)
    rest = value - high
    middle = rest.astype(jnp.bfloat16).astype(jnp.float32)
    return high, middle, rest - middle


def pair_kernel(members, slots, head_row, place_ref, *refs):
    piece_count = members // 2
    pieces = refs[:piece_count]
    (rim_ref, off_ref, inner_ref, edge_ref, table, list_words, lists, order_words, order, gathered,
     parts, spots, acc, sems) = refs[piece_count:]
    along_z, along_y = place_ref[0], place_ref[1]
    own_rows = pieces[0].shape[1] - head_row
    inner_blocks = members * own_rows * 4
    list_rows = head_row + 8

    copies = []
    owners = []
    for k in range(piece_count):
        for side in range(2):
            member = lax.rem(along_z - k + piece_count, piece_count) * 2 + (
                along_y if side == 0 else 1 - along_y
            )
            owners.append(member)
            at = pl.ds(pl.multiple_of(member * list_rows, 8), list_rows)
            list_words[at, :] = pieces[k][side, pl.ds(0, list_rows), :].astype(jnp.int32)
    copy = pltpu.make_async_copy(list_words, lists, sems.at[0])
    copy.start()

    def unpack(source, row, first):
        rows = source[pl.ds(row, 32), :]
        for sub in range(4):
            shifted = rows if sub == 0 else pltpu.roll(rows, LANES - 32 * sub, axis=1)
            table[pl.ds(pl.multiple_of(first + sub * 32, 32), 32), :] = shifted

    for k in range(piece_count):
        for side in range(2):
            base = owners[2 * k + side] * (own_rows * 4)

            def take(part, carry, k=k, side=side, base=base):
                unpack(
                    pieces[k].at[side],
                    pl.multiple_of(head_row + part * 32, 8),
                    base + part * LANES,
                )
                return carry

            lax.fori_loop(0, own_rows // 32, take, 0)
    for end in range(2):
        unpack(rim_ref, end * 32, inner_blocks + end * LANES)

    def clear(turn, carry):
        acc[pl.ds(pl.multiple_of(turn * 144, 8), 144), :] = jnp.zeros((144, LANES), jnp.float32)
        return carry

    lax.fori_loop(0, acc.shape[0] // 144, clear, 0)

    copy.wait()
    counts = [lists[member * list_rows + head_row, 15] for member in range(members)]
    total = functools.reduce(lambda left, right: left + right, counts)
    me = along_z * 2 + along_y
    begin = (total * me) // members
    finish = (total * (me + 1)) // members
    number = finish - begin

    wide = order_words.shape[0]
    at = lax.broadcasted_iota(jnp.int32, (wide, LANES), 0) * LANES + lax.broadcasted_iota(
        jnp.int32, (wide, LANES), 1
    )
    at = jnp.minimum(at + begin, finish - 1)
    address = at
    passed = jnp.int32(0)
    for member in range(members - 1):
        passed = passed + counts[member]
        address = address + jnp.where(at >= passed, list_rows * LANES - counts[member], 0)
    order_words[...] = address
    copy = pltpu.make_async_copy(order_words, order, sems.at[1])
    copy.start()
    copy.wait()

    lane = lax.broadcasted_iota(jnp.int32, (2 * CHUNK, LANES), 1)
    column_of = jnp.where(lane < LANES // 2, 0, 16)
    lane_f = (lane & 7).astype(jnp.float32)
    pick_low = lane < 8
    pick_all = lane < 16
    lane24 = lax.broadcasted_iota(jnp.int32, (24, LANES), 1)
    row8 = lax.broadcasted_iota(jnp.int32, (8, LANES), 0)
    lane8 = lax.broadcasted_iota(jnp.int32, (8, LANES), 1)
    row_first = (row8 & 3) == 0
    row_second = (row8 & 3) == 1
    half8 = (row8 < 4) == (lane8 < LANES // 2)
    ones_half = jnp.where(half8, 1.0, 0.0)
    row_sum = lax.broadcasted_iota(jnp.int32, (2 * LANES, 2 * LANES), 0)
    col_sum = lax.broadcasted_iota(jnp.int32, (2 * LANES, 2 * LANES), 1)
    halves = jnp.where(
        ((row_sum & (LANES - 1)) >= LANES // 2) == (col_sum >= LANES), 1.0, 0.0
    ).astype(jnp.bfloat16)
    row16 = lax.broadcasted_iota(jnp.int32, (16, LANES), 0)
    keeps = [jnp.where((row16 & 7) == sub, 1.0, 0.0).astype(jnp.bfloat16) for sub in range(8)]

    def fetch(first):
        def step(turn, carry):
            for sub in range(8):
                index = turn * 8 + sub
                spot = jnp.minimum(first + index, slots - 1)
                word = order[spot >> 7, spot & (LANES - 1)]
                near = lists[word >> 7, word & (LANES - 1)]
                far = lists[(word >> 7) + head_row // 2, word & (LANES - 1)]
                gathered[pl.ds(index, 1), :] = table[pl.ds(near, 1), :]
                gathered[pl.ds(CHUNK + index, 1), :] = table[pl.ds(far, 1), :]
                spots[0, index] = near
                spots[1, index] = far
            return carry

        lax.fori_loop(0, CHUNK // 8, step, 0)

    def keep_part(slot, value):
        parts[pl.ds(slot * CHUNK, CHUNK), :] = value

    def arrange():
        packed = gathered[...]

        def spread(column):
            return jnp.take_along_axis(
                packed, column_of + column, axis=1, mode="promise_in_bounds"
            )

        kind_low = jnp.take_along_axis(
            packed, jnp.where(pick_low, 12, 28), axis=1, mode="promise_in_bounds"
        )
        pick = jnp.where(pick_all & (kind_low == lane_f), 1.0, 0.0).astype(jnp.bfloat16)
        offsets = jnp.dot(pick, off_ref[...], preferred_element_type=jnp.float32)
        where_at = []
        for axis in range(3):
            value = spread(axis)
            for mode in range(3):
                value = value + spread(3 + 3 * axis + mode) * offsets[:, mode * LANES : (mode + 1) * LANES]
            where_at.append(value)
        near = [value[:CHUNK] for value in where_at]
        far = [value[CHUNK:] for value in where_at]
        near_sq = near[0] * near[0] + near[1] * near[1] + near[2] * near[2]
        far_sq = far[0] * far[0] + far[1] * far[1] + far[2] * far[2]
        for axis, value in enumerate(near + [REACH_SQUARED - near_sq]):
            for part, piece in enumerate(split3(value)):
                keep_part(4 * part + axis, piece)
        for axis, value in enumerate([2.0 * value for value in far] + [-far_sq]):
            for part, piece in enumerate(split3(value)):
                keep_part(12 + 4 * part + axis, piece)
        for axis in range(3):
            keep_part(24 + axis, far[axis])

    one8 = jnp.ones((8, LANES), jnp.float32)

    def choose(first, second, third):
        return jnp.where(row_first, first, jnp.where(row_second, second, third))

    def octet(group, first):
        base = pl.multiple_of(group * 8, 8)

        def part(slot):
            return parts[pl.ds(slot * CHUNK + base, 8), :]

        near = [[part(4 * which + axis) for axis in range(4)] for which in range(3)]
        far = [[part(12 + 4 * which + axis) for axis in range(4)] for which in range(3)]
        rows_a, rows_b = [], []
        for a, b, a_last, b_last in (
            (0, 0, near[0][3], one8),
            (0, 1, one8, far[1][3]),
            (1, 0, near[1][3], one8),
            (1, 1, one8, far[0][3]),
            (0, 2, one8, far[2][3]),
            (2, 0, near[2][3], one8),
        ):
            rows_a += near[a][:3] + [a_last]
            rows_b += far[b][:3] + [b_last]
        all_a = jnp.concatenate(rows_a, 0).astype(jnp.bfloat16)
        tiles_b = [
            jnp.concatenate(rows_b[2 * tile : 2 * tile + 2], 0).astype(jnp.bfloat16)
            for tile in range(12)
        ]
        terms = []
        for couple in range(4):
            pair = (2 * couple, 2 * couple + 1)
            side_b = jnp.concatenate(
                [
                    jnp.concatenate([tile * keeps[sub] for tile in tiles_b], 0)
                    for sub in pair
                ],
                1,
            )
            reach = lax.dot_general(
                all_a, side_b, (((0,), (0,)), ((), ())), preferred_element_type=jnp.float32
            )
            weight = jnp.maximum(reach, 0.0)
            weight_high = weight.astype(jnp.bfloat16)
            weight_low = (weight - weight_high.astype(jnp.float32)).astype(jnp.bfloat16)
            side_c = []
            for sub in pair:
                def repeated(slot, sub=sub):
                    return parts[pl.ds(slot * CHUNK + base + sub, 8, stride=0), :]

                for which in range(3):
                    row = choose(*[repeated(4 * which + axis) for axis in range(3)])
                    side_c.append(jnp.where(half8, row, 0.0))
                side_c.append(ones_half)
            side_c = jnp.concatenate(side_c, 0).astype(jnp.bfloat16)
            sums = jnp.dot(
                jnp.concatenate([side_c, side_c], 1),
                jnp.concatenate([weight_high, weight_low], 0),
                preferred_element_type=jnp.float32,
            )
            for place, sub in enumerate(pair):
                mine = sums[32 * place : 32 * place + 32, LANES * place : LANES * place + LANES]
                axes = [
                    parts[pl.ds((24 + axis) * CHUNK + base + sub, 8, stride=0), :]
                    for axis in range(3)
                ]
                force = mine[24:32] * choose(*axes) - (mine[0:8] + mine[8:16] + mine[16:24])
                terms += [
                    force,
                    force * choose(axes[1], axes[2], axes[0]),
                    force * choose(axes[2], axes[0], axes[1]),
                ]
        terms = jnp.concatenate(terms, 0)
        terms_high = terms.astype(jnp.bfloat16)
        terms_low = (terms - terms_high.astype(jnp.float32)).astype(jnp.bfloat16)
        folded = jnp.dot(
            jnp.concatenate([terms_high, terms_low], 1), halves, preferred_element_type=jnp.float32
        )
        for sub in range(8):
            lower = folded[24 * sub : 24 * sub + 24, :LANES]
            upper = folded[24 * sub : 24 * sub + 24, LANES:]
            index = base + sub
            live = first + index < number
            block = spots[0, index]
            here = lane24 == jnp.where(live, block & (LANES - 1), -1)
            at = pl.multiple_of((block >> 7) * 72, 8)
            acc[pl.ds(at, 24), :] += jnp.where(here, lower + upper, 0.0)
            block = spots[1, index]
            here = lane24 == jnp.where(live, block & (LANES - 1), -1)
            at = pl.multiple_of((block >> 7) * 72 + 24, 8)
            acc[pl.ds(at, 24), :] += jnp.where(here, lower, 0.0)
            at = pl.multiple_of((block >> 7) * 72 + 48, 8)
            acc[pl.ds(at, 24), :] += jnp.where(here, upper, 0.0)

    def chunk(turn, carry):
        first = turn * CHUNK
        fetch(first)
        arrange()
        todo = jnp.minimum(number - first, CHUNK)

        def step(turn, carry):
            for sub in range(UNROLL):
                octet(turn * UNROLL + sub, first)
            return carry

        lax.fori_loop(0, (todo + 8 * UNROLL - 1) // (8 * UNROLL), step, 0)
        return carry

    lax.fori_loop(0, (number + CHUNK - 1) // CHUNK, chunk, 0)

    def total_of(row, half, tiles, start):
        def get(which, line):
            return acc[pl.ds(start * 72 + which * 24 + line, tiles, stride=72), :]

        line = (row // 3) * 8 + row % 3
        mine = get(0, line + 4 * half)
        other = get(1 + half, line) + get(1 + half, line + 4)
        return (other - mine) * STIFFNESS

    for tiles, start, out in ((inner_blocks // LANES, 0, inner_ref), (2, inner_blocks // LANES, edge_ref)):
        for half in range(2):
            rows = [total_of(row, half, tiles, start) for row in range(9)]
            results = rows[0:3] + [rows[6 + (axis + 2) % 3] - rows[3 + (axis + 1) % 3] for axis in range(3)]
            for axis in range(6):
                out[pl.ds(6 * half + axis, tiles, stride=COMPS), :] = results[axis]


def neighbour_swap(rows_low, rows_high, axis):
    count = lax.axis_size(axis)
    index = lax.axis_index(axis)
    even = index % 2 == 0
    inside = [(i, i ^ 1) for i in range(count)]
    across = [(i, (i + 1) % count if i % 2 else (i - 1) % count) for i in range(count)]
    got_across = lax.ppermute(jnp.where(even, rows_low, rows_high), axis, across)
    got_inside = lax.ppermute(jnp.where(even, rows_high, rows_low), axis, inside)
    from_below = jnp.where(even, got_across, got_inside)
    from_above = jnp.where(even, got_inside, got_across)
    return from_below, from_above


def shards(positions, rotations, clump_kind, sub_offsets, pair_blocks, pair_count):
    members = lax.axis_size("dev")
    groups = lax.axis_size("grp")
    group = lax.axis_index("grp")
    me = lax.axis_index("dev")
    along_z, along_y = me // 2, me % 2
    rings = members // 2
    clumps = positions.shape[1]
    slots = pair_blocks.shape[1]
    own_blocks = clumps // 2
    kinds, _, subs = sub_offsets.shape
    head_row = 2 * slots // LANES

    values = jnp.concatenate(
        [
            positions,
            rotations,
            clump_kind.astype(jnp.float32)[None],
            jnp.zeros((3, clumps), jnp.float32),
        ],
        0,
    )
    values = values.T.reshape(own_blocks, 32)
    lane = lax.broadcasted_iota(jnp.int32, values.shape, 1)
    values = jnp.where(lane == 15, pair_count[0].astype(jnp.float32), values)
    packed = (
        values.reshape(own_blocks // LANES, 4, 32, 32)
        .transpose(0, 2, 1, 3)
        .reshape(own_blocks // 4, LANES)
    )
    inner_blocks = own_blocks * members
    blocks = pair_blocks - group * inner_blocks
    blocks = jnp.where(
        blocks < 0,
        blocks + inner_blocks + RIM,
        jnp.where(blocks >= inner_blocks, blocks + RIM, blocks),
    )
    payload = jnp.concatenate([blocks.astype(jnp.float32).reshape(head_row, LANES), packed], 0)

    pair_y = [(i, i ^ 1) for i in range(members)]
    both = jnp.stack([payload, lax.ppermute(payload, "dev", pair_y)])
    pieces = [both]
    for k in range(1, rings):
        pieces.append(
            lax.ppermute(both, "dev", [(i, (i + 2 * k) % members) for i in range(members)])
        )

    def piece_rows(member, start, count):
        z, y = member // 2, member % 2
        found = None
        for k in range(rings):
            rows = lax.dynamic_slice_in_dim(pieces[k], start, count, 1)
            side = jnp.where(along_y == y, rows[0], rows[1])
            hit = (along_z - k + rings) % rings == z
            found = side if found is None else jnp.where(hit, side, found)
        return found

    rim_rows = RIM // 4
    first_rows = piece_rows(0, head_row, rim_rows)
    last_rows = piece_rows(members - 1, head_row + packed.shape[0] - rim_rows, rim_rows)
    from_below, from_above = neighbour_swap(first_rows, last_rows, "grp")
    rims = jnp.concatenate([from_below, from_above], 0)

    offset_table = sub_offsets.astype(jnp.float32) * OFFSET_UNIT
    blank = jnp.zeros_like(offset_table)
    offset_rows = jnp.concatenate(
        [
            jnp.concatenate([offset_table, blank], 2).reshape(kinds, -1),
            jnp.concatenate([blank, offset_table], 2).reshape(kinds, -1),
        ],
        0,
    )
    offset_rows = jnp.concatenate(
        [offset_rows, jnp.zeros((LANES - 2 * kinds, offset_rows.shape[1]), jnp.float32)], 0
    ).astype(jnp.bfloat16)

    place = jnp.stack([along_z, along_y, group]).astype(jnp.int32)
    tiles = inner_blocks // LANES
    vmem = pl.BlockSpec(memory_space=pltpu.VMEM)
    inner, edge = pl.pallas_call(
        functools.partial(pair_kernel, members, slots, head_row),
        out_shape=(
            jax.ShapeDtypeStruct((tiles * COMPS, LANES), jnp.float32),
            jax.ShapeDtypeStruct((2 * COMPS, LANES), jnp.float32),
        ),
        in_specs=[pl.BlockSpec(memory_space=pltpu.SMEM)] + [vmem] * (rings + 2),
        out_specs=(vmem, vmem),
        scratch_shapes=[
            pltpu.VMEM((inner_blocks + 2 * RIM, LANES), jnp.float32),
            pltpu.VMEM((members * (head_row + 8), LANES), jnp.int32),
            pltpu.SMEM((members * (head_row + 8), LANES), jnp.int32),
            pltpu.VMEM((slots // LANES, LANES), jnp.int32),
            pltpu.SMEM((slots // LANES, LANES), jnp.int32),
            pltpu.VMEM((2 * CHUNK, LANES), jnp.float32),
            pltpu.VMEM((27 * CHUNK, LANES), jnp.float32),
            pltpu.SMEM((2, CHUNK), jnp.int32),
            pltpu.VMEM(((tiles + 2) * 72, LANES), jnp.float32),
            pltpu.SemaphoreType.DMA((2,)),
        ],
        name="pair_kernel",
    )(place, *pieces, rims, offset_rows)

    below, above = neighbour_swap(edge[:COMPS], edge[COMPS:], "grp")
    below = jnp.where(group > 0, below, 0.0)
    above = jnp.where(group < groups - 1, above, 0.0)
    inner = inner.at[:COMPS].add(below)
    inner = inner.at[(tiles - 1) * COMPS :].add(above)

    own_rows = tiles * COMPS // members
    ranks = inner.reshape(rings, 2, own_rows, LANES)
    mine = lax.dynamic_index_in_dim(ranks, along_y, 1, False)
    other = lax.dynamic_index_in_dim(ranks, 1 - along_y, 1, False)
    column = mine + lax.ppermute(other, "dev", pair_y)
    summed = lax.dynamic_index_in_dim(column, along_z, 0, False)
    for k in range(1, rings):
        part = lax.dynamic_index_in_dim(column, (along_z + k) % rings, 0, False)
        summed = summed + lax.ppermute(
            part, "dev", [(i, (i + 2 * k) % members) for i in range(members)]
        )
    summed = summed.reshape(own_blocks // LANES, 2, 6, LANES).transpose(2, 0, 3, 1).reshape(6, clumps)
    clump_force = summed[0:3]
    clump_torque = summed[3:6] - cross_axis(positions, clump_force)
    return (clump_force, clump_torque)


def solution(mesh):
    placed = (
        P(None, ("grp", "dev")),
        P(None, ("grp", "dev")),
        P(("grp", "dev")),
        P(),
        P(None, ("grp", "dev")),
        P(("grp", "dev")),
    )
    return jax.shard_map(
        shards,
        mesh=mesh,
        in_specs=placed,
        out_specs=(P(None, ("grp", "dev")), P(None, ("grp", "dev"))),
        check_vma=False,
    )
```

```python
import functools

import jax
import jax.numpy as jnp
from jax import lax
from jax.experimental import pallas as pl
from jax.experimental.pallas import tpu as pltpu
from jax.sharding import PartitionSpec as P

RIM = 128
LANES = 128
OFFSET_UNIT = 0.125
REACH_SQUARED = 4.0
STIFFNESS = 1.0 / 256.0
CHUNK = 64
COMPS = 12
DEPTH = 2


def cross_axis(left_vec, right_vec):
    return jnp.stack(
        [
            left_vec[1] * right_vec[2] - left_vec[2] * right_vec[1],
            left_vec[2] * right_vec[0] - left_vec[0] * right_vec[2],
            left_vec[0] * right_vec[1] - left_vec[1] * right_vec[0],
        ],
        0,
    )


def split3(value):
    high = value.astype(jnp.bfloat16).astype(jnp.float32)
    rest = value - high
    middle = rest.astype(jnp.bfloat16).astype(jnp.float32)
    return high, middle, rest - middle


def pair_kernel(members, slots, head_row, place_ref, *refs):
    piece_count = members // 2
    pieces = refs[:piece_count]
    (rim_ref, off_ref, inner_ref, edge_ref, table, word_ref, words, gathered,
     parts, reach_ref, sums_ref, folded_ref, acc_near, acc_far, sem) = refs[piece_count:]
    along_z, along_y = place_ref[0], place_ref[1]
    own_rows = pieces[0].shape[1] - head_row
    inner_blocks = members * own_rows * 4
    slot_rows = head_row // 2

    owners = []
    for k in range(piece_count):
        for side in range(2):
            owners.append(
                lax.rem(along_z - k + piece_count, piece_count) * 2
                + (along_y if side == 0 else 1 - along_y)
            )
    before = [jnp.int32(0)]
    for member in range(members):
        before.append(before[-1] + place_ref[2 + member])
    total = before[-1]
    me = along_z * 2 + along_y
    begin = (total * me) // members
    finish = (total * (me + 1)) // members
    number = finish - begin

    flat = lax.broadcasted_iota(jnp.int32, (slot_rows, LANES), 0) * LANES
    column = lax.broadcasted_iota(jnp.int32, (slot_rows, LANES), 1)
    flat = flat + column
    near_list = jnp.zeros((slot_rows, LANES), jnp.float32)
    far_list = jnp.zeros((slot_rows, LANES), jnp.float32)
    for k in range(piece_count):
        for side in range(2):
            member = owners[2 * k + side]
            start = jnp.int32(0)
            for other in range(members):
                start = start + jnp.where(other < member, place_ref[2 + other], 0)
            low = jnp.maximum(start, begin) - begin
            high = jnp.minimum(start + place_ref[2 + member], finish) - begin
            shift = jnp.bitwise_and(start - begin, slots - 1)
            wanted = (flat >= low) & (flat < high)

            def moved(rows):
                turned = pltpu.roll(rows, shift & (LANES - 1), axis=1)
                same = pltpu.roll(turned, shift >> 7, axis=0)
                following = pltpu.roll(turned, (shift >> 7) + 1, axis=0)
                return jnp.where(column < (shift & (LANES - 1)), following, same)

            near_list = jnp.where(wanted, moved(pieces[k][side, pl.ds(0, slot_rows), :]), near_list)
            far_list = jnp.where(
                wanted, moved(pieces[k][side, pl.ds(slot_rows, slot_rows), :]), far_list
            )
    word_ref[pl.ds(0, slot_rows), :] = near_list.astype(jnp.int32)
    word_ref[pl.ds(slot_rows, slot_rows), :] = far_list.astype(jnp.int32)
    copy = pltpu.make_async_copy(word_ref, words, sem)
    copy.start()

    def unpack(source, row, first):
        rows = source[pl.ds(row, 32), :]
        for sub in range(4):
            shifted = rows if sub == 0 else pltpu.roll(rows, LANES - 32 * sub, axis=1)
            table[pl.ds(pl.multiple_of(first + sub * 32, 32), 32), :] = shifted

    for k in range(piece_count):
        for side in range(2):
            base = owners[2 * k + side] * (own_rows * 4)

            def take(part, carry, k=k, side=side, base=base):
                unpack(
                    pieces[k].at[side],
                    pl.multiple_of(head_row + part * 32, 8),
                    base + part * LANES,
                )
                return carry

            lax.fori_loop(0, own_rows // 32, take, 0)
    for end in range(2):
        unpack(rim_ref, end * 32, inner_blocks + end * LANES)

    def clear(turn, carry):
        acc_near[pl.ds(pl.multiple_of(turn * 48, 8), 48), :] = jnp.zeros((48, LANES), jnp.float32)
        acc_far[pl.ds(pl.multiple_of(turn * 96, 8), 96), :] = jnp.zeros((96, LANES), jnp.float32)
        return carry

    lax.fori_loop(0, acc_near.shape[0] // 48, clear, 0)

    copy.wait()

    lane = lax.broadcasted_iota(jnp.int32, (2 * CHUNK, LANES), 1)
    column_of = jnp.where(lane < LANES // 2, 0, 16)
    lane_f = (lane & 7).astype(jnp.float32)
    pick_low = lane < 8
    pick_all = lane < 16
    lane24 = lax.broadcasted_iota(jnp.int32, (24, LANES), 1)
    row8 = lax.broadcasted_iota(jnp.int32, (8, LANES), 0)
    lane8 = lax.broadcasted_iota(jnp.int32, (8, LANES), 1)
    row_first = (row8 & 3) == 0
    row_second = (row8 & 3) == 1
    half8 = (row8 < 4) == (lane8 < LANES // 2)
    ones_half = jnp.where(half8, 1.0, 0.0)
    row_sum = lax.broadcasted_iota(jnp.int32, (2 * LANES, 2 * LANES), 0)
    col_sum = lax.broadcasted_iota(jnp.int32, (2 * LANES, 2 * LANES), 1)
    halves = jnp.where(
        ((row_sum & (LANES - 1)) >= LANES // 2) == (col_sum >= LANES), 1.0, 0.0
    ).astype(jnp.bfloat16)
    row16 = lax.broadcasted_iota(jnp.int32, (16, LANES), 0)
    keeps = [jnp.where((row16 & 7) == sub, 1.0, 0.0).astype(jnp.bfloat16) for sub in range(8)]

    def fetch(first):
        def step(turn, carry):
            row = (first + turn * 8) >> 7
            base = (first + turn * 8) & (LANES - 1)
            for sub in range(8):
                index = turn * 8 + sub
                near = words[row, base + sub]
                far = words[slot_rows + row, base + sub]
                gathered[pl.ds(index, 1), :] = table[pl.ds(near, 1), :]
                gathered[pl.ds(CHUNK + index, 1), :] = table[pl.ds(far, 1), :]
            return carry

        lax.fori_loop(0, CHUNK // 8, step, 0)

    def arrange(first):
        def keep_part(slot, value):
            parts[pl.ds(pl.multiple_of(slot * slots + first, 8), CHUNK), :] = value

        packed = gathered[...]

        def spread(column):
            return jnp.take_along_axis(
                packed, column_of + column, axis=1, mode="promise_in_bounds"
            )

        kind_low = jnp.take_along_axis(
            packed, jnp.where(pick_low, 12, 28), axis=1, mode="promise_in_bounds"
        )
        pick = jnp.where(pick_all & (kind_low == lane_f), 1.0, 0.0).astype(jnp.bfloat16)
        offsets = jnp.dot(pick, off_ref[...], preferred_element_type=jnp.float32)
        where_at = []
        for axis in range(3):
            value = spread(axis)
            for mode in range(3):
                value = value + spread(3 + 3 * axis + mode) * offsets[:, mode * LANES : (mode + 1) * LANES]
            where_at.append(value)
        near = [value[:CHUNK] for value in where_at]
        far = [value[CHUNK:] for value in where_at]
        near_sq = near[0] * near[0] + near[1] * near[1] + near[2] * near[2]
        far_sq = far[0] * far[0] + far[1] * far[1] + far[2] * far[2]
        for axis, value in enumerate(near + [REACH_SQUARED - near_sq]):
            for part, piece in enumerate(split3(value)):
                keep_part(4 * part + axis, piece)
        for axis, value in enumerate([2.0 * value for value in far] + [-far_sq]):
            for part, piece in enumerate(split3(value)):
                keep_part(12 + 4 * part + axis, piece)
        for axis in range(3):
            keep_part(24 + axis, far[axis])

    one8 = jnp.ones((8, LANES), jnp.float32)

    def choose(first, second, third):
        return jnp.where(row_first, first, jnp.where(row_second, second, third))

    def prepare(base):
        def part(slot):
            return parts[pl.ds(slot * slots + base, 8), :]

        near = [[part(4 * which + axis) for axis in range(4)] for which in range(3)]
        far = [[part(12 + 4 * which + axis) for axis in range(4)] for which in range(3)]
        rows_a, rows_b = [], []
        for a, b, a_last, b_last in (
            (0, 0, near[0][3], one8),
            (0, 1, one8, far[1][3]),
            (1, 0, near[1][3], one8),
            (1, 1, one8, far[0][3]),
            (0, 2, one8, far[2][3]),
            (2, 0, near[2][3], one8),
        ):
            rows_a += near[a][:3] + [a_last]
            rows_b += far[b][:3] + [b_last]
        all_a = jnp.concatenate(rows_a, 0).astype(jnp.bfloat16)
        tiles_b = [
            jnp.concatenate(rows_b[2 * tile : 2 * tile + 2], 0).astype(jnp.bfloat16)
            for tile in range(12)
        ]
        return all_a, tiles_b

    def reach_of(all_a, tiles_b, pair):
        side_b = jnp.concatenate(
            [jnp.concatenate([tile * keeps[sub] for tile in tiles_b], 0) for sub in pair], 1
        )
        return lax.dot_general(
            all_a, side_b, (((0,), (0,)), ((), ())), preferred_element_type=jnp.float32
        )

    def sums_of(reach, base, pair):
        weight = jnp.maximum(reach, 0.0)
        weight_high = weight.astype(jnp.bfloat16)
        weight_low = (weight - weight_high.astype(jnp.float32)).astype(jnp.bfloat16)
        side_c = []
        for sub in pair:
            for which in range(3):
                row = choose(
                    *[
                        parts[pl.ds((4 * which + axis) * slots + base + sub, 8, stride=0), :]
                        for axis in range(3)
                    ]
                )
                side_c.append(jnp.where(half8, row, 0.0))
            side_c.append(ones_half)
        side_c = jnp.concatenate(side_c, 0).astype(jnp.bfloat16)
        return jnp.dot(
            jnp.concatenate([side_c, side_c], 1),
            jnp.concatenate([weight_high, weight_low], 0),
            preferred_element_type=jnp.float32,
        )

    def terms_of(sums, base, pair):
        terms = []
        for place, sub in enumerate(pair):
            mine = sums[32 * place : 32 * place + 32, LANES * place : LANES * place + LANES]
            axes = [
                parts[pl.ds((24 + axis) * slots + base + sub, 8, stride=0), :] for axis in range(3)
            ]
            force = mine[24:32] * choose(*axes) - (mine[0:8] + mine[8:16] + mine[16:24])
            terms += [
                force,
                force * choose(axes[1], axes[2], axes[0]),
                force * choose(axes[2], axes[0], axes[1]),
            ]
        terms = jnp.concatenate(terms, 0)
        terms_high = terms.astype(jnp.bfloat16)
        terms_low = (terms - terms_high.astype(jnp.float32)).astype(jnp.bfloat16)
        return jnp.concatenate([terms_high, terms_low], 1)

    def scatter(group):
        base = jnp.clip(group, 0, groups - 1) * 8
        row = base >> 7
        spot = base & (LANES - 1)
        for sub in range(8):
            lower = folded_ref[pl.ds(24 * sub, 24), :LANES]
            upper = folded_ref[pl.ds(24 * sub, 24), LANES:]
            live = (group >= 0) & (group * 8 + sub < number)
            block = words[row, spot + sub]
            here = lane24 == jnp.where(live, block & (LANES - 1), -1)
            at = pl.ds(pl.multiple_of((block >> 7) * 24, 8), 24)
            acc_near[at, :] += jnp.where(here, lower + upper, 0.0)
            block = words[slot_rows + row, spot + sub]
            here = lane24 == jnp.where(live, block & (LANES - 1), -1)
            at = pl.ds(pl.multiple_of((block >> 7) * 48, 8), 48)
            acc_far[at, :] += jnp.concatenate(
                [jnp.where(here, lower, 0.0), jnp.where(here, upper, 0.0)], 0
            )

    def chunk(turn, carry):
        first = pl.multiple_of(turn * CHUNK, CHUNK)
        fetch(first)
        arrange(first)
        return carry

    lax.fori_loop(0, (number + CHUNK - 1) // CHUNK, chunk, 0)

    groups = (number + 7) // 8
    pairs = [(2 * couple, 2 * couple + 1) for couple in range(4)]

    def octet(turn, slot):
        fresh = 4 * LANES * slot
        stale = 4 * LANES * (1 - slot)
        scatter(turn - 3)
        base = jnp.clip(turn - 2, 0, groups - 1) * 8
        terms = [
            terms_of(sums_ref[pl.ds(64 * couple, 64), :], base, pair)
            for couple, pair in enumerate(pairs)
        ]
        folded_ref[...] = jnp.dot(
            jnp.concatenate(terms, 0), halves, preferred_element_type=jnp.float32
        )
        ready = prepare(pl.multiple_of(jnp.minimum(turn, groups - 1) * 8, 8))
        for couple, pair in enumerate(pairs):
            reach_ref[pl.ds(fresh + LANES * couple, LANES), :] = reach_of(*ready, pair)
        base = jnp.clip(turn - 1, 0, groups - 1) * 8
        for couple, pair in enumerate(pairs):
            sums_ref[pl.ds(64 * couple, 64), :] = sums_of(
                reach_ref[pl.ds(stale + LANES * couple, LANES), :], base, pair
            )

    def octet_pair(turn, carry):
        for sub in range(DEPTH):
            octet(DEPTH * turn + sub, sub % 2)
        return carry

    lax.fori_loop(0, (groups + 2 + DEPTH) // DEPTH, octet_pair, 0)

    def total_of(row, half, tiles, start):
        line = (row // 3) * 8 + row % 3
        mine = acc_near[pl.ds(start * 24 + line + 4 * half, tiles, stride=24), :]
        line += 24 * half
        other = (
            acc_far[pl.ds(start * 48 + line, tiles, stride=48), :]
            + acc_far[pl.ds(start * 48 + line + 4, tiles, stride=48), :]
        )
        return (other - mine) * STIFFNESS

    for tiles, start, out in ((inner_blocks // LANES, 0, inner_ref), (2, inner_blocks // LANES, edge_ref)):
        for half in range(2):
            rows = [total_of(row, half, tiles, start) for row in range(9)]
            results = rows[0:3] + [rows[6 + (axis + 2) % 3] - rows[3 + (axis + 1) % 3] for axis in range(3)]
            for axis in range(6):
                out[pl.ds(6 * half + axis, tiles, stride=COMPS), :] = results[axis]


def neighbour_swap(rows_low, rows_high, axis):
    count = lax.axis_size(axis)
    index = lax.axis_index(axis)
    even = index % 2 == 0
    inside = [(i, i ^ 1) for i in range(count)]
    across = [(i, (i + 1) % count if i % 2 else (i - 1) % count) for i in range(count)]
    got_across = lax.ppermute(jnp.where(even, rows_low, rows_high), axis, across)
    got_inside = lax.ppermute(jnp.where(even, rows_high, rows_low), axis, inside)
    from_below = jnp.where(even, got_across, got_inside)
    from_above = jnp.where(even, got_inside, got_across)
    return from_below, from_above


def shards(positions, rotations, clump_kind, sub_offsets, pair_blocks, pair_count):
    members = lax.axis_size("dev")
    groups = lax.axis_size("grp")
    group = lax.axis_index("grp")
    me = lax.axis_index("dev")
    along_z, along_y = me // 2, me % 2
    rings = members // 2
    clumps = positions.shape[1]
    slots = pair_blocks.shape[1]
    own_blocks = clumps // 2
    kinds, _, subs = sub_offsets.shape
    head_row = 2 * slots // LANES

    values = jnp.concatenate(
        [
            positions,
            rotations,
            clump_kind.astype(jnp.float32)[None],
            jnp.zeros((3, clumps), jnp.float32),
        ],
        0,
    )
    values = values.T.reshape(own_blocks, 32)
    lane = lax.broadcasted_iota(jnp.int32, values.shape, 1)
    values = jnp.where(lane == 15, pair_count[0].astype(jnp.float32), values)
    packed = (
        values.reshape(own_blocks // LANES, 4, 32, 32)
        .transpose(0, 2, 1, 3)
        .reshape(own_blocks // 4, LANES)
    )
    inner_blocks = own_blocks * members
    blocks = pair_blocks - group * inner_blocks
    blocks = jnp.where(
        blocks < 0,
        blocks + inner_blocks + RIM,
        jnp.where(blocks >= inner_blocks, blocks + RIM, blocks),
    )
    payload = jnp.concatenate([blocks.astype(jnp.float32).reshape(head_row, LANES), packed], 0)

    pair_y = [(i, i ^ 1) for i in range(members)]
    both = jnp.stack([payload, lax.ppermute(payload, "dev", pair_y)])
    pieces = [both]
    for k in range(1, rings):
        pieces.append(
            lax.ppermute(both, "dev", [(i, (i + 2 * k) % members) for i in range(members)])
        )

    def piece_rows(member, start, count):
        z, y = member // 2, member % 2
        found = None
        for k in range(rings):
            rows = lax.dynamic_slice_in_dim(pieces[k], start, count, 1)
            side = jnp.where(along_y == y, rows[0], rows[1])
            hit = (along_z - k + rings) % rings == z
            found = side if found is None else jnp.where(hit, side, found)
        return found

    rim_rows = RIM // 4
    first_rows = piece_rows(0, head_row, rim_rows)
    last_rows = piece_rows(members - 1, head_row + packed.shape[0] - rim_rows, rim_rows)
    from_below, from_above = neighbour_swap(first_rows, last_rows, "grp")
    rims = jnp.concatenate([from_below, from_above], 0)

    offset_table = sub_offsets.astype(jnp.float32) * OFFSET_UNIT
    blank = jnp.zeros_like(offset_table)
    offset_rows = jnp.concatenate(
        [
            jnp.concatenate([offset_table, blank], 2).reshape(kinds, -1),
            jnp.concatenate([blank, offset_table], 2).reshape(kinds, -1),
        ],
        0,
    )
    offset_rows = jnp.concatenate(
        [offset_rows, jnp.zeros((LANES - 2 * kinds, offset_rows.shape[1]), jnp.float32)], 0
    ).astype(jnp.bfloat16)

    counts = jnp.zeros((members,), jnp.float32)
    for k in range(rings):
        for side in range(2):
            member = (along_z - k + rings) % rings * 2 + (along_y if side == 0 else 1 - along_y)
            counts = counts + jnp.where(
                jnp.arange(members) == member, pieces[k][side, head_row, 15], 0.0
            )
    place = jnp.concatenate(
        [jnp.stack([along_z, along_y]).astype(jnp.int32), counts.astype(jnp.int32)]
    )
    tiles = inner_blocks // LANES
    vmem = pl.BlockSpec(memory_space=pltpu.VMEM)
    inner, edge = pl.pallas_call(
        functools.partial(pair_kernel, members, slots, head_row),
        out_shape=(
            jax.ShapeDtypeStruct((tiles * COMPS, LANES), jnp.float32),
            jax.ShapeDtypeStruct((2 * COMPS, LANES), jnp.float32),
        ),
        in_specs=[pl.BlockSpec(memory_space=pltpu.SMEM)] + [vmem] * (rings + 2),
        out_specs=(vmem, vmem),
        scratch_shapes=[
            pltpu.VMEM((inner_blocks + 2 * RIM, LANES), jnp.float32),
            pltpu.VMEM((head_row, LANES), jnp.int32),
            pltpu.SMEM((head_row, LANES), jnp.int32),
            pltpu.VMEM((2 * CHUNK, LANES), jnp.float32),
            pltpu.VMEM((27 * slots, LANES), jnp.float32),
            pltpu.VMEM((8 * LANES, 2 * LANES), jnp.float32),
            pltpu.VMEM((4 * 64, 2 * LANES), jnp.float32),
            pltpu.VMEM((192, 2 * LANES), jnp.float32),
            pltpu.VMEM(((tiles + 2) * 24, LANES), jnp.float32),
            pltpu.VMEM(((tiles + 2) * 48, LANES), jnp.float32),
            pltpu.SemaphoreType.DMA,
        ],
        name="pair_kernel",
    )(place, *pieces, rims, offset_rows)

    below, above = neighbour_swap(edge[:COMPS], edge[COMPS:], "grp")
    below = jnp.where(group > 0, below, 0.0)
    above = jnp.where(group < groups - 1, above, 0.0)
    inner = inner + jnp.concatenate(
        [below, jnp.zeros(((tiles - 2) * COMPS, LANES), jnp.float32), above], 0
    )

    own_rows = tiles * COMPS // members
    ranks = inner.reshape(rings, 2, own_rows, LANES)
    mine = lax.dynamic_index_in_dim(ranks, along_y, 1, False)
    other = lax.dynamic_index_in_dim(ranks, 1 - along_y, 1, False)
    column = mine + lax.ppermute(other, "dev", pair_y)
    summed = lax.dynamic_index_in_dim(column, along_z, 0, False)
    for k in range(1, rings):
        part = lax.dynamic_index_in_dim(column, (along_z + k) % rings, 0, False)
        summed = summed + lax.ppermute(
            part, "dev", [(i, (i + 2 * k) % members) for i in range(members)]
        )
    summed = summed.reshape(own_blocks // LANES, 2, 6, LANES).transpose(2, 0, 3, 1).reshape(6, clumps)
    clump_force = summed[0:3]
    clump_torque = summed[3:6] - cross_axis(positions, clump_force)
    return (clump_force, clump_torque)


def solution(mesh):
    placed = (
        P(None, ("grp", "dev")),
        P(None, ("grp", "dev")),
        P(("grp", "dev")),
        P(),
        P(None, ("grp", "dev")),
        P(("grp", "dev")),
    )
    return jax.shard_map(
        shards,
        mesh=mesh,
        in_specs=placed,
        out_specs=(P(None, ("grp", "dev")), P(None, ("grp", "dev"))),
        check_vma=False,
    )
```

```python
import functools

import jax
import jax.numpy as jnp
from jax import lax
from jax.experimental import pallas as pl
from jax.experimental.pallas import tpu as pltpu
from jax.sharding import PartitionSpec as P

RIM = 128
LANES = 128
OFFSET_UNIT = 0.125
REACH_SQUARED = 4.0
STIFFNESS = 1.0 / 256.0
CHUNK = 64
COMPS = 12
PARAMS = 10
ROWS = 24
DEPTH = 2


def split3(value):
    high = value.astype(jnp.bfloat16).astype(jnp.float32)
    rest = value - high
    middle = rest.astype(jnp.bfloat16).astype(jnp.float32)
    return high, middle, rest - middle


def payload_kernel(slots, members, position_ref, rotation_ref, kind_ref, pair_ref, count_ref, out_ref):
    clumps = position_ref.shape[1]
    blocks = clumps // 2
    inner_blocks = blocks * members
    wide = 2 * LANES
    row = lax.broadcasted_iota(jnp.int32, (wide, wide), 0)
    column = lax.broadcasted_iota(jnp.int32, (wide, wide), 1)
    source = jnp.where(column < LANES, 2 * column, 2 * column - (wide - 1))
    picked = jnp.where(row == source, 1.0, 0.0).astype(jnp.bfloat16)
    parts = []
    for turn in range(clumps // wide):
        at = slice(turn * wide, (turn + 1) * wide)
        kinds = kind_ref[2 * turn : 2 * turn + 2, :].astype(jnp.float32)
        value = jnp.concatenate(
            [
                position_ref[:, at],
                rotation_ref[0:6, at],
                jnp.concatenate([kinds[0:1], kinds[1:2]], 1),
                jnp.zeros((16 - PARAMS, wide), jnp.float32),
            ],
            0,
        )
        parts += [piece.astype(jnp.bfloat16) for piece in split3(value)]
    sorted_parts = jnp.dot(
        jnp.concatenate(parts, 0), picked, preferred_element_type=jnp.float32
    )
    for turn in range(clumps // wide):
        high, middle, low = (sorted_parts[16 * (3 * turn + part) : 16 * (3 * turn + part) + 16] for part in range(3))
        value = (high + middle) + low
        at = slice(turn * LANES, (turn + 1) * LANES)
        out_ref[0:PARAMS, at] = value[0:PARAMS, :LANES]
        out_ref[PARAMS : 2 * PARAMS, at] = value[0:PARAMS, LANES:]
    pairs = pair_ref[...] - lax.axis_index("grp") * inner_blocks
    pairs = jnp.where(
        pairs < 0,
        pairs + inner_blocks + RIM,
        jnp.where(pairs >= inner_blocks, pairs + RIM, pairs),
    )
    live = lax.broadcasted_iota(jnp.int32, pairs.shape, 1) < count_ref[0]
    pairs = jnp.where(live, pairs, -1).astype(jnp.float32)
    lists = slots // blocks
    for which in range(2):
        for part in range(lists):
            out_ref[pl.ds(2 * PARAMS + which * lists + part, 1), :] = pairs[
                which : which + 1, part * blocks : (part + 1) * blocks
            ]


def finish_kernel(own_ref, *refs):
    parts = refs[:-4]
    position_ref, force_ref, torque_ref, total_ref = refs[-4:]
    total = own_ref[...]
    for part in parts:
        total = total + part[...]
    total_ref[...] = total
    tiles = own_ref.shape[0] // COMPS
    wide = 2 * LANES
    row = lax.broadcasted_iota(jnp.int32, (wide, wide), 0)
    column = lax.broadcasted_iota(jnp.int32, (wide, wide), 1)
    target = jnp.where(row < LANES, 2 * row, 2 * row - (wide - 1))
    placed = jnp.where(column == target, 1.0, 0.0).astype(jnp.bfloat16)
    halves = [
        jnp.concatenate(
            [total_ref[pl.ds(6 * half + comp, tiles, stride=COMPS), :] for comp in range(6)], 0
        )
        for half in range(2)
    ]
    value = jnp.concatenate(halves, 1)
    rows = value.shape[0]
    joined = jnp.dot(
        jnp.concatenate([part.astype(jnp.bfloat16) for part in split3(value)], 0),
        placed,
        preferred_element_type=jnp.float32,
    )
    value = (joined[0:rows] + joined[rows : 2 * rows]) + joined[2 * rows : 3 * rows]
    comps = [value[comp * tiles : (comp + 1) * tiles] for comp in range(6)]
    centre = [
        jnp.concatenate(
            [position_ref[axis : axis + 1, tile * wide : (tile + 1) * wide] for tile in range(tiles)], 0
        )
        for axis in range(3)
    ]
    for axis in range(3):
        after, last = (axis + 1) % 3, (axis + 2) % 3
        torque = comps[3 + axis] - (centre[after] * comps[last] - centre[last] * comps[after])
        for tile in range(tiles):
            at = slice(tile * wide, (tile + 1) * wide)
            force_ref[axis : axis + 1, at] = comps[axis][tile : tile + 1]
            torque_ref[axis : axis + 1, at] = torque[tile : tile + 1]


def pair_kernel(members, slots, *refs):
    piece_count = members // 2
    pieces = refs[:piece_count]
    (inside_ref, across_ref, off_ref, inner_ref, edge_in_ref, edge_over_ref, table, list_ref, word_ref,
     words, gathered, parts, reach_ref, sums_ref, folded_ref, acc_near, acc_far, sem) = refs[piece_count:]
    me = lax.axis_index("dev")
    along_z, along_y = me // 2, lax.rem(me, 2)
    even = lax.rem(lax.axis_index("grp"), 2) == 0
    own_blocks = pieces[0].shape[2]
    inner_blocks = members * own_blocks
    slot_rows = slots // LANES
    lists = slots // own_blocks

    owners = []
    counts = []
    for k in range(piece_count):
        for side in range(2):
            owners.append(
                lax.rem(along_z - k + piece_count, piece_count) * 2
                + (along_y if side == 0 else 1 - along_y)
            )
            base = (2 * k + side) * 2 * slot_rows
            for part in range(2 * slot_rows):
                line, spot = part // (own_blocks // LANES), part % (own_blocks // LANES)
                list_ref[pl.ds(base + part, 1), :] = pieces[k][
                    side, pl.ds(2 * PARAMS + line, 1), spot * LANES : (spot + 1) * LANES
                ]
            found = jnp.where(list_ref[pl.ds(base, slot_rows), :] >= 0.0, 1.0, 0.0)
            counts.append(jnp.sum(found).astype(jnp.int32))
    starts = []
    total = jnp.int32(0)
    for index in range(members):
        start = jnp.int32(0)
        for other in range(members):
            if other != index:
                start = start + jnp.where(owners[other] < owners[index], counts[other], 0)
        starts.append(start)
        total = total + counts[index]
    begin = (total * me) // members
    finish = (total * (me + 1)) // members
    number = finish - begin

    flat = lax.broadcasted_iota(jnp.int32, (slot_rows, LANES), 0) * LANES
    column = lax.broadcasted_iota(jnp.int32, (slot_rows, LANES), 1)
    flat = flat + column
    near_list = jnp.zeros((slot_rows, LANES), jnp.float32)
    far_list = jnp.zeros((slot_rows, LANES), jnp.float32)
    for index in range(members):
        start = starts[index]
        low = jnp.maximum(start, begin) - begin
        high = jnp.minimum(start + counts[index], finish) - begin
        shift = jnp.bitwise_and(start - begin, slots - 1)
        wanted = (flat >= low) & (flat < high)

        def moved(rows, shift=shift):
            turned = pltpu.roll(rows, shift & (LANES - 1), axis=1)
            same = pltpu.roll(turned, shift >> 7, axis=0)
            following = pltpu.roll(turned, (shift >> 7) + 1, axis=0)
            return jnp.where(column < (shift & (LANES - 1)), following, same)

        base = index * 2 * slot_rows
        near_list = jnp.where(wanted, moved(list_ref[pl.ds(base, slot_rows), :]), near_list)
        far_list = jnp.where(wanted, moved(list_ref[pl.ds(base + slot_rows, slot_rows), :]), far_list)
    word_ref[pl.ds(0, slot_rows), :] = near_list.astype(jnp.int32)
    word_ref[pl.ds(slot_rows, slot_rows), :] = far_list.astype(jnp.int32)
    copy = pltpu.make_async_copy(word_ref, words, sem)
    copy.start()

    for k in range(piece_count):
        for side in range(2):
            base = pl.multiple_of(owners[2 * k + side] * own_blocks, LANES)
            for tile in range(own_blocks // LANES):
                at = slice(tile * LANES, (tile + 1) * LANES)
                table[pl.ds(base + tile * LANES, LANES), 0:ROWS] = pieces[k][side, :, at].T
    below = jnp.where(even, 0, LANES)
    table[pl.ds(pl.multiple_of(inner_blocks + below, LANES), LANES), 0:ROWS] = across_ref[...].T
    table[pl.ds(pl.multiple_of(inner_blocks + LANES - below, LANES), LANES), 0:ROWS] = inside_ref[...].T

    def clear(turn, carry):
        acc_near[pl.ds(pl.multiple_of(turn * 48, 8), 48), :] = jnp.zeros((48, LANES), jnp.float32)
        acc_far[pl.ds(pl.multiple_of(turn * 96, 8), 96), :] = jnp.zeros((96, LANES), jnp.float32)
        return carry

    lax.fori_loop(0, acc_near.shape[0] // 48, clear, 0)

    copy.wait()

    lane = lax.broadcasted_iota(jnp.int32, (2 * CHUNK, LANES), 1)
    column_of = jnp.where(lane < LANES // 2, 0, PARAMS)
    lane_f = (lane & 7).astype(jnp.float32)
    pick_low = lane < 8
    pick_all = lane < 16
    lane24 = lax.broadcasted_iota(jnp.int32, (24, LANES), 1)
    row8 = lax.broadcasted_iota(jnp.int32, (8, LANES), 0)
    lane8 = lax.broadcasted_iota(jnp.int32, (8, LANES), 1)
    row_first = (row8 & 3) == 0
    row_second = (row8 & 3) == 1
    half8 = (row8 < 4) == (lane8 < LANES // 2)
    ones_half = jnp.where(half8, 1.0, 0.0)
    row_sum = lax.broadcasted_iota(jnp.int32, (2 * LANES, 2 * LANES), 0)
    col_sum = lax.broadcasted_iota(jnp.int32, (2 * LANES, 2 * LANES), 1)
    halves = jnp.where(
        ((row_sum & (LANES - 1)) >= LANES // 2) == (col_sum >= LANES), 1.0, 0.0
    ).astype(jnp.bfloat16)
    row16 = lax.broadcasted_iota(jnp.int32, (16, LANES), 0)
    keeps = [jnp.where((row16 & 7) == sub, 1.0, 0.0).astype(jnp.bfloat16) for sub in range(8)]

    def fetch(first):
        def step(turn, carry):
            row = (first + turn * 8) >> 7
            base = (first + turn * 8) & (LANES - 1)
            for sub in range(8):
                index = turn * 8 + sub
                near = words[row, base + sub]
                far = words[slot_rows + row, base + sub]
                gathered[pl.ds(index, 1), :] = table[pl.ds(near, 1), :]
                gathered[pl.ds(CHUNK + index, 1), :] = table[pl.ds(far, 1), :]
            return carry

        lax.fori_loop(0, CHUNK // 8, step, 0)

    def arrange(first):
        def keep_part(slot, value):
            parts[pl.ds(pl.multiple_of(slot * slots + first, 8), CHUNK), :] = value

        packed = gathered[...]

        def spread(column):
            return jnp.take_along_axis(
                packed, column_of + column, axis=1, mode="promise_in_bounds"
            )

        kind_low = jnp.take_along_axis(
            packed, jnp.where(pick_low, 9, PARAMS + 9), axis=1, mode="promise_in_bounds"
        )
        pick = jnp.where(pick_all & (kind_low == lane_f), 1.0, 0.0).astype(jnp.bfloat16)
        offsets = jnp.dot(pick, off_ref[...], preferred_element_type=jnp.float32)
        turns = [spread(3 + entry) for entry in range(6)]
        for mode in range(3):
            after, last = (mode + 1) % 3, (mode + 2) % 3
            turns.append(turns[after] * turns[3 + last] - turns[last] * turns[3 + after])
        where_at = []
        for axis in range(3):
            value = spread(axis)
            for mode in range(3):
                value = value + turns[3 * axis + mode] * offsets[:, mode * LANES : (mode + 1) * LANES]
            where_at.append(value)
        near = [value[:CHUNK] for value in where_at]
        far = [value[CHUNK:] for value in where_at]
        near_sq = near[0] * near[0] + near[1] * near[1] + near[2] * near[2]
        far_sq = far[0] * far[0] + far[1] * far[1] + far[2] * far[2]
        for axis, value in enumerate(near + [REACH_SQUARED - near_sq]):
            for part, piece in enumerate(split3(value)):
                keep_part(4 * part + axis, piece)
        for axis, value in enumerate([2.0 * value for value in far] + [-far_sq]):
            for part, piece in enumerate(split3(value)):
                keep_part(12 + 4 * part + axis, piece)
        for axis in range(3):
            keep_part(24 + axis, far[axis])

    one8 = jnp.ones((8, LANES), jnp.float32)

    def choose(first, second, third):
        return jnp.where(row_first, first, jnp.where(row_second, second, third))

    def prepare(base):
        def part(slot):
            return parts[pl.ds(slot * slots + base, 8), :]

        near = [[part(4 * which + axis) for axis in range(4)] for which in range(3)]
        far = [[part(12 + 4 * which + axis) for axis in range(4)] for which in range(3)]
        rows_a, rows_b = [], []
        for a, b, a_last, b_last in (
            (0, 0, near[0][3], one8),
            (0, 1, one8, far[1][3]),
            (1, 0, near[1][3], one8),
            (1, 1, one8, far[0][3]),
            (0, 2, one8, far[2][3]),
            (2, 0, near[2][3], one8),
        ):
            rows_a += near[a][:3] + [a_last]
            rows_b += far[b][:3] + [b_last]
        all_a = jnp.concatenate(rows_a, 0).astype(jnp.bfloat16)
        tiles_b = [
            jnp.concatenate(rows_b[2 * tile : 2 * tile + 2], 0).astype(jnp.bfloat16)
            for tile in range(12)
        ]
        return all_a, tiles_b

    def reach_of(all_a, tiles_b, pair):
        side_b = jnp.concatenate(
            [jnp.concatenate([tile * keeps[sub] for tile in tiles_b], 0) for sub in pair], 1
        )
        return lax.dot_general(
            all_a, side_b, (((0,), (0,)), ((), ())), preferred_element_type=jnp.float32
        )

    def sums_of(reach, base, pair):
        weight = jnp.maximum(reach, 0.0)
        weight_high = weight.astype(jnp.bfloat16)
        weight_low = (weight - weight_high.astype(jnp.float32)).astype(jnp.bfloat16)
        side_c = []
        for sub in pair:
            for which in range(3):
                row = choose(
                    *[
                        parts[pl.ds((4 * which + axis) * slots + base + sub, 8, stride=0), :]
                        for axis in range(3)
                    ]
                )
                side_c.append(jnp.where(half8, row, 0.0))
            side_c.append(ones_half)
        side_c = jnp.concatenate(side_c, 0).astype(jnp.bfloat16)
        return jnp.dot(
            jnp.concatenate([side_c, side_c], 1),
            jnp.concatenate([weight_high, weight_low], 0),
            preferred_element_type=jnp.float32,
        )

    def terms_of(sums, base, pair):
        terms = []
        for place, sub in enumerate(pair):
            mine = sums[32 * place : 32 * place + 32, LANES * place : LANES * place + LANES]
            axes = [
                parts[pl.ds((24 + axis) * slots + base + sub, 8, stride=0), :] for axis in range(3)
            ]
            force = mine[24:32] * choose(*axes) - (mine[0:8] + mine[8:16] + mine[16:24])
            terms += [
                force,
                force * choose(axes[1], axes[2], axes[0]),
                force * choose(axes[2], axes[0], axes[1]),
            ]
        terms = jnp.concatenate(terms, 0)
        terms_high = terms.astype(jnp.bfloat16)
        terms_low = (terms - terms_high.astype(jnp.float32)).astype(jnp.bfloat16)
        return jnp.concatenate([terms_high, terms_low], 1)

    def scatter(group):
        base = jnp.clip(group, 0, groups - 1) * 8
        row = base >> 7
        spot = base & (LANES - 1)
        for sub in range(8):
            lower = folded_ref[pl.ds(24 * sub, 24), :LANES]
            upper = folded_ref[pl.ds(24 * sub, 24), LANES:]
            live = (group >= 0) & (group * 8 + sub < number)
            block = words[row, spot + sub]
            here = lane24 == jnp.where(live, block & (LANES - 1), -1)
            at = pl.ds(pl.multiple_of((block >> 7) * 24, 8), 24)
            acc_near[at, :] += jnp.where(here, lower + upper, 0.0)
            block = words[slot_rows + row, spot + sub]
            here = lane24 == jnp.where(live, block & (LANES - 1), -1)
            at = pl.ds(pl.multiple_of((block >> 7) * 48, 8), 48)
            acc_far[at, :] += jnp.concatenate(
                [jnp.where(here, lower, 0.0), jnp.where(here, upper, 0.0)], 0
            )

    def chunk(turn, carry):
        first = pl.multiple_of(turn * CHUNK, CHUNK)
        fetch(first)
        arrange(first)
        return carry

    lax.fori_loop(0, (number + CHUNK - 1) // CHUNK, chunk, 0)

    groups = (number + 7) // 8
    pairs = [(2 * couple, 2 * couple + 1) for couple in range(4)]

    def octet(turn, slot):
        fresh = 4 * LANES * slot
        stale = 4 * LANES * (1 - slot)
        scatter(turn - 3)
        base = jnp.clip(turn - 2, 0, groups - 1) * 8
        terms = [
            terms_of(sums_ref[pl.ds(64 * couple, 64), :], base, pair)
            for couple, pair in enumerate(pairs)
        ]
        folded_ref[...] = jnp.dot(
            jnp.concatenate(terms, 0), halves, preferred_element_type=jnp.float32
        )
        ready = prepare(pl.multiple_of(jnp.minimum(turn, groups - 1) * 8, 8))
        for couple, pair in enumerate(pairs):
            reach_ref[pl.ds(fresh + LANES * couple, LANES), :] = reach_of(*ready, pair)
        base = jnp.clip(turn - 1, 0, groups - 1) * 8
        for couple, pair in enumerate(pairs):
            sums_ref[pl.ds(64 * couple, 64), :] = sums_of(
                reach_ref[pl.ds(stale + LANES * couple, LANES), :], base, pair
            )

    def octet_pair(turn, carry):
        for sub in range(DEPTH):
            octet(DEPTH * turn + sub, sub % 2)
        return carry

    lax.fori_loop(0, (groups + 2 + DEPTH) // DEPTH, octet_pair, 0)

    def total_of(row, half, tiles, start):
        line = (row // 3) * 8 + row % 3
        mine = acc_near[pl.ds(start * 24 + line + 4 * half, tiles, stride=24), :]
        line += 24 * half
        other = (
            acc_far[pl.ds(start * 48 + line, tiles, stride=48), :]
            + acc_far[pl.ds(start * 48 + line + 4, tiles, stride=48), :]
        )
        return (other - mine) * STIFFNESS

    def results_of(half, tiles, start):
        rows = [total_of(row, half, tiles, start) for row in range(9)]
        return rows[0:3] + [
            rows[6 + (axis + 2) % 3] - rows[3 + (axis + 1) % 3] for axis in range(3)
        ]

    inner_tiles = inner_blocks // LANES
    for half in range(2):
        for axis, value in enumerate(results_of(half, inner_tiles, 0)):
            inner_ref[pl.ds(6 * half + axis, inner_tiles, stride=COMPS), :] = value
        for axis, value in enumerate(results_of(half, 2, inner_tiles)):
            at = pl.ds(6 * half + axis, 1)
            edge_in_ref[at, :] = jnp.where(even, value[1:2], value[0:1])
            edge_over_ref[at, :] = jnp.where(even, value[0:1], value[1:2])


def swaps(count):
    inside = [(i, i ^ 1) for i in range(count)]
    across = [(i, (i + 1) % count if i % 2 else (i - 1) % count) for i in range(count)]
    return inside, across


def shards(positions, rotations, clump_kind, sub_offsets, pair_blocks, pair_count):
    members = lax.axis_size("dev")
    groups = lax.axis_size("grp")
    group = lax.axis_index("grp")
    me = lax.axis_index("dev")
    along_z, along_y = me // 2, me % 2
    rings = members // 2
    clumps = positions.shape[1]
    slots = pair_blocks.shape[1]
    own_blocks = clumps // 2
    kinds, _, subs = sub_offsets.shape
    even = group % 2 == 0
    inside, across = swaps(groups)
    vmem = pl.BlockSpec(memory_space=pltpu.VMEM)
    smem = pl.BlockSpec(memory_space=pltpu.SMEM)

    payload = pl.pallas_call(
        functools.partial(payload_kernel, slots, members),
        out_shape=jax.ShapeDtypeStruct((ROWS, own_blocks), jnp.float32),
        in_specs=[vmem] * 4 + [smem],
        out_specs=vmem,
        name="payload_kernel",
    )(positions, rotations, clump_kind.reshape(-1, LANES), pair_blocks, pair_count)

    pair_y = [(i, i ^ 1) for i in range(members)]
    both = jnp.stack([payload, lax.ppermute(payload, "dev", pair_y)])
    pieces = [both]
    for k in range(1, rings):
        pieces.append(
            lax.ppermute(both, "dev", [(i, (i + 2 * k) % members) for i in range(members)])
        )

    def piece_columns(member, start):
        z, y = member // 2, member % 2
        found = None
        for k in range(rings):
            part = pieces[k][:, :, start : start + RIM]
            part = jnp.where(along_y == y, part[0], part[1])
            hit = (along_z - k + rings) % rings == z
            found = part if found is None else jnp.where(hit, part, found)
        return found

    first = piece_columns(0, 0)
    last = piece_columns(members - 1, own_blocks - RIM)
    got_across = lax.ppermute(jnp.where(even, first, last), "grp", across)
    got_inside = lax.ppermute(jnp.where(even, last, first), "grp", inside)

    offset_table = sub_offsets.astype(jnp.float32) * OFFSET_UNIT
    blank = jnp.zeros_like(offset_table)
    offset_rows = jnp.concatenate(
        [
            jnp.concatenate([offset_table, blank], 2).reshape(kinds, -1),
            jnp.concatenate([blank, offset_table], 2).reshape(kinds, -1),
        ],
        0,
    )
    offset_rows = jnp.concatenate(
        [offset_rows, jnp.zeros((LANES - 2 * kinds, offset_rows.shape[1]), jnp.float32)], 0
    ).astype(jnp.bfloat16)

    inner_blocks = own_blocks * members
    tiles = inner_blocks // LANES
    inner, edge_in, edge_over = pl.pallas_call(
        functools.partial(pair_kernel, members, slots),
        out_shape=(
            jax.ShapeDtypeStruct((tiles * COMPS, LANES), jnp.float32),
            jax.ShapeDtypeStruct((COMPS, LANES), jnp.float32),
            jax.ShapeDtypeStruct((COMPS, LANES), jnp.float32),
        ),
        in_specs=[vmem] * (rings + 3),
        out_specs=(vmem, vmem, vmem),
        scratch_shapes=[
            pltpu.VMEM((inner_blocks + 2 * RIM, LANES), jnp.float32),
            pltpu.VMEM((members * 2 * slots // LANES, LANES), jnp.float32),
            pltpu.VMEM((2 * slots // LANES, LANES), jnp.int32),
            pltpu.SMEM((2 * slots // LANES, LANES), jnp.int32),
            pltpu.VMEM((2 * CHUNK, LANES), jnp.float32),
            pltpu.VMEM((27 * slots, LANES), jnp.float32),
            pltpu.VMEM((8 * LANES, 2 * LANES), jnp.float32),
            pltpu.VMEM((4 * 64, 2 * LANES), jnp.float32),
            pltpu.VMEM((192, 2 * LANES), jnp.float32),
            pltpu.VMEM(((tiles + 2) * 24, LANES), jnp.float32),
            pltpu.VMEM(((tiles + 2) * 48, LANES), jnp.float32),
            pltpu.SemaphoreType.DMA,
        ],
        name="pair_kernel",
    )(*pieces, got_inside, got_across, offset_rows)

    got_over = lax.ppermute(edge_over, "grp", across)
    got_in = lax.ppermute(edge_in, "grp", inside)
    below = jnp.where(group > 0, jnp.where(even, got_over, got_in), 0.0)
    above = jnp.where(group < groups - 1, jnp.where(even, got_in, got_over), 0.0)
    inner = inner + jnp.concatenate(
        [below, jnp.zeros(((tiles - 2) * COMPS, LANES), jnp.float32), above], 0
    )

    own_rows = tiles * COMPS // members
    ranks = inner.reshape(rings, 2, own_rows, LANES)
    mine = lax.dynamic_index_in_dim(ranks, along_y, 1, False)
    other = lax.dynamic_index_in_dim(ranks, 1 - along_y, 1, False)
    column = mine + lax.ppermute(other, "dev", pair_y)
    shares = [lax.dynamic_index_in_dim(column, along_z, 0, False)]
    for k in range(1, rings):
        part = lax.dynamic_index_in_dim(column, (along_z + k) % rings, 0, False)
        shares.append(
            lax.ppermute(part, "dev", [(i, (i + 2 * k) % members) for i in range(members)])
        )
    clump_force, clump_torque = pl.pallas_call(
        finish_kernel,
        out_shape=(jax.ShapeDtypeStruct((3, clumps), jnp.float32),) * 2,
        in_specs=[vmem] * (rings + 1),
        out_specs=(vmem, vmem),
        scratch_shapes=[pltpu.VMEM((own_rows, LANES), jnp.float32)],
        name="finish_kernel",
    )(*shares, positions)
    return (clump_force, clump_torque)


def solution(mesh):
    placed = (
        P(None, ("grp", "dev")),
        P(None, ("grp", "dev")),
        P(("grp", "dev")),
        P(),
        P(None, ("grp", "dev")),
        P(("grp", "dev")),
    )
    return jax.shard_map(
        shards,
        mesh=mesh,
        in_specs=placed,
        out_specs=(P(None, ("grp", "dev")), P(None, ("grp", "dev"))),
        check_vma=False,
    )
```

```python
import functools

import jax
import jax.numpy as jnp
from jax import lax
from jax.experimental import pallas as pl
from jax.experimental.pallas import tpu as pltpu
from jax.sharding import PartitionSpec as P

RIM = 128
LANES = 128
OFFSET_UNIT = 0.125
REACH_SQUARED = 4.0
STIFFNESS = 1.0 / 256.0
CHUNK = 64
COMPS = 12
PARAMS = 10
ROWS = 24
DEPTH = 4


def split3(value):
    high = value.astype(jnp.bfloat16).astype(jnp.float32)
    rest = value - high
    middle = rest.astype(jnp.bfloat16).astype(jnp.float32)
    return high, middle, rest - middle


def clique_order(count):
    return [0, count - 1] + list(range(1, count - 1))


def payload_kernel(slots, members, position_ref, rotation_ref, kind_ref, pair_ref, count_ref, out_ref):
    clumps = position_ref.shape[1]
    blocks = clumps // 2
    inner_blocks = blocks * members
    wide = 2 * LANES
    row = lax.broadcasted_iota(jnp.int32, (wide, wide), 0)
    column = lax.broadcasted_iota(jnp.int32, (wide, wide), 1)
    source = jnp.where(column < LANES, 2 * column, 2 * column - (wide - 1))
    picked = jnp.where(row == source, 1.0, 0.0).astype(jnp.bfloat16)
    parts = []
    for turn in range(clumps // wide):
        at = slice(turn * wide, (turn + 1) * wide)
        kinds = kind_ref[2 * turn : 2 * turn + 2, :].astype(jnp.float32)
        value = jnp.concatenate(
            [
                position_ref[:, at],
                rotation_ref[0:6, at],
                jnp.concatenate([kinds[0:1], kinds[1:2]], 1),
                jnp.zeros((16 - PARAMS, wide), jnp.float32),
            ],
            0,
        )
        parts += [piece.astype(jnp.bfloat16) for piece in split3(value)]
    sorted_parts = jnp.dot(
        jnp.concatenate(parts, 0), picked, preferred_element_type=jnp.float32
    )
    for turn in range(clumps // wide):
        high, middle, low = (sorted_parts[16 * (3 * turn + part) : 16 * (3 * turn + part) + 16] for part in range(3))
        value = (high + middle) + low
        at = slice(turn * LANES, (turn + 1) * LANES)
        out_ref[0:PARAMS, at] = value[0:PARAMS, :LANES]
        out_ref[PARAMS : 2 * PARAMS, at] = value[0:PARAMS, LANES:]
    pairs = pair_ref[...] - lax.axis_index("grp") * inner_blocks
    pairs = jnp.where(
        pairs < 0,
        pairs + inner_blocks + RIM,
        jnp.where(pairs >= inner_blocks, pairs + RIM, pairs),
    )
    live = lax.broadcasted_iota(jnp.int32, pairs.shape, 1) < count_ref[0]
    pairs = jnp.where(live, pairs, -1).astype(jnp.float32)
    lists = slots // blocks
    for which in range(2):
        for part in range(lists):
            out_ref[pl.ds(2 * PARAMS + which * lists + part, 1), :] = pairs[
                which : which + 1, part * blocks : (part + 1) * blocks
            ]


def finish_kernel(own_ref, *refs):
    parts = refs[:-4]
    position_ref, force_ref, torque_ref, total_ref = refs[-4:]
    total = own_ref[...]
    for part in parts:
        total = total + part[...]
    total_ref[...] = total
    tiles = own_ref.shape[0] // COMPS
    wide = 2 * LANES
    row = lax.broadcasted_iota(jnp.int32, (wide, wide), 0)
    column = lax.broadcasted_iota(jnp.int32, (wide, wide), 1)
    target = jnp.where(row < LANES, 2 * row, 2 * row - (wide - 1))
    placed = jnp.where(column == target, 1.0, 0.0).astype(jnp.bfloat16)
    halves = [
        jnp.concatenate(
            [total_ref[pl.ds(6 * half + comp, tiles, stride=COMPS), :] for comp in range(6)], 0
        )
        for half in range(2)
    ]
    value = jnp.concatenate(halves, 1)
    rows = value.shape[0]
    joined = jnp.dot(
        jnp.concatenate([part.astype(jnp.bfloat16) for part in split3(value)], 0),
        placed,
        preferred_element_type=jnp.float32,
    )
    value = (joined[0:rows] + joined[rows : 2 * rows]) + joined[2 * rows : 3 * rows]
    comps = [value[comp * tiles : (comp + 1) * tiles] for comp in range(6)]
    centre = [
        jnp.concatenate(
            [position_ref[axis : axis + 1, tile * wide : (tile + 1) * wide] for tile in range(tiles)], 0
        )
        for axis in range(3)
    ]
    for axis in range(3):
        after, last = (axis + 1) % 3, (axis + 2) % 3
        torque = comps[3 + axis] - (centre[after] * comps[last] - centre[last] * comps[after])
        for tile in range(tiles):
            at = slice(tile * wide, (tile + 1) * wide)
            force_ref[axis : axis + 1, at] = comps[axis][tile : tile + 1]
            torque_ref[axis : axis + 1, at] = torque[tile : tile + 1]


def pair_kernel(members, slots, *refs):
    piece_count = members // 2
    pieces = refs[:piece_count]
    (inside_ref, across_ref, off_ref, inner_ref, edge_in_ref, edge_over_ref, table, list_ref, word_ref,
     words, gathered, parts, reach_ref, sums_ref, folded_ref, acc_near, acc_far, sem) = refs[piece_count:]
    me = lax.axis_index("dev")
    even = lax.rem(lax.axis_index("grp"), 2) == 0
    own_blocks = pieces[0].shape[2]
    inner_blocks = members * own_blocks
    slot_rows = slots // LANES
    lists = slots // own_blocks

    owners = []
    counts = []
    for k in range(piece_count):
        for side in range(2):
            owners.append(jnp.bitwise_xor(me, clique_order(piece_count)[k] + side * piece_count))
            base = (2 * k + side) * 2 * slot_rows
            for part in range(2 * slot_rows):
                line, spot = part // (own_blocks // LANES), part % (own_blocks // LANES)
                list_ref[pl.ds(base + part, 1), :] = pieces[k][
                    side, pl.ds(2 * PARAMS + line, 1), spot * LANES : (spot + 1) * LANES
                ]
            found = jnp.where(list_ref[pl.ds(base, slot_rows), :] >= 0.0, 1.0, 0.0)
            counts.append(jnp.sum(found).astype(jnp.int32))
    starts = []
    total = jnp.int32(0)
    for index in range(members):
        start = jnp.int32(0)
        for other in range(members):
            if other != index:
                start = start + jnp.where(owners[other] < owners[index], counts[other], 0)
        starts.append(start)
        total = total + counts[index]
    begin = (total * me) // members
    finish = (total * (me + 1)) // members
    number = finish - begin

    flat = lax.broadcasted_iota(jnp.int32, (slot_rows, LANES), 0) * LANES
    column = lax.broadcasted_iota(jnp.int32, (slot_rows, LANES), 1)
    flat = flat + column
    near_list = jnp.zeros((slot_rows, LANES), jnp.float32)
    far_list = jnp.zeros((slot_rows, LANES), jnp.float32)
    for index in range(members):
        start = starts[index]
        low = jnp.maximum(start, begin) - begin
        high = jnp.minimum(start + counts[index], finish) - begin
        shift = jnp.bitwise_and(start - begin, slots - 1)
        wanted = (flat >= low) & (flat < high)

        def moved(rows, shift=shift):
            turned = pltpu.roll(rows, shift & (LANES - 1), axis=1)
            same = pltpu.roll(turned, shift >> 7, axis=0)
            following = pltpu.roll(turned, (shift >> 7) + 1, axis=0)
            return jnp.where(column < (shift & (LANES - 1)), following, same)

        base = index * 2 * slot_rows
        near_list = jnp.where(wanted, moved(list_ref[pl.ds(base, slot_rows), :]), near_list)
        far_list = jnp.where(wanted, moved(list_ref[pl.ds(base + slot_rows, slot_rows), :]), far_list)
    word_ref[pl.ds(0, slot_rows), :] = near_list.astype(jnp.int32)
    word_ref[pl.ds(slot_rows, slot_rows), :] = far_list.astype(jnp.int32)
    copy = pltpu.make_async_copy(word_ref, words, sem)
    copy.start()

    for k in range(piece_count):
        for side in range(2):
            base = pl.multiple_of(owners[2 * k + side] * own_blocks, LANES)
            for tile in range(own_blocks // LANES):
                at = slice(tile * LANES, (tile + 1) * LANES)
                table[pl.ds(base + tile * LANES, LANES), 0:ROWS] = pieces[k][side, :, at].T
    below = jnp.where(even, 0, LANES)
    table[pl.ds(pl.multiple_of(inner_blocks + below, LANES), LANES), 0:ROWS] = across_ref[...].T
    table[pl.ds(pl.multiple_of(inner_blocks + LANES - below, LANES), LANES), 0:ROWS] = inside_ref[...].T

    def clear(turn, carry):
        acc_near[pl.ds(pl.multiple_of(turn * 48, 8), 48), :] = jnp.zeros((48, LANES), jnp.float32)
        acc_far[pl.ds(pl.multiple_of(turn * 96, 8), 96), :] = jnp.zeros((96, LANES), jnp.float32)
        return carry

    lax.fori_loop(0, acc_near.shape[0] // 48, clear, 0)

    copy.wait()

    lane = lax.broadcasted_iota(jnp.int32, (2 * CHUNK, LANES), 1)
    column_of = jnp.where(lane < LANES // 2, 0, PARAMS)
    lane_f = (lane & 7).astype(jnp.float32)
    pick_low = lane < 8
    pick_all = lane < 16
    lane24 = lax.broadcasted_iota(jnp.int32, (24, LANES), 1)
    row8 = lax.broadcasted_iota(jnp.int32, (8, LANES), 0)
    lane8 = lax.broadcasted_iota(jnp.int32, (8, LANES), 1)
    row_first = (row8 & 3) == 0
    row_second = (row8 & 3) == 1
    half8 = (row8 < 4) == (lane8 < LANES // 2)
    ones_half = jnp.where(half8, 1.0, 0.0)
    row_sum = lax.broadcasted_iota(jnp.int32, (2 * LANES, 2 * LANES), 0)
    col_sum = lax.broadcasted_iota(jnp.int32, (2 * LANES, 2 * LANES), 1)
    halves = jnp.where(
        ((row_sum & (LANES - 1)) >= LANES // 2) == (col_sum >= LANES), 1.0, 0.0
    ).astype(jnp.bfloat16)
    row16 = lax.broadcasted_iota(jnp.int32, (16, LANES), 0)
    keeps = [jnp.where((row16 & 7) == sub, 1.0, 0.0).astype(jnp.bfloat16) for sub in range(8)]

    def fetch(first):
        row = first >> 7
        base = first & (LANES - 1)
        for index in range(CHUNK):
            near = words[row, base + index]
            far = words[slot_rows + row, base + index]
            gathered[pl.ds(index, 1), :] = table[pl.ds(near, 1), :]
            gathered[pl.ds(CHUNK + index, 1), :] = table[pl.ds(far, 1), :]

    def arrange(first):
        def keep_part(slot, value):
            parts[pl.ds(pl.multiple_of(slot * slots + first, 8), CHUNK), :] = value

        packed = gathered[...]

        def spread(column):
            return jnp.take_along_axis(
                packed, column_of + column, axis=1, mode="promise_in_bounds"
            )

        kind_low = jnp.take_along_axis(
            packed, jnp.where(pick_low, 9, PARAMS + 9), axis=1, mode="promise_in_bounds"
        )
        pick = jnp.where(pick_all & (kind_low == lane_f), 1.0, 0.0).astype(jnp.bfloat16)
        offsets = jnp.dot(pick, off_ref[...], preferred_element_type=jnp.float32)
        turns = [spread(3 + entry) for entry in range(6)]
        for mode in range(3):
            after, last = (mode + 1) % 3, (mode + 2) % 3
            turns.append(turns[after] * turns[3 + last] - turns[last] * turns[3 + after])
        where_at = []
        for axis in range(3):
            value = spread(axis)
            for mode in range(3):
                value = value + turns[3 * axis + mode] * offsets[:, mode * LANES : (mode + 1) * LANES]
            where_at.append(value)
        near = [value[:CHUNK] for value in where_at]
        far = [value[CHUNK:] for value in where_at]
        near_sq = near[0] * near[0] + near[1] * near[1] + near[2] * near[2]
        far_sq = far[0] * far[0] + far[1] * far[1] + far[2] * far[2]
        for axis, value in enumerate(near + [REACH_SQUARED - near_sq]):
            for part, piece in enumerate(split3(value)):
                keep_part(4 * part + axis, piece)
        for axis, value in enumerate([2.0 * value for value in far] + [-far_sq]):
            for part, piece in enumerate(split3(value)):
                keep_part(12 + 4 * part + axis, piece)
        for axis in range(3):
            keep_part(24 + axis, far[axis])

    one8 = jnp.ones((8, LANES), jnp.float32)

    def choose(first, second, third):
        return jnp.where(row_first, first, jnp.where(row_second, second, third))

    def prepare(base):
        def part(slot):
            return parts[pl.ds(slot * slots + base, 8), :]

        near = [[part(4 * which + axis) for axis in range(4)] for which in range(3)]
        far = [[part(12 + 4 * which + axis) for axis in range(4)] for which in range(3)]
        rows_a, rows_b = [], []
        for a, b, a_last, b_last in (
            (0, 0, near[0][3], one8),
            (0, 1, one8, far[1][3]),
            (1, 0, near[1][3], one8),
            (1, 1, one8, far[0][3]),
            (0, 2, one8, far[2][3]),
            (2, 0, near[2][3], one8),
        ):
            rows_a += near[a][:3] + [a_last]
            rows_b += far[b][:3] + [b_last]
        all_a = jnp.concatenate(rows_a, 0).astype(jnp.bfloat16)
        tiles_b = [
            jnp.concatenate(rows_b[2 * tile : 2 * tile + 2], 0).astype(jnp.bfloat16)
            for tile in range(12)
        ]
        return all_a, tiles_b

    def reach_of(all_a, tiles_b, pair):
        side_b = jnp.concatenate(
            [jnp.concatenate([tile * keeps[sub] for tile in tiles_b], 0) for sub in pair], 1
        )
        return lax.dot_general(
            all_a, side_b, (((0,), (0,)), ((), ())), preferred_element_type=jnp.float32
        )

    def sums_of(reach, base, pair):
        weight = jnp.maximum(reach, 0.0)
        weight_high = weight.astype(jnp.bfloat16)
        weight_low = (weight - weight_high.astype(jnp.float32)).astype(jnp.bfloat16)
        side_c = []
        for sub in pair:
            for which in range(3):
                row = choose(
                    *[
                        parts[pl.ds((4 * which + axis) * slots + base + sub, 8, stride=0), :]
                        for axis in range(3)
                    ]
                )
                side_c.append(jnp.where(half8, row, 0.0))
            side_c.append(ones_half)
        side_c = jnp.concatenate(side_c, 0).astype(jnp.bfloat16)
        return jnp.dot(
            jnp.concatenate([side_c, side_c], 1),
            jnp.concatenate([weight_high, weight_low], 0),
            preferred_element_type=jnp.float32,
        )

    def terms_of(sums, base, pair):
        terms = []
        for place, sub in enumerate(pair):
            mine = sums[32 * place : 32 * place + 32, LANES * place : LANES * place + LANES]
            axes = [
                parts[pl.ds((24 + axis) * slots + base + sub, 8, stride=0), :] for axis in range(3)
            ]
            force = mine[24:32] * choose(*axes) - (mine[0:8] + mine[8:16] + mine[16:24])
            terms += [
                force,
                force * choose(axes[1], axes[2], axes[0]),
                force * choose(axes[2], axes[0], axes[1]),
            ]
        terms = jnp.concatenate(terms, 0)
        terms_high = terms.astype(jnp.bfloat16)
        terms_low = (terms - terms_high.astype(jnp.float32)).astype(jnp.bfloat16)
        return jnp.concatenate([terms_high, terms_low], 1)

    def scatter(group):
        base = jnp.clip(group, 0, groups - 1) * 8
        row = base >> 7
        spot = base & (LANES - 1)
        for sub in range(8):
            lower = folded_ref[pl.ds(24 * sub, 24), :LANES]
            upper = folded_ref[pl.ds(24 * sub, 24), LANES:]
            live = (group >= 0) & (group * 8 + sub < number)
            block = words[row, spot + sub]
            here = lane24 == jnp.where(live, block & (LANES - 1), -1)
            at = pl.ds(pl.multiple_of((block >> 7) * 24, 8), 24)
            acc_near[at, :] += jnp.where(here, lower + upper, 0.0)
            block = words[slot_rows + row, spot + sub]
            here = lane24 == jnp.where(live, block & (LANES - 1), -1)
            at = pl.ds(pl.multiple_of((block >> 7) * 48, 8), 48)
            acc_far[at, :] += jnp.concatenate(
                [jnp.where(here, lower, 0.0), jnp.where(here, upper, 0.0)], 0
            )

    def chunk(turn, carry):
        arrange(pl.multiple_of(turn * CHUNK, CHUNK))
        fetch(jnp.minimum((turn + 1) * CHUNK, slots - CHUNK))
        return carry

    fetch(jnp.int32(0))
    lax.fori_loop(0, (number + CHUNK - 1) // CHUNK, chunk, 0)

    groups = (number + 7) // 8
    pairs = [(2 * couple, 2 * couple + 1) for couple in range(4)]

    def octet(turn, slot):
        fresh = 4 * LANES * slot
        stale = 4 * LANES * (1 - slot)
        ready = prepare(pl.multiple_of(jnp.minimum(turn, groups - 1) * 8, 8))
        for couple, pair in enumerate(pairs):
            reach_ref[pl.ds(fresh + LANES * couple, LANES), :] = reach_of(*ready, pair)
        scatter(turn - 3)
        base = jnp.clip(turn - 2, 0, groups - 1) * 8
        terms = [
            terms_of(sums_ref[pl.ds(64 * couple, 64), :], base, pair)
            for couple, pair in enumerate(pairs)
        ]
        folded_ref[...] = jnp.dot(
            jnp.concatenate(terms, 0), halves, preferred_element_type=jnp.float32
        )
        base = jnp.clip(turn - 1, 0, groups - 1) * 8
        for couple, pair in enumerate(pairs):
            sums_ref[pl.ds(64 * couple, 64), :] = sums_of(
                reach_ref[pl.ds(stale + LANES * couple, LANES), :], base, pair
            )

    def octets(turn, carry):
        for sub in range(DEPTH):
            octet(DEPTH * turn + sub, sub % 2)
        return carry

    lax.fori_loop(0, (groups + 2 + DEPTH) // DEPTH, octets, 0)

    def total_of(row, half, tiles, start):
        line = (row // 3) * 8 + row % 3
        mine = acc_near[pl.ds(start * 24 + line + 4 * half, tiles, stride=24), :]
        line += 24 * half
        other = (
            acc_far[pl.ds(start * 48 + line, tiles, stride=48), :]
            + acc_far[pl.ds(start * 48 + line + 4, tiles, stride=48), :]
        )
        return (other - mine) * STIFFNESS

    def results_of(half, tiles, start):
        rows = [total_of(row, half, tiles, start) for row in range(9)]
        return rows[0:3] + [
            rows[6 + (axis + 2) % 3] - rows[3 + (axis + 1) % 3] for axis in range(3)
        ]

    inner_tiles = inner_blocks // LANES
    for half in range(2):
        for axis, value in enumerate(results_of(half, inner_tiles, 0)):
            inner_ref[pl.ds(6 * half + axis, inner_tiles, stride=COMPS), :] = value
        for axis, value in enumerate(results_of(half, 2, inner_tiles)):
            at = pl.ds(6 * half + axis, 1)
            edge_in_ref[at, :] = jnp.where(even, value[1:2], value[0:1])
            edge_over_ref[at, :] = jnp.where(even, value[0:1], value[1:2])


def swaps(count):
    inside = [(i, i ^ 1) for i in range(count)]
    across = [(i, (i + 1) % count if i % 2 else (i - 1) % count) for i in range(count)]
    return inside, across


def shards(positions, rotations, clump_kind, sub_offsets, pair_blocks, pair_count):
    members = lax.axis_size("dev")
    groups = lax.axis_size("grp")
    group = lax.axis_index("grp")
    me = lax.axis_index("dev")
    rings = members // 2
    clique, far = me % rings, me // rings
    clumps = positions.shape[1]
    slots = pair_blocks.shape[1]
    own_blocks = clumps // 2
    kinds, _, subs = sub_offsets.shape
    even = group % 2 == 0
    inside, across = swaps(groups)
    vmem = pl.BlockSpec(memory_space=pltpu.VMEM)
    smem = pl.BlockSpec(memory_space=pltpu.SMEM)

    payload = pl.pallas_call(
        functools.partial(payload_kernel, slots, members),
        out_shape=jax.ShapeDtypeStruct((ROWS, own_blocks), jnp.float32),
        in_specs=[vmem] * 4 + [smem],
        out_specs=vmem,
        name="payload_kernel",
    )(positions, rotations, clump_kind.reshape(-1, LANES), pair_blocks, pair_count)

    def trade(value, k):
        return lax.ppermute(value, "dev", [(i, i ^ k) for i in range(members)])

    both = jnp.stack([payload, trade(payload, rings)])
    order = clique_order(rings)
    pieces = [both] + [trade(both, k) for k in order[1:]]

    def piece_columns(member, start):
        found = None
        for k, piece in zip(order, pieces):
            part = piece[:, :, start : start + RIM]
            part = jnp.where(far == member // rings, part[0], part[1])
            hit = clique ^ k == member % rings
            found = part if found is None else jnp.where(hit, part, found)
        return found

    first = piece_columns(0, 0)
    last = piece_columns(members - 1, own_blocks - RIM)
    got_across = lax.ppermute(jnp.where(even, first, last), "grp", across)
    got_inside = lax.ppermute(jnp.where(even, last, first), "grp", inside)

    offset_table = sub_offsets.astype(jnp.float32) * OFFSET_UNIT
    blank = jnp.zeros_like(offset_table)
    offset_rows = jnp.concatenate(
        [
            jnp.concatenate([offset_table, blank], 2).reshape(kinds, -1),
            jnp.concatenate([blank, offset_table], 2).reshape(kinds, -1),
        ],
        0,
    )
    offset_rows = jnp.concatenate(
        [offset_rows, jnp.zeros((LANES - 2 * kinds, offset_rows.shape[1]), jnp.float32)], 0
    ).astype(jnp.bfloat16)

    inner_blocks = own_blocks * members
    tiles = inner_blocks // LANES
    inner, edge_in, edge_over = pl.pallas_call(
        functools.partial(pair_kernel, members, slots),
        out_shape=(
            jax.ShapeDtypeStruct((tiles * COMPS, LANES), jnp.float32),
            jax.ShapeDtypeStruct((COMPS, LANES), jnp.float32),
            jax.ShapeDtypeStruct((COMPS, LANES), jnp.float32),
        ),
        in_specs=[vmem] * (rings + 3),
        out_specs=(vmem, vmem, vmem),
        scratch_shapes=[
            pltpu.VMEM((inner_blocks + 2 * RIM, LANES), jnp.float32),
            pltpu.VMEM((members * 2 * slots // LANES, LANES), jnp.float32),
            pltpu.VMEM((2 * slots // LANES, LANES), jnp.int32),
            pltpu.SMEM((2 * slots // LANES, LANES), jnp.int32),
            pltpu.VMEM((2 * CHUNK, LANES), jnp.float32),
            pltpu.VMEM((27 * slots, LANES), jnp.float32),
            pltpu.VMEM((8 * LANES, 2 * LANES), jnp.float32),
            pltpu.VMEM((4 * 64, 2 * LANES), jnp.float32),
            pltpu.VMEM((192, 2 * LANES), jnp.float32),
            pltpu.VMEM(((tiles + 2) * 24, LANES), jnp.float32),
            pltpu.VMEM(((tiles + 2) * 48, LANES), jnp.float32),
            pltpu.SemaphoreType.DMA,
        ],
        name="pair_kernel",
    )(*pieces, got_inside, got_across, offset_rows)

    got_over = lax.ppermute(edge_over, "grp", across)
    got_in = lax.ppermute(edge_in, "grp", inside)
    below = jnp.where(group > 0, jnp.where(even, got_over, got_in), 0.0)
    above = jnp.where(group < groups - 1, jnp.where(even, got_in, got_over), 0.0)
    inner = inner + jnp.concatenate(
        [below, jnp.zeros(((tiles - 2) * COMPS, LANES), jnp.float32), above], 0
    )

    own_rows = tiles * COMPS // members
    ranks = inner.reshape(2, rings, own_rows, LANES)

    def share(k):
        return lax.dynamic_index_in_dim(ranks, clique ^ k, 1, False)

    column = share(0)
    for k in order[:0:-1]:
        column = column + trade(share(k), k)
    kept = lax.dynamic_index_in_dim(column, far, 0, False)
    shares = [kept, trade(lax.dynamic_index_in_dim(column, 1 - far, 0, False), rings)]
    clump_force, clump_torque = pl.pallas_call(
        finish_kernel,
        out_shape=(jax.ShapeDtypeStruct((3, clumps), jnp.float32),) * 2,
        in_specs=[vmem] * 3,
        out_specs=(vmem, vmem),
        scratch_shapes=[pltpu.VMEM((own_rows, LANES), jnp.float32)],
        name="finish_kernel",
    )(*shares, positions)
    return (clump_force, clump_torque)


def solution(mesh):
    placed = (
        P(None, ("grp", "dev")),
        P(None, ("grp", "dev")),
        P(("grp", "dev")),
        P(),
        P(None, ("grp", "dev")),
        P(("grp", "dev")),
    )
    return jax.shard_map(
        shards,
        mesh=mesh,
        in_specs=placed,
        out_specs=(P(None, ("grp", "dev")), P(None, ("grp", "dev"))),
        check_vma=False,
    )
```

```python
import functools

import jax
import jax.numpy as jnp
from jax import lax
from jax.experimental import pallas as pl
from jax.experimental.pallas import tpu as pltpu
from jax.sharding import PartitionSpec as P

RIM = 128
LANES = 128
OFFSET_UNIT = 0.125
REACH_SQUARED = 4.0
STIFFNESS = 1.0 / 256.0
CHUNK = 64
COMPS = 12
PARAMS = 10
ROWS = 24
RIM_ROWS = 16
DEPTH = 4


def split3(value):
    high = value.astype(jnp.bfloat16).astype(jnp.float32)
    rest = value - high
    middle = rest.astype(jnp.bfloat16).astype(jnp.float32)
    return high, middle, rest - middle


def clique_order(count):
    return [0, count - 1] + list(range(1, count - 1))


def payload_kernel(slots, members, position_ref, rotation_ref, kind_ref, pair_ref, count_ref, out_ref, end_ref):
    clumps = position_ref.shape[1]
    blocks = clumps // 2
    inner_blocks = blocks * members
    wide = 2 * LANES
    row = lax.broadcasted_iota(jnp.int32, (wide, wide), 0)
    column = lax.broadcasted_iota(jnp.int32, (wide, wide), 1)
    source = jnp.where(column < LANES, 2 * column, 2 * column - (wide - 1))
    picked = jnp.where(row == source, 1.0, 0.0).astype(jnp.bfloat16)
    parts = []
    for turn in range(clumps // wide):
        at = slice(turn * wide, (turn + 1) * wide)
        kinds = kind_ref[2 * turn : 2 * turn + 2, :].astype(jnp.float32)
        value = jnp.concatenate(
            [
                position_ref[:, at],
                rotation_ref[0:6, at],
                jnp.concatenate([kinds[0:1], kinds[1:2]], 1),
                jnp.zeros((16 - PARAMS, wide), jnp.float32),
            ],
            0,
        )
        parts += [piece.astype(jnp.bfloat16) for piece in split3(value)]
    sorted_parts = jnp.dot(
        jnp.concatenate(parts, 0), picked, preferred_element_type=jnp.float32
    )
    for turn in range(clumps // wide):
        high, middle, low = (sorted_parts[16 * (3 * turn + part) : 16 * (3 * turn + part) + 16] for part in range(3))
        value = (high + middle) + low
        at = slice(turn * LANES, (turn + 1) * LANES)
        out_ref[0:PARAMS, at] = value[0:PARAMS, :LANES]
        out_ref[PARAMS : 2 * PARAMS, at] = value[0:PARAMS, LANES:]
    pairs = pair_ref[...] - lax.axis_index("grp") * inner_blocks
    pairs = jnp.where(
        pairs < 0,
        pairs + inner_blocks + RIM,
        jnp.where(pairs >= inner_blocks, pairs + RIM, pairs),
    )
    live = lax.broadcasted_iota(jnp.int32, pairs.shape, 1) < count_ref[0]
    pairs = jnp.where(live, pairs, -1).astype(jnp.float32)
    lists = slots // blocks
    for which in range(2):
        for part in range(lists):
            out_ref[pl.ds(2 * PARAMS + which * lists + part, 1), :] = pairs[
                which : which + 1, part * blocks : (part + 1) * blocks
            ]
    in_low = lax.axis_index("dev") < members // 2
    end_ref[...] = jnp.where(in_low, out_ref[:, :RIM], out_ref[:, blocks - RIM :])


def finish_kernel(members, groups, own_ref, *refs):
    other_ref, rim_a_ref, rim_b_ref, position_ref, force_ref, torque_ref, total_ref = refs
    me, group = lax.axis_index("dev"), lax.axis_index("grp")
    total_ref[...] = own_ref[...] + other_ref[...]
    rim = rim_a_ref[0:COMPS] + rim_b_ref[0:COMPS]
    first = (me == 0) & (group > 0)
    final = (me == members - 1) & (group < groups - 1)
    total_ref[0:COMPS] += jnp.where(first, rim, 0.0)
    total_ref[own_ref.shape[0] - COMPS :] += jnp.where(final, rim, 0.0)
    tiles = own_ref.shape[0] // COMPS
    wide = 2 * LANES
    row = lax.broadcasted_iota(jnp.int32, (wide, wide), 0)
    column = lax.broadcasted_iota(jnp.int32, (wide, wide), 1)
    target = jnp.where(row < LANES, 2 * row, 2 * row - (wide - 1))
    placed = jnp.where(column == target, 1.0, 0.0).astype(jnp.bfloat16)
    halves = [
        jnp.concatenate(
            [total_ref[pl.ds(6 * half + comp, tiles, stride=COMPS), :] for comp in range(6)], 0
        )
        for half in range(2)
    ]
    value = jnp.concatenate(halves, 1)
    rows = value.shape[0]
    joined = jnp.dot(
        jnp.concatenate([part.astype(jnp.bfloat16) for part in split3(value)], 0),
        placed,
        preferred_element_type=jnp.float32,
    )
    value = (joined[0:rows] + joined[rows : 2 * rows]) + joined[2 * rows : 3 * rows]
    comps = [value[comp * tiles : (comp + 1) * tiles] for comp in range(6)]
    centre = [
        jnp.concatenate(
            [position_ref[axis : axis + 1, tile * wide : (tile + 1) * wide] for tile in range(tiles)], 0
        )
        for axis in range(3)
    ]
    for axis in range(3):
        after, last = (axis + 1) % 3, (axis + 2) % 3
        torque = comps[3 + axis] - (centre[after] * comps[last] - centre[last] * comps[after])
        for tile in range(tiles):
            at = slice(tile * wide, (tile + 1) * wide)
            force_ref[axis : axis + 1, at] = comps[axis][tile : tile + 1]
            torque_ref[axis : axis + 1, at] = torque[tile : tile + 1]


def pair_kernel(members, slots, *refs):
    piece_count = members // 2
    pieces = refs[:piece_count]
    off_ref = refs[piece_count]
    outs = refs[piece_count + 1 : 2 * piece_count + 1]
    (table, list_ref, word_ref, words, gathered, parts, reach_ref, sums_ref, folded_ref, acc_near,
     acc_far, sem) = refs[2 * piece_count + 1 :]
    me = lax.axis_index("dev")
    clique = lax.rem(me, piece_count)
    own_blocks = (pieces[0].shape[1] - RIM) // 2
    inner_blocks = members * own_blocks
    slot_rows = slots // LANES
    lists = slots // own_blocks

    owners = []
    counts = []
    for k in range(piece_count):
        for side in range(2):
            owners.append(jnp.bitwise_xor(me, clique_order(piece_count)[k] + side * piece_count))
            base = (2 * k + side) * 2 * slot_rows
            for part in range(2 * slot_rows):
                line, spot = part // (own_blocks // LANES), part % (own_blocks // LANES)
                at = side * own_blocks + spot * LANES
                list_ref[pl.ds(base + part, 1), :] = pieces[k][
                    pl.ds(2 * PARAMS + line, 1), at : at + LANES
                ]
            found = jnp.where(list_ref[pl.ds(base, slot_rows), :] >= 0.0, 1.0, 0.0)
            counts.append(jnp.sum(found).astype(jnp.int32))
    starts = []
    total = jnp.int32(0)
    for index in range(members):
        start = jnp.int32(0)
        for other in range(members):
            if other != index:
                start = start + jnp.where(owners[other] < owners[index], counts[other], 0)
        starts.append(start)
        total = total + counts[index]
    begin = (total * me) // members
    finish = (total * (me + 1)) // members
    number = finish - begin

    flat = lax.broadcasted_iota(jnp.int32, (slot_rows, LANES), 0) * LANES
    column = lax.broadcasted_iota(jnp.int32, (slot_rows, LANES), 1)
    flat = flat + column
    near_list = jnp.zeros((slot_rows, LANES), jnp.float32)
    far_list = jnp.zeros((slot_rows, LANES), jnp.float32)
    for index in range(members):
        start = starts[index]
        low = jnp.maximum(start, begin) - begin
        high = jnp.minimum(start + counts[index], finish) - begin
        shift = jnp.bitwise_and(start - begin, slots - 1)
        wanted = (flat >= low) & (flat < high)

        def moved(rows, shift=shift):
            turned = pltpu.roll(rows, shift & (LANES - 1), axis=1)
            same = pltpu.roll(turned, shift >> 7, axis=0)
            following = pltpu.roll(turned, (shift >> 7) + 1, axis=0)
            return jnp.where(column < (shift & (LANES - 1)), following, same)

        base = index * 2 * slot_rows
        near_list = jnp.where(wanted, moved(list_ref[pl.ds(base, slot_rows), :]), near_list)
        far_list = jnp.where(wanted, moved(list_ref[pl.ds(base + slot_rows, slot_rows), :]), far_list)
    word_ref[pl.ds(0, slot_rows), :] = near_list.astype(jnp.int32)
    word_ref[pl.ds(slot_rows, slot_rows), :] = far_list.astype(jnp.int32)
    copy = pltpu.make_async_copy(word_ref, words, sem)
    copy.start()

    for k in range(piece_count):
        for side in range(2):
            base = pl.multiple_of(owners[2 * k + side] * own_blocks, LANES)
            for tile in range(own_blocks // LANES):
                at = side * own_blocks + tile * LANES
                table[pl.ds(base + tile * LANES, LANES), 0:ROWS] = pieces[k][:, at : at + LANES].T
        place = jnp.bitwise_xor(clique, clique_order(piece_count)[k])
        base = jnp.where(place == 0, RIM, jnp.where(place == piece_count - 1, 0, 2 * RIM))
        table[pl.ds(pl.multiple_of(inner_blocks + base, RIM), RIM), 0:ROWS] = pieces[k][
            :, 2 * own_blocks :
        ].T

    def clear(turn, carry):
        acc_near[pl.ds(pl.multiple_of(turn * 48, 8), 48), :] = jnp.zeros((48, LANES), jnp.float32)
        acc_far[pl.ds(pl.multiple_of(turn * 96, 8), 96), :] = jnp.zeros((96, LANES), jnp.float32)
        return carry

    lax.fori_loop(0, acc_near.shape[0] // 48, clear, 0)

    copy.wait()

    lane = lax.broadcasted_iota(jnp.int32, (2 * CHUNK, LANES), 1)
    column_of = jnp.where(lane < LANES // 2, 0, PARAMS)
    lane_f = (lane & 7).astype(jnp.float32)
    pick_low = lane < 8
    pick_all = lane < 16
    lane24 = lax.broadcasted_iota(jnp.int32, (24, LANES), 1)
    row8 = lax.broadcasted_iota(jnp.int32, (8, LANES), 0)
    lane8 = lax.broadcasted_iota(jnp.int32, (8, LANES), 1)
    row_first = (row8 & 3) == 0
    row_second = (row8 & 3) == 1
    half8 = (row8 < 4) == (lane8 < LANES // 2)
    ones_half = jnp.where(half8, 1.0, 0.0)
    row_sum = lax.broadcasted_iota(jnp.int32, (2 * LANES, 2 * LANES), 0)
    col_sum = lax.broadcasted_iota(jnp.int32, (2 * LANES, 2 * LANES), 1)
    halves = jnp.where(
        ((row_sum & (LANES - 1)) >= LANES // 2) == (col_sum >= LANES), 1.0, 0.0
    ).astype(jnp.bfloat16)
    row16 = lax.broadcasted_iota(jnp.int32, (16, LANES), 0)
    keeps = [jnp.where((row16 & 7) == sub, 1.0, 0.0).astype(jnp.bfloat16) for sub in range(8)]

    def fetch(first):
        row = first >> 7
        base = first & (LANES - 1)
        for index in range(CHUNK):
            near = words[row, base + index]
            far = words[slot_rows + row, base + index]
            gathered[pl.ds(index, 1), :] = table[pl.ds(near, 1), :]
            gathered[pl.ds(CHUNK + index, 1), :] = table[pl.ds(far, 1), :]

    def arrange(first):
        def keep_part(slot, value):
            parts[pl.ds(pl.multiple_of(slot * slots + first, 8), CHUNK), :] = value

        packed = gathered[...]

        def spread(column):
            return jnp.take_along_axis(
                packed, column_of + column, axis=1, mode="promise_in_bounds"
            )

        kind_low = jnp.take_along_axis(
            packed, jnp.where(pick_low, 9, PARAMS + 9), axis=1, mode="promise_in_bounds"
        )
        pick = jnp.where(pick_all & (kind_low == lane_f), 1.0, 0.0).astype(jnp.bfloat16)
        offsets = jnp.dot(pick, off_ref[...], preferred_element_type=jnp.float32)
        turns = [spread(3 + entry) for entry in range(6)]
        for mode in range(3):
            after, last = (mode + 1) % 3, (mode + 2) % 3
            turns.append(turns[after] * turns[3 + last] - turns[last] * turns[3 + after])
        where_at = []
        for axis in range(3):
            value = spread(axis)
            for mode in range(3):
                value = value + turns[3 * axis + mode] * offsets[:, mode * LANES : (mode + 1) * LANES]
            where_at.append(value)
        near = [value[:CHUNK] for value in where_at]
        far = [value[CHUNK:] for value in where_at]
        near_sq = near[0] * near[0] + near[1] * near[1] + near[2] * near[2]
        far_sq = far[0] * far[0] + far[1] * far[1] + far[2] * far[2]
        for axis, value in enumerate(near + [REACH_SQUARED - near_sq]):
            for part, piece in enumerate(split3(value)):
                keep_part(4 * part + axis, piece)
        for axis, value in enumerate([2.0 * value for value in far] + [-far_sq]):
            for part, piece in enumerate(split3(value)):
                keep_part(12 + 4 * part + axis, piece)
        for axis in range(3):
            keep_part(24 + axis, far[axis])

    one8 = jnp.ones((8, LANES), jnp.float32)

    def choose(first, second, third):
        return jnp.where(row_first, first, jnp.where(row_second, second, third))

    def prepare(base):
        def part(slot):
            return parts[pl.ds(slot * slots + base, 8), :]

        near = [[part(4 * which + axis) for axis in range(4)] for which in range(3)]
        far = [[part(12 + 4 * which + axis) for axis in range(4)] for which in range(3)]
        rows_a, rows_b = [], []
        for a, b, a_last, b_last in (
            (0, 0, near[0][3], one8),
            (0, 1, one8, far[1][3]),
            (1, 0, near[1][3], one8),
            (1, 1, one8, far[0][3]),
            (0, 2, one8, far[2][3]),
            (2, 0, near[2][3], one8),
        ):
            rows_a += near[a][:3] + [a_last]
            rows_b += far[b][:3] + [b_last]
        all_a = jnp.concatenate(rows_a, 0).astype(jnp.bfloat16)
        tiles_b = [
            jnp.concatenate(rows_b[2 * tile : 2 * tile + 2], 0).astype(jnp.bfloat16)
            for tile in range(12)
        ]
        return all_a, tiles_b

    def reach_of(all_a, tiles_b, pair):
        side_b = jnp.concatenate(
            [jnp.concatenate([tile * keeps[sub] for tile in tiles_b], 0) for sub in pair], 1
        )
        return lax.dot_general(
            all_a, side_b, (((0,), (0,)), ((), ())), preferred_element_type=jnp.float32
        )

    def sums_of(reach, base, pair):
        weight = jnp.maximum(reach, 0.0)
        weight_high = weight.astype(jnp.bfloat16)
        weight_low = (weight - weight_high.astype(jnp.float32)).astype(jnp.bfloat16)
        side_c = []
        for sub in pair:
            for which in range(3):
                row = choose(
                    *[
                        parts[pl.ds((4 * which + axis) * slots + base + sub, 8, stride=0), :]
                        for axis in range(3)
                    ]
                )
                side_c.append(jnp.where(half8, row, 0.0))
            side_c.append(ones_half)
        side_c = jnp.concatenate(side_c, 0).astype(jnp.bfloat16)
        return jnp.dot(
            jnp.concatenate([side_c, side_c], 1),
            jnp.concatenate([weight_high, weight_low], 0),
            preferred_element_type=jnp.float32,
        )

    def terms_of(sums, base, pair):
        terms = []
        for place, sub in enumerate(pair):
            mine = sums[32 * place : 32 * place + 32, LANES * place : LANES * place + LANES]
            axes = [
                parts[pl.ds((24 + axis) * slots + base + sub, 8, stride=0), :] for axis in range(3)
            ]
            force = mine[24:32] * choose(*axes) - (mine[0:8] + mine[8:16] + mine[16:24])
            terms += [
                force,
                force * choose(axes[1], axes[2], axes[0]),
                force * choose(axes[2], axes[0], axes[1]),
            ]
        terms = jnp.concatenate(terms, 0)
        terms_high = terms.astype(jnp.bfloat16)
        terms_low = (terms - terms_high.astype(jnp.float32)).astype(jnp.bfloat16)
        return jnp.concatenate([terms_high, terms_low], 1)

    def scatter(group):
        base = jnp.clip(group, 0, groups - 1) * 8
        row = base >> 7
        spot = base & (LANES - 1)
        for sub in range(8):
            lower = folded_ref[pl.ds(24 * sub, 24), :LANES]
            upper = folded_ref[pl.ds(24 * sub, 24), LANES:]
            live = (group >= 0) & (group * 8 + sub < number)
            block = words[row, spot + sub]
            here = lane24 == jnp.where(live, block & (LANES - 1), -1)
            at = pl.ds(pl.multiple_of((block >> 7) * 24, 8), 24)
            acc_near[at, :] += jnp.where(here, lower + upper, 0.0)
            block = words[slot_rows + row, spot + sub]
            here = lane24 == jnp.where(live, block & (LANES - 1), -1)
            at = pl.ds(pl.multiple_of((block >> 7) * 48, 8), 48)
            acc_far[at, :] += jnp.concatenate(
                [jnp.where(here, lower, 0.0), jnp.where(here, upper, 0.0)], 0
            )

    def chunk(turn, carry):
        arrange(pl.multiple_of(turn * CHUNK, CHUNK))
        fetch(jnp.minimum((turn + 1) * CHUNK, slots - CHUNK))
        return carry

    fetch(jnp.int32(0))
    lax.fori_loop(0, (number + CHUNK - 1) // CHUNK, chunk, 0)

    groups = (number + 7) // 8
    pairs = [(2 * couple, 2 * couple + 1) for couple in range(4)]

    def octet(turn, slot):
        fresh = 4 * LANES * slot
        stale = 4 * LANES * (1 - slot)
        ready = prepare(pl.multiple_of(jnp.minimum(turn, groups - 1) * 8, 8))
        for couple, pair in enumerate(pairs):
            reach_ref[pl.ds(fresh + LANES * couple, LANES), :] = reach_of(*ready, pair)
        scatter(turn - 3)
        base = jnp.clip(turn - 2, 0, groups - 1) * 8
        terms = [
            terms_of(sums_ref[pl.ds(64 * couple, 64), :], base, pair)
            for couple, pair in enumerate(pairs)
        ]
        folded_ref[...] = jnp.dot(
            jnp.concatenate(terms, 0), halves, preferred_element_type=jnp.float32
        )
        base = jnp.clip(turn - 1, 0, groups - 1) * 8
        for couple, pair in enumerate(pairs):
            sums_ref[pl.ds(64 * couple, 64), :] = sums_of(
                reach_ref[pl.ds(stale + LANES * couple, LANES), :], base, pair
            )

    def octets(turn, carry):
        for sub in range(DEPTH):
            octet(DEPTH * turn + sub, sub % 2)
        return carry

    lax.fori_loop(0, (groups + 2 + DEPTH) // DEPTH, octets, 0)

    def total_of(row, half, tiles, start):
        line = (row // 3) * 8 + row % 3
        mine = acc_near[pl.ds(start * 24 + line + 4 * half, tiles, stride=24), :]
        line += 24 * half
        other = (
            acc_far[pl.ds(start * 48 + line, tiles, stride=48), :]
            + acc_far[pl.ds(start * 48 + line + 4, tiles, stride=48), :]
        )
        return (other - mine) * STIFFNESS

    def results_of(half, tiles, start):
        rows = [total_of(row, half, tiles, start) for row in range(9)]
        return rows[0:3] + [
            rows[6 + (axis + 2) % 3] - rows[3 + (axis + 1) % 3] for axis in range(3)
        ]

    own_tiles = own_blocks // LANES
    own_rows = own_tiles * COMPS
    edges = [results_of(half, 2, inner_blocks // LANES) for half in range(2)]
    for k, out in zip(clique_order(piece_count), outs):
        place = jnp.bitwise_xor(clique, k)
        for side in range(2):
            start = (side * piece_count + place) * own_tiles
            for half in range(2):
                for axis, value in enumerate(results_of(half, own_tiles, start)):
                    at = pl.ds(side * own_rows + 6 * half + axis, own_tiles, stride=COMPS)
                    out[at, :] = value
        out[pl.ds(2 * own_rows, RIM_ROWS), :] = jnp.zeros((RIM_ROWS, LANES), jnp.float32)
        for half in range(2):
            for axis, value in enumerate(edges[half]):
                rim = jnp.where(place == 0, value[1:2], value[0:1])
                rim = jnp.where((place == 0) | (place == piece_count - 1), rim, 0.0)
                out[pl.ds(2 * own_rows + 6 * half + axis, 1), :] = rim


def shards(positions, rotations, clump_kind, sub_offsets, pair_blocks, pair_count):
    members = lax.axis_size("dev")
    groups = lax.axis_size("grp")
    group = lax.axis_index("grp")
    me = lax.axis_index("dev")
    rings = members // 2
    clique, far = me % rings, me // rings
    clumps = positions.shape[1]
    slots = pair_blocks.shape[1]
    own_blocks = clumps // 2
    kinds, _, subs = sub_offsets.shape
    vmem = pl.BlockSpec(memory_space=pltpu.VMEM)
    smem = pl.BlockSpec(memory_space=pltpu.SMEM)

    payload, end = pl.pallas_call(
        functools.partial(payload_kernel, slots, members),
        out_shape=(
            jax.ShapeDtypeStruct((ROWS, own_blocks), jnp.float32),
            jax.ShapeDtypeStruct((ROWS, RIM), jnp.float32),
        ),
        in_specs=[vmem] * 4 + [smem],
        out_specs=(vmem, vmem),
        name="payload_kernel",
    )(positions, rotations, clump_kind.reshape(-1, LANES), pair_blocks, pair_count)

    def trade(value, k):
        return lax.ppermute(value, "dev", [(i, i ^ k) for i in range(members)])

    def cross(value, step, flip):
        steps = [
            (
                g * members + d,
                (g + (step if d < rings else -step)) % groups * members + (d ^ flip),
            )
            for g in range(groups)
            for d in range(members)
        ]
        return lax.ppermute(value, ("grp", "dev"), steps)

    rim_a, rim_b = cross(end, -1, 0), cross(end, -1, rings)
    far_payload = trade(payload, rings)
    rim = jnp.where((clique == 0) == (far == 0), rim_a, rim_b)
    both = jnp.concatenate([payload, far_payload, rim], 1)
    order = clique_order(rings)
    pieces = [both] + [trade(both, k) for k in order[1:]]

    offset_table = sub_offsets.astype(jnp.float32) * OFFSET_UNIT
    blank = jnp.zeros_like(offset_table)
    offset_rows = jnp.concatenate(
        [
            jnp.concatenate([offset_table, blank], 2).reshape(kinds, -1),
            jnp.concatenate([blank, offset_table], 2).reshape(kinds, -1),
        ],
        0,
    )
    offset_rows = jnp.concatenate(
        [offset_rows, jnp.zeros((LANES - 2 * kinds, offset_rows.shape[1]), jnp.float32)], 0
    ).astype(jnp.bfloat16)

    inner_blocks = own_blocks * members
    tiles = inner_blocks // LANES
    own_rows = own_blocks // LANES * COMPS
    outs = pl.pallas_call(
        functools.partial(pair_kernel, members, slots),
        out_shape=(jax.ShapeDtypeStruct((2 * own_rows + RIM_ROWS, LANES), jnp.float32),) * rings,
        in_specs=[vmem] * (rings + 1),
        out_specs=(vmem,) * rings,
        scratch_shapes=[
            pltpu.VMEM((inner_blocks + 3 * RIM, LANES), jnp.float32),
            pltpu.VMEM((members * 2 * slots // LANES, LANES), jnp.float32),
            pltpu.VMEM((2 * slots // LANES, LANES), jnp.int32),
            pltpu.SMEM((2 * slots // LANES, LANES), jnp.int32),
            pltpu.VMEM((2 * CHUNK, LANES), jnp.float32),
            pltpu.VMEM((27 * slots, LANES), jnp.float32),
            pltpu.VMEM((8 * LANES, 2 * LANES), jnp.float32),
            pltpu.VMEM((4 * 64, 2 * LANES), jnp.float32),
            pltpu.VMEM((192, 2 * LANES), jnp.float32),
            pltpu.VMEM(((tiles + 2) * 24, LANES), jnp.float32),
            pltpu.VMEM(((tiles + 2) * 48, LANES), jnp.float32),
            pltpu.SemaphoreType.DMA,
        ],
        name="pair_kernel",
    )(*pieces, offset_rows)

    column = outs[0]
    for k, out in list(zip(order, outs))[:0:-1]:
        column = column + trade(out, k)
    in_low = far == 0
    low, high = column[:own_rows], column[own_rows : 2 * own_rows]
    rim = column[2 * own_rows :]
    rim_a, rim_b = cross(rim, 1, 0), cross(rim, -1, rings)
    other = trade(jnp.where(in_low, high, low), rings)
    shares = [jnp.where(in_low, low, high), other, rim_a, rim_b]
    clump_force, clump_torque = pl.pallas_call(
        functools.partial(finish_kernel, members, groups),
        out_shape=(jax.ShapeDtypeStruct((3, clumps), jnp.float32),) * 2,
        in_specs=[vmem] * 5,
        out_specs=(vmem, vmem),
        scratch_shapes=[pltpu.VMEM((own_rows, LANES), jnp.float32)],
        name="finish_kernel",
    )(*shares, positions)
    return (clump_force, clump_torque)


def solution(mesh):
    placed = (
        P(None, ("grp", "dev")),
        P(None, ("grp", "dev")),
        P(("grp", "dev")),
        P(),
        P(None, ("grp", "dev")),
        P(("grp", "dev")),
    )
    return jax.shard_map(
        shards,
        mesh=mesh,
        in_specs=placed,
        out_specs=(P(None, ("grp", "dev")), P(None, ("grp", "dev"))),
        check_vma=False,
    )
```

```python
import functools

import jax
import jax.numpy as jnp
from jax import lax
from jax.experimental import pallas as pl
from jax.experimental.pallas import tpu as pltpu
from jax.sharding import PartitionSpec as P

RIM = 128
LANES = 128
OFFSET_UNIT = 0.125
REACH_SQUARED = 4.0
STIFFNESS = 1.0 / 256.0
CHUNK = 64
COMPS = 12
PARAMS = 10
ROWS = 24
RIM_ROWS = 16
DEPTH = 4


def split3(value):
    high = value.astype(jnp.bfloat16).astype(jnp.float32)
    rest = value - high
    middle = rest.astype(jnp.bfloat16).astype(jnp.float32)
    return high, middle, rest - middle


def clique_order(count):
    return [0, count - 1] + list(range(1, count - 1))


def payload_kernel(slots, members, *refs):
    sources, (count_ref, out_ref, end_ref), landed, sems = refs[:4], refs[4:7], refs[7:11], refs[11]
    copies = [
        pltpu.make_async_copy(source, target, sems.at[turn])
        for turn, (source, target) in enumerate(zip(sources, landed))
    ]
    for copy in copies:
        copy.start()
    for copy in copies:
        copy.wait()
    position_ref, rotation_ref, kind_ref, pair_ref = landed
    clumps = position_ref.shape[1]
    blocks = clumps // 2
    inner_blocks = blocks * members
    wide = 2 * LANES
    row = lax.broadcasted_iota(jnp.int32, (wide, wide), 0)
    column = lax.broadcasted_iota(jnp.int32, (wide, wide), 1)
    source = jnp.where(column < LANES, 2 * column, 2 * column - (wide - 1))
    picked = jnp.where(row == source, 1.0, 0.0).astype(jnp.bfloat16)
    parts = []
    for turn in range(clumps // wide):
        at = slice(turn * wide, (turn + 1) * wide)
        kinds = kind_ref[2 * turn : 2 * turn + 2, :].astype(jnp.float32)
        value = jnp.concatenate(
            [
                position_ref[:, at],
                rotation_ref[0:6, at],
                jnp.concatenate([kinds[0:1], kinds[1:2]], 1),
                jnp.zeros((16 - PARAMS, wide), jnp.float32),
            ],
            0,
        )
        parts += [piece.astype(jnp.bfloat16) for piece in split3(value)]
    sorted_parts = jnp.dot(
        jnp.concatenate(parts, 0), picked, preferred_element_type=jnp.float32
    )
    for turn in range(clumps // wide):
        high, middle, low = (sorted_parts[16 * (3 * turn + part) : 16 * (3 * turn + part) + 16] for part in range(3))
        value = (high + middle) + low
        at = slice(turn * LANES, (turn + 1) * LANES)
        out_ref[0:PARAMS, at] = value[0:PARAMS, :LANES]
        out_ref[PARAMS : 2 * PARAMS, at] = value[0:PARAMS, LANES:]
    pairs = pair_ref[...] - lax.axis_index("grp") * inner_blocks
    pairs = jnp.where(
        pairs < 0,
        pairs + inner_blocks + RIM,
        jnp.where(pairs >= inner_blocks, pairs + RIM, pairs),
    )
    live = lax.broadcasted_iota(jnp.int32, pairs.shape, 1) < count_ref[0]
    pairs = jnp.where(live, pairs, -1).astype(jnp.float32)
    lists = slots // blocks
    for which in range(2):
        for part in range(lists):
            out_ref[pl.ds(2 * PARAMS + which * lists + part, 1), :] = pairs[
                which : which + 1, part * blocks : (part + 1) * blocks
            ]
    in_low = lax.axis_index("dev") < members // 2
    end_ref[...] = jnp.where(in_low, out_ref[:, :RIM], out_ref[:, blocks - RIM :])


def finish_kernel(members, groups, own_ref, *refs):
    other_ref, rim_a_ref, rim_b_ref, position_ref, force_ref, torque_ref, total_ref = refs
    me, group = lax.axis_index("dev"), lax.axis_index("grp")
    total_ref[...] = own_ref[...] + other_ref[...]
    rim = rim_a_ref[0:COMPS] + rim_b_ref[0:COMPS]
    first = (me == 0) & (group > 0)
    final = (me == members - 1) & (group < groups - 1)
    total_ref[0:COMPS] += jnp.where(first, rim, 0.0)
    total_ref[own_ref.shape[0] - COMPS :] += jnp.where(final, rim, 0.0)
    tiles = own_ref.shape[0] // COMPS
    wide = 2 * LANES
    row = lax.broadcasted_iota(jnp.int32, (wide, wide), 0)
    column = lax.broadcasted_iota(jnp.int32, (wide, wide), 1)
    target = jnp.where(row < LANES, 2 * row, 2 * row - (wide - 1))
    placed = jnp.where(column == target, 1.0, 0.0).astype(jnp.bfloat16)
    halves = [
        jnp.concatenate(
            [total_ref[pl.ds(6 * half + comp, tiles, stride=COMPS), :] for comp in range(6)], 0
        )
        for half in range(2)
    ]
    value = jnp.concatenate(halves, 1)
    rows = value.shape[0]
    joined = jnp.dot(
        jnp.concatenate([part.astype(jnp.bfloat16) for part in split3(value)], 0),
        placed,
        preferred_element_type=jnp.float32,
    )
    value = (joined[0:rows] + joined[rows : 2 * rows]) + joined[2 * rows : 3 * rows]
    comps = [value[comp * tiles : (comp + 1) * tiles] for comp in range(6)]
    centre = [
        jnp.concatenate(
            [position_ref[axis : axis + 1, tile * wide : (tile + 1) * wide] for tile in range(tiles)], 0
        )
        for axis in range(3)
    ]
    for axis in range(3):
        after, last = (axis + 1) % 3, (axis + 2) % 3
        torque = comps[3 + axis] - (centre[after] * comps[last] - centre[last] * comps[after])
        for tile in range(tiles):
            at = slice(tile * wide, (tile + 1) * wide)
            force_ref[axis : axis + 1, at] = comps[axis][tile : tile + 1]
            torque_ref[axis : axis + 1, at] = torque[tile : tile + 1]


def pair_kernel(members, slots, *refs):
    piece_count = members // 2
    pieces = refs[:piece_count]
    off_ref = refs[piece_count]
    outs = refs[piece_count + 1 : 2 * piece_count + 1]
    (table, list_ref, word_ref, words, gathered, parts, reach_ref, sums_ref, folded_ref, acc_near,
     acc_far, sem) = refs[2 * piece_count + 1 :]
    me = lax.axis_index("dev")
    clique = lax.rem(me, piece_count)
    own_blocks = (pieces[0].shape[1] - RIM) // 2
    inner_blocks = members * own_blocks
    slot_rows = slots // LANES
    lists = slots // own_blocks

    owners = []
    counts = []
    for k in range(piece_count):
        for side in range(2):
            owners.append(jnp.bitwise_xor(me, clique_order(piece_count)[k] + side * piece_count))
            base = (2 * k + side) * 2 * slot_rows
            for part in range(2 * slot_rows):
                line, spot = part // (own_blocks // LANES), part % (own_blocks // LANES)
                at = side * own_blocks + spot * LANES
                list_ref[pl.ds(base + part, 1), :] = pieces[k][
                    pl.ds(2 * PARAMS + line, 1), at : at + LANES
                ]
            found = jnp.where(list_ref[pl.ds(base, slot_rows), :] >= 0.0, 1.0, 0.0)
            counts.append(jnp.sum(found).astype(jnp.int32))
    starts = []
    total = jnp.int32(0)
    for index in range(members):
        start = jnp.int32(0)
        for other in range(members):
            if other != index:
                start = start + jnp.where(owners[other] < owners[index], counts[other], 0)
        starts.append(start)
        total = total + counts[index]
    begin = (total * me) // members
    finish = (total * (me + 1)) // members
    number = finish - begin

    flat = lax.broadcasted_iota(jnp.int32, (slot_rows, LANES), 0) * LANES
    column = lax.broadcasted_iota(jnp.int32, (slot_rows, LANES), 1)
    flat = flat + column
    near_list = jnp.zeros((slot_rows, LANES), jnp.float32)
    far_list = jnp.zeros((slot_rows, LANES), jnp.float32)
    for index in range(members):
        start = starts[index]
        low = jnp.maximum(start, begin) - begin
        high = jnp.minimum(start + counts[index], finish) - begin
        shift = jnp.bitwise_and(start - begin, slots - 1)
        wanted = (flat >= low) & (flat < high)

        def moved(rows, shift=shift):
            turned = pltpu.roll(rows, shift & (LANES - 1), axis=1)
            same = pltpu.roll(turned, shift >> 7, axis=0)
            following = pltpu.roll(turned, (shift >> 7) + 1, axis=0)
            return jnp.where(column < (shift & (LANES - 1)), following, same)

        base = index * 2 * slot_rows
        near_list = jnp.where(wanted, moved(list_ref[pl.ds(base, slot_rows), :]), near_list)
        far_list = jnp.where(wanted, moved(list_ref[pl.ds(base + slot_rows, slot_rows), :]), far_list)
    word_ref[pl.ds(0, slot_rows), :] = near_list.astype(jnp.int32)
    word_ref[pl.ds(slot_rows, slot_rows), :] = far_list.astype(jnp.int32)
    copy = pltpu.make_async_copy(word_ref, words, sem)
    copy.start()

    for k in range(piece_count):
        for side in range(2):
            base = pl.multiple_of(owners[2 * k + side] * own_blocks, LANES)
            for tile in range(own_blocks // LANES):
                at = side * own_blocks + tile * LANES
                table[pl.ds(base + tile * LANES, LANES), 0:ROWS] = pieces[k][:, at : at + LANES].T
        place = jnp.bitwise_xor(clique, clique_order(piece_count)[k])
        base = jnp.where(place == 0, RIM, jnp.where(place == piece_count - 1, 0, 2 * RIM))
        table[pl.ds(pl.multiple_of(inner_blocks + base, RIM), RIM), 0:ROWS] = pieces[k][
            :, 2 * own_blocks :
        ].T

    def clear(turn, carry):
        acc_near[pl.ds(pl.multiple_of(turn * 48, 8), 48), :] = jnp.zeros((48, LANES), jnp.float32)
        acc_far[pl.ds(pl.multiple_of(turn * 96, 8), 96), :] = jnp.zeros((96, LANES), jnp.float32)
        return carry

    lax.fori_loop(0, acc_near.shape[0] // 48, clear, 0)

    copy.wait()

    lane = lax.broadcasted_iota(jnp.int32, (2 * CHUNK, LANES), 1)
    column_of = jnp.where(lane < LANES // 2, 0, PARAMS)
    lane_f = (lane & 7).astype(jnp.float32)
    pick_low = lane < 8
    pick_all = lane < 16
    lane24 = lax.broadcasted_iota(jnp.int32, (24, LANES), 1)
    row8 = lax.broadcasted_iota(jnp.int32, (8, LANES), 0)
    lane8 = lax.broadcasted_iota(jnp.int32, (8, LANES), 1)
    row_first = (row8 & 3) == 0
    row_second = (row8 & 3) == 1
    half8 = (row8 < 4) == (lane8 < LANES // 2)
    ones_half = jnp.where(half8, 1.0, 0.0)
    row_sum = lax.broadcasted_iota(jnp.int32, (2 * LANES, 2 * LANES), 0)
    col_sum = lax.broadcasted_iota(jnp.int32, (2 * LANES, 2 * LANES), 1)
    halves = jnp.where(
        ((row_sum & (LANES - 1)) >= LANES // 2) == (col_sum >= LANES), 1.0, 0.0
    ).astype(jnp.bfloat16)
    row16 = lax.broadcasted_iota(jnp.int32, (16, LANES), 0)
    keeps = [jnp.where((row16 & 7) == sub, 1.0, 0.0).astype(jnp.bfloat16) for sub in range(8)]

    def fetch(first):
        row = first >> 7
        base = first & (LANES - 1)
        for index in range(CHUNK):
            near = words[row, base + index]
            far = words[slot_rows + row, base + index]
            gathered[pl.ds(index, 1), :] = table[pl.ds(near, 1), :]
            gathered[pl.ds(CHUNK + index, 1), :] = table[pl.ds(far, 1), :]

    def arrange(first):
        def keep_part(slot, value):
            parts[pl.ds(pl.multiple_of(slot * slots + first, 8), CHUNK), :] = value

        packed = gathered[...]

        def spread(column):
            return jnp.take_along_axis(
                packed, column_of + column, axis=1, mode="promise_in_bounds"
            )

        kind_low = jnp.take_along_axis(
            packed, jnp.where(pick_low, 9, PARAMS + 9), axis=1, mode="promise_in_bounds"
        )
        pick = jnp.where(pick_all & (kind_low == lane_f), 1.0, 0.0).astype(jnp.bfloat16)
        offsets = jnp.dot(pick, off_ref[...], preferred_element_type=jnp.float32)
        turns = [spread(3 + entry) for entry in range(6)]
        for mode in range(3):
            after, last = (mode + 1) % 3, (mode + 2) % 3
            turns.append(turns[after] * turns[3 + last] - turns[last] * turns[3 + after])
        where_at = []
        for axis in range(3):
            value = spread(axis)
            for mode in range(3):
                value = value + turns[3 * axis + mode] * offsets[:, mode * LANES : (mode + 1) * LANES]
            where_at.append(value)
        near = [value[:CHUNK] for value in where_at]
        far = [value[CHUNK:] for value in where_at]
        near_sq = near[0] * near[0] + near[1] * near[1] + near[2] * near[2]
        far_sq = far[0] * far[0] + far[1] * far[1] + far[2] * far[2]
        for axis, value in enumerate(near + [REACH_SQUARED - near_sq]):
            for part, piece in enumerate(split3(value)):
                keep_part(4 * part + axis, piece)
        for axis, value in enumerate([2.0 * value for value in far] + [-far_sq]):
            for part, piece in enumerate(split3(value)):
                keep_part(12 + 4 * part + axis, piece)
        for axis in range(3):
            keep_part(24 + axis, far[axis])

    one8 = jnp.ones((8, LANES), jnp.float32)

    def choose(first, second, third):
        return jnp.where(row_first, first, jnp.where(row_second, second, third))

    def prepare(base):
        def part(slot):
            return parts[pl.ds(slot * slots + base, 8), :]

        near = [[part(4 * which + axis) for axis in range(4)] for which in range(3)]
        far = [[part(12 + 4 * which + axis) for axis in range(4)] for which in range(3)]
        rows_a, rows_b = [], []
        for a, b, a_last, b_last in (
            (0, 0, near[0][3], one8),
            (0, 1, one8, far[1][3]),
            (1, 0, near[1][3], one8),
            (1, 1, one8, far[0][3]),
            (0, 2, one8, far[2][3]),
            (2, 0, near[2][3], one8),
        ):
            rows_a += near[a][:3] + [a_last]
            rows_b += far[b][:3] + [b_last]
        all_a = jnp.concatenate(rows_a, 0).astype(jnp.bfloat16)
        tiles_b = [
            jnp.concatenate(rows_b[2 * tile : 2 * tile + 2], 0).astype(jnp.bfloat16)
            for tile in range(12)
        ]
        return all_a, tiles_b

    def reach_of(all_a, tiles_b, pair):
        side_b = jnp.concatenate(
            [jnp.concatenate([tile * keeps[sub] for tile in tiles_b], 0) for sub in pair], 1
        )
        return lax.dot_general(
            all_a, side_b, (((0,), (0,)), ((), ())), preferred_element_type=jnp.float32
        )

    def sums_of(reach, base, pair):
        weight = jnp.maximum(reach, 0.0)
        weight_high = weight.astype(jnp.bfloat16)
        weight_low = (weight - weight_high.astype(jnp.float32)).astype(jnp.bfloat16)
        side_c = []
        for sub in pair:
            for which in range(3):
                row = choose(
                    *[
                        parts[pl.ds((4 * which + axis) * slots + base + sub, 8, stride=0), :]
                        for axis in range(3)
                    ]
                )
                side_c.append(jnp.where(half8, row, 0.0))
            side_c.append(ones_half)
        side_c = jnp.concatenate(side_c, 0).astype(jnp.bfloat16)
        return jnp.dot(
            jnp.concatenate([side_c, side_c], 1),
            jnp.concatenate([weight_high, weight_low], 0),
            preferred_element_type=jnp.float32,
        )

    def terms_of(sums, base, pair):
        terms = []
        for place, sub in enumerate(pair):
            mine = sums[32 * place : 32 * place + 32, LANES * place : LANES * place + LANES]
            axes = [
                parts[pl.ds((24 + axis) * slots + base + sub, 8, stride=0), :] for axis in range(3)
            ]
            force = mine[24:32] * choose(*axes) - (mine[0:8] + mine[8:16] + mine[16:24])
            terms += [
                force,
                force * choose(axes[1], axes[2], axes[0]),
                force * choose(axes[2], axes[0], axes[1]),
            ]
        terms = jnp.concatenate(terms, 0)
        terms_high = terms.astype(jnp.bfloat16)
        terms_low = (terms - terms_high.astype(jnp.float32)).astype(jnp.bfloat16)
        return jnp.concatenate([terms_high, terms_low], 1)

    def scatter(group):
        base = jnp.clip(group, 0, groups - 1) * 8
        row = base >> 7
        spot = base & (LANES - 1)
        for sub in range(8):
            lower = folded_ref[pl.ds(24 * sub, 24), :LANES]
            upper = folded_ref[pl.ds(24 * sub, 24), LANES:]
            live = (group >= 0) & (group * 8 + sub < number)
            block = words[row, spot + sub]
            here = lane24 == jnp.where(live, block & (LANES - 1), -1)
            at = pl.ds(pl.multiple_of((block >> 7) * 24, 8), 24)
            acc_near[at, :] += jnp.where(here, lower + upper, 0.0)
            block = words[slot_rows + row, spot + sub]
            here = lane24 == jnp.where(live, block & (LANES - 1), -1)
            at = pl.ds(pl.multiple_of((block >> 7) * 48, 8), 48)
            acc_far[at, :] += jnp.concatenate(
                [jnp.where(here, lower, 0.0), jnp.where(here, upper, 0.0)], 0
            )

    def chunk(turn, carry):
        arrange(pl.multiple_of(turn * CHUNK, CHUNK))
        fetch(jnp.minimum((turn + 1) * CHUNK, slots - CHUNK))
        return carry

    fetch(jnp.int32(0))
    lax.fori_loop(0, (number + CHUNK - 1) // CHUNK, chunk, 0)

    groups = (number + 7) // 8
    pairs = [(2 * couple, 2 * couple + 1) for couple in range(4)]

    def octet(turn, slot):
        fresh = 4 * LANES * slot
        stale = 4 * LANES * (1 - slot)
        ready = prepare(pl.multiple_of(jnp.minimum(turn, groups - 1) * 8, 8))
        for couple, pair in enumerate(pairs):
            reach_ref[pl.ds(fresh + LANES * couple, LANES), :] = reach_of(*ready, pair)
        scatter(turn - 3)
        base = jnp.clip(turn - 2, 0, groups - 1) * 8
        terms = [
            terms_of(sums_ref[pl.ds(64 * couple, 64), :], base, pair)
            for couple, pair in enumerate(pairs)
        ]
        folded_ref[...] = jnp.dot(
            jnp.concatenate(terms, 0), halves, preferred_element_type=jnp.float32
        )
        base = jnp.clip(turn - 1, 0, groups - 1) * 8
        for couple, pair in enumerate(pairs):
            sums_ref[pl.ds(64 * couple, 64), :] = sums_of(
                reach_ref[pl.ds(stale + LANES * couple, LANES), :], base, pair
            )

    def octets(turn, carry):
        for sub in range(DEPTH):
            octet(DEPTH * turn + sub, sub % 2)
        return carry

    lax.fori_loop(0, (groups + 2 + DEPTH) // DEPTH, octets, 0)

    def total_of(row, half, tiles, start):
        line = (row // 3) * 8 + row % 3
        mine = acc_near[pl.ds(start * 24 + line + 4 * half, tiles, stride=24), :]
        line += 24 * half
        other = (
            acc_far[pl.ds(start * 48 + line, tiles, stride=48), :]
            + acc_far[pl.ds(start * 48 + line + 4, tiles, stride=48), :]
        )
        return (other - mine) * STIFFNESS

    def results_of(half, tiles, start):
        rows = [total_of(row, half, tiles, start) for row in range(9)]
        return rows[0:3] + [
            rows[6 + (axis + 2) % 3] - rows[3 + (axis + 1) % 3] for axis in range(3)
        ]

    own_tiles = own_blocks // LANES
    own_rows = own_tiles * COMPS
    edges = [results_of(half, 2, inner_blocks // LANES) for half in range(2)]
    for k, out in zip(clique_order(piece_count), outs):
        place = jnp.bitwise_xor(clique, k)
        for side in range(2):
            start = (side * piece_count + place) * own_tiles
            for half in range(2):
                for axis, value in enumerate(results_of(half, own_tiles, start)):
                    at = pl.ds(side * own_rows + 6 * half + axis, own_tiles, stride=COMPS)
                    out[at, :] = value
        out[pl.ds(2 * own_rows, RIM_ROWS), :] = jnp.zeros((RIM_ROWS, LANES), jnp.float32)
        for half in range(2):
            for axis, value in enumerate(edges[half]):
                rim = jnp.where(place == 0, value[1:2], value[0:1])
                rim = jnp.where((place == 0) | (place == piece_count - 1), rim, 0.0)
                out[pl.ds(2 * own_rows + 6 * half + axis, 1), :] = rim


def shards(positions, rotations, clump_kind, sub_offsets, pair_blocks, pair_count):
    members = lax.axis_size("dev")
    groups = lax.axis_size("grp")
    group = lax.axis_index("grp")
    me = lax.axis_index("dev")
    rings = members // 2
    clique, far = me % rings, me // rings
    clumps = positions.shape[1]
    slots = pair_blocks.shape[1]
    own_blocks = clumps // 2
    kinds, _, subs = sub_offsets.shape
    vmem = pl.BlockSpec(memory_space=pltpu.VMEM)
    smem = pl.BlockSpec(memory_space=pltpu.SMEM)

    payload, end = pl.pallas_call(
        functools.partial(payload_kernel, slots, members),
        out_shape=(
            jax.ShapeDtypeStruct((ROWS, own_blocks), jnp.float32),
            jax.ShapeDtypeStruct((ROWS, RIM), jnp.float32),
        ),
        in_specs=[pl.BlockSpec(memory_space=pltpu.HBM)] * 4 + [smem],
        out_specs=(vmem, vmem),
        scratch_shapes=[
            pltpu.VMEM((3, clumps), jnp.float32),
            pltpu.VMEM((9, clumps), jnp.float32),
            pltpu.VMEM((clumps // LANES, LANES), jnp.int32),
            pltpu.VMEM((2, slots), jnp.int32),
            pltpu.SemaphoreType.DMA((4,)),
        ],
        compiler_params=pltpu.CompilerParams(vmem_limit_bytes=4 << 20),
        name="payload_kernel",
    )(positions, rotations, clump_kind.reshape(-1, LANES), pair_blocks, pair_count)

    def trade(value, k):
        return lax.ppermute(value, "dev", [(i, i ^ k) for i in range(members)])

    def cross(value, step, flip):
        steps = [
            (
                g * members + d,
                (g + (step if d < rings else -step)) % groups * members + (d ^ flip),
            )
            for g in range(groups)
            for d in range(members)
        ]
        return lax.ppermute(value, ("grp", "dev"), steps)

    rim_a, rim_b = cross(end, -1, 0), cross(end, -1, rings)
    far_payload = trade(payload, rings)
    rim = jnp.where((clique == 0) == (far == 0), rim_a, rim_b)
    both = jnp.concatenate([payload, far_payload, rim], 1)
    order = clique_order(rings)
    pieces = [both] + [trade(both, k) for k in order[1:]]

    offset_table = sub_offsets.astype(jnp.float32) * OFFSET_UNIT
    blank = jnp.zeros_like(offset_table)
    offset_rows = jnp.concatenate(
        [
            jnp.concatenate([offset_table, blank], 2).reshape(kinds, -1),
            jnp.concatenate([blank, offset_table], 2).reshape(kinds, -1),
        ],
        0,
    )
    offset_rows = jnp.concatenate(
        [offset_rows, jnp.zeros((LANES - 2 * kinds, offset_rows.shape[1]), jnp.float32)], 0
    ).astype(jnp.bfloat16)

    inner_blocks = own_blocks * members
    tiles = inner_blocks // LANES
    own_rows = own_blocks // LANES * COMPS
    outs = pl.pallas_call(
        functools.partial(pair_kernel, members, slots),
        out_shape=(jax.ShapeDtypeStruct((2 * own_rows + RIM_ROWS, LANES), jnp.float32),) * rings,
        in_specs=[vmem] * (rings + 1),
        out_specs=(vmem,) * rings,
        scratch_shapes=[
            pltpu.VMEM((inner_blocks + 3 * RIM, LANES), jnp.float32),
            pltpu.VMEM((members * 2 * slots // LANES, LANES), jnp.float32),
            pltpu.VMEM((2 * slots // LANES, LANES), jnp.int32),
            pltpu.SMEM((2 * slots // LANES, LANES), jnp.int32),
            pltpu.VMEM((2 * CHUNK, LANES), jnp.float32),
            pltpu.VMEM((27 * slots, LANES), jnp.float32),
            pltpu.VMEM((8 * LANES, 2 * LANES), jnp.float32),
            pltpu.VMEM((4 * 64, 2 * LANES), jnp.float32),
            pltpu.VMEM((192, 2 * LANES), jnp.float32),
            pltpu.VMEM(((tiles + 2) * 24, LANES), jnp.float32),
            pltpu.VMEM(((tiles + 2) * 48, LANES), jnp.float32),
            pltpu.SemaphoreType.DMA,
        ],
        compiler_params=pltpu.CompilerParams(vmem_limit_bytes=32 << 20),
        name="pair_kernel",
    )(*pieces, offset_rows)

    column = outs[0]
    for k, out in list(zip(order, outs))[:0:-1]:
        column = column + trade(out, k)
    in_low = far == 0
    low, high = column[:own_rows], column[own_rows : 2 * own_rows]
    rim = column[2 * own_rows :]
    rim_a, rim_b = cross(rim, 1, 0), cross(rim, -1, rings)
    other = trade(jnp.where(in_low, high, low), rings)
    shares = [jnp.where(in_low, low, high), other, rim_a, rim_b]
    clump_force, clump_torque = pl.pallas_call(
        functools.partial(finish_kernel, members, groups),
        out_shape=(jax.ShapeDtypeStruct((3, clumps), jnp.float32),) * 2,
        in_specs=[vmem] * 5,
        out_specs=(vmem, vmem),
        scratch_shapes=[pltpu.VMEM((own_rows, LANES), jnp.float32)],
        compiler_params=pltpu.CompilerParams(vmem_limit_bytes=4 << 20),
        name="finish_kernel",
    )(*shares, positions)
    return (clump_force, clump_torque)


def solution(mesh):
    placed = (
        P(None, ("grp", "dev")),
        P(None, ("grp", "dev")),
        P(("grp", "dev")),
        P(),
        P(None, ("grp", "dev")),
        P(("grp", "dev")),
    )
    return jax.shard_map(
        shards,
        mesh=mesh,
        in_specs=placed,
        out_specs=(P(None, ("grp", "dev")), P(None, ("grp", "dev"))),
        check_vma=False,
    )
```

```python
import functools

import jax
import jax.numpy as jnp
from jax import lax
from jax.experimental import pallas as pl
from jax.experimental.pallas import tpu as pltpu
from jax.sharding import PartitionSpec as P

RIM = 128
LANES = 128
OFFSET_UNIT = 0.125
REACH_SQUARED = 4.0
STIFFNESS = 1.0 / 256.0
CHUNK = 64
COMPS = 12
PARAMS = 10
ROWS = 24
RIM_ROWS = 16
DEPTH = 4


def split3(value):
    high = value.astype(jnp.bfloat16).astype(jnp.float32)
    rest = value - high
    middle = rest.astype(jnp.bfloat16).astype(jnp.float32)
    return high, middle, rest - middle


def clique_order(count):
    return [0, count - 1] + list(range(1, count - 1))


def payload_kernel(slots, members, *refs):
    sources, (count_ref, out_ref, end_ref), landed, sems = refs[:4], refs[4:7], refs[7:11], refs[11]
    copies = [
        pltpu.make_async_copy(source, target, sems.at[turn])
        for turn, (source, target) in enumerate(zip(sources, landed))
    ]
    for copy in copies:
        copy.start()
    for copy in copies:
        copy.wait()
    position_ref, rotation_ref, kind_ref, pair_ref = landed
    clumps = position_ref.shape[1]
    blocks = clumps // 2
    inner_blocks = blocks * members
    wide = 2 * LANES
    row = lax.broadcasted_iota(jnp.int32, (wide, wide), 0)
    column = lax.broadcasted_iota(jnp.int32, (wide, wide), 1)
    source = jnp.where(column < LANES, 2 * column, 2 * column - (wide - 1))
    picked = jnp.where(row == source, 1.0, 0.0).astype(jnp.bfloat16)
    parts = []
    for turn in range(clumps // wide):
        at = slice(turn * wide, (turn + 1) * wide)
        kinds = kind_ref[2 * turn : 2 * turn + 2, :].astype(jnp.float32)
        value = jnp.concatenate(
            [
                position_ref[:, at],
                rotation_ref[0:6, at],
                jnp.concatenate([kinds[0:1], kinds[1:2]], 1),
                jnp.zeros((16 - PARAMS, wide), jnp.float32),
            ],
            0,
        )
        parts += [piece.astype(jnp.bfloat16) for piece in split3(value)]
    sorted_parts = jnp.dot(
        jnp.concatenate(parts, 0), picked, preferred_element_type=jnp.float32
    )
    for turn in range(clumps // wide):
        high, middle, low = (sorted_parts[16 * (3 * turn + part) : 16 * (3 * turn + part) + 16] for part in range(3))
        value = (high + middle) + low
        at = slice(turn * LANES, (turn + 1) * LANES)
        out_ref[0:PARAMS, at] = value[0:PARAMS, :LANES]
        out_ref[PARAMS : 2 * PARAMS, at] = value[0:PARAMS, LANES:]
    pairs = pair_ref[...] - lax.axis_index("grp") * inner_blocks
    pairs = jnp.where(
        pairs < 0,
        pairs + inner_blocks + RIM,
        jnp.where(pairs >= inner_blocks, pairs + RIM, pairs),
    )
    live = lax.broadcasted_iota(jnp.int32, pairs.shape, 1) < count_ref[0]
    pairs = jnp.where(live, pairs, -1).astype(jnp.float32)
    lists = slots // blocks
    for which in range(2):
        for part in range(lists):
            out_ref[pl.ds(2 * PARAMS + which * lists + part, 1), :] = pairs[
                which : which + 1, part * blocks : (part + 1) * blocks
            ]
    in_low = lax.axis_index("dev") < members // 2
    end_ref[...] = jnp.where(in_low, out_ref[:, :RIM], out_ref[:, blocks - RIM :])


def finish_kernel(members, groups, own_ref, *refs):
    other_ref, rim_a_ref, rim_b_ref, position_ref, force_ref, torque_ref, total_ref = refs
    me, group = lax.axis_index("dev"), lax.axis_index("grp")
    total_ref[...] = own_ref[...] + other_ref[...]
    rim = rim_a_ref[0:COMPS] + rim_b_ref[0:COMPS]
    first = (me == 0) & (group > 0)
    final = (me == members - 1) & (group < groups - 1)
    total_ref[0:COMPS] += jnp.where(first, rim, 0.0)
    total_ref[own_ref.shape[0] - COMPS :] += jnp.where(final, rim, 0.0)
    tiles = own_ref.shape[0] // COMPS
    wide = 2 * LANES
    row = lax.broadcasted_iota(jnp.int32, (wide, wide), 0)
    column = lax.broadcasted_iota(jnp.int32, (wide, wide), 1)
    target = jnp.where(row < LANES, 2 * row, 2 * row - (wide - 1))
    placed = jnp.where(column == target, 1.0, 0.0).astype(jnp.bfloat16)
    halves = [
        jnp.concatenate(
            [total_ref[pl.ds(6 * half + comp, tiles, stride=COMPS), :] for comp in range(6)], 0
        )
        for half in range(2)
    ]
    value = jnp.concatenate(halves, 1)
    rows = value.shape[0]
    joined = jnp.dot(
        jnp.concatenate([part.astype(jnp.bfloat16) for part in split3(value)], 0),
        placed,
        preferred_element_type=jnp.float32,
    )
    value = (joined[0:rows] + joined[rows : 2 * rows]) + joined[2 * rows : 3 * rows]
    comps = [value[comp * tiles : (comp + 1) * tiles] for comp in range(6)]
    centre = [
        jnp.concatenate(
            [position_ref[axis : axis + 1, tile * wide : (tile + 1) * wide] for tile in range(tiles)], 0
        )
        for axis in range(3)
    ]
    for axis in range(3):
        after, last = (axis + 1) % 3, (axis + 2) % 3
        torque = comps[3 + axis] - (centre[after] * comps[last] - centre[last] * comps[after])
        for tile in range(tiles):
            at = slice(tile * wide, (tile + 1) * wide)
            force_ref[axis : axis + 1, at] = comps[axis][tile : tile + 1]
            torque_ref[axis : axis + 1, at] = torque[tile : tile + 1]


def pair_kernel(members, slots, *refs):
    piece_count = members // 2
    pieces = refs[:piece_count]
    off_ref = refs[piece_count]
    outs = refs[piece_count + 1 : 2 * piece_count + 1]
    (table, list_ref, word_ref, words, gathered, parts, reach_ref, sums_ref, folded_ref, acc_near,
     acc_far, sem) = refs[2 * piece_count + 1 :]
    me = lax.axis_index("dev")
    clique = lax.rem(me, piece_count)
    own_blocks = (pieces[0].shape[1] - RIM) // 2
    inner_blocks = members * own_blocks
    slot_rows = slots // LANES
    lists = slots // own_blocks

    owners = []
    counts = []
    for k in range(piece_count):
        for side in range(2):
            owners.append(jnp.bitwise_xor(me, clique_order(piece_count)[k] + side * piece_count))
            base = (2 * k + side) * 2 * slot_rows
            for part in range(2 * slot_rows):
                line, spot = part // (own_blocks // LANES), part % (own_blocks // LANES)
                at = side * own_blocks + spot * LANES
                list_ref[pl.ds(base + part, 1), :] = pieces[k][
                    pl.ds(2 * PARAMS + line, 1), at : at + LANES
                ]
            found = jnp.where(list_ref[pl.ds(base, slot_rows), :] >= 0.0, 1.0, 0.0)
            counts.append(jnp.sum(found).astype(jnp.int32))
    starts = []
    total = jnp.int32(0)
    for index in range(members):
        start = jnp.int32(0)
        for other in range(members):
            if other != index:
                start = start + jnp.where(owners[other] < owners[index], counts[other], 0)
        starts.append(start)
        total = total + counts[index]
    begin = (total * me) // members
    finish = (total * (me + 1)) // members
    number = finish - begin

    flat = lax.broadcasted_iota(jnp.int32, (slot_rows, LANES), 0) * LANES
    column = lax.broadcasted_iota(jnp.int32, (slot_rows, LANES), 1)
    flat = flat + column
    near_list = jnp.zeros((slot_rows, LANES), jnp.float32)
    far_list = jnp.zeros((slot_rows, LANES), jnp.float32)
    for index in range(members):
        start = starts[index]
        low = jnp.maximum(start, begin) - begin
        high = jnp.minimum(start + counts[index], finish) - begin
        shift = jnp.bitwise_and(start - begin, slots - 1)
        wanted = (flat >= low) & (flat < high)

        def moved(rows, shift=shift):
            turned = pltpu.roll(rows, shift & (LANES - 1), axis=1)
            same = pltpu.roll(turned, shift >> 7, axis=0)
            following = pltpu.roll(turned, (shift >> 7) + 1, axis=0)
            return jnp.where(column < (shift & (LANES - 1)), following, same)

        base = index * 2 * slot_rows
        near_list = jnp.where(wanted, moved(list_ref[pl.ds(base, slot_rows), :]), near_list)
        far_list = jnp.where(wanted, moved(list_ref[pl.ds(base + slot_rows, slot_rows), :]), far_list)
    word_ref[pl.ds(0, slot_rows), :] = near_list.astype(jnp.int32)
    word_ref[pl.ds(slot_rows, slot_rows), :] = far_list.astype(jnp.int32)
    copy = pltpu.make_async_copy(word_ref, words, sem)
    copy.start()

    for k in range(piece_count):
        for side in range(2):
            base = pl.multiple_of(owners[2 * k + side] * own_blocks, LANES)
            for tile in range(own_blocks // LANES):
                at = side * own_blocks + tile * LANES
                table[pl.ds(base + tile * LANES, LANES), 0:ROWS] = pieces[k][:, at : at + LANES].T
        place = jnp.bitwise_xor(clique, clique_order(piece_count)[k])
        base = jnp.where(place == 0, RIM, jnp.where(place == piece_count - 1, 0, 2 * RIM))
        table[pl.ds(pl.multiple_of(inner_blocks + base, RIM), RIM), 0:ROWS] = pieces[k][
            :, 2 * own_blocks :
        ].T

    def clear(turn, carry):
        acc_near[pl.ds(pl.multiple_of(turn * 48, 8), 48), :] = jnp.zeros((48, LANES), jnp.float32)
        acc_far[pl.ds(pl.multiple_of(turn * 96, 8), 96), :] = jnp.zeros((96, LANES), jnp.float32)
        return carry

    lax.fori_loop(0, acc_near.shape[0] // 48, clear, 0)

    copy.wait()

    lane = lax.broadcasted_iota(jnp.int32, (2 * CHUNK, LANES), 1)
    column_of = jnp.where(lane < LANES // 2, 0, PARAMS)
    lane_f = (lane & 7).astype(jnp.float32)
    pick_low = lane < 8
    pick_all = lane < 16
    lane24 = lax.broadcasted_iota(jnp.int32, (24, LANES), 1)
    row8 = lax.broadcasted_iota(jnp.int32, (8, LANES), 0)
    lane8 = lax.broadcasted_iota(jnp.int32, (8, LANES), 1)
    row_first = (row8 & 3) == 0
    row_second = (row8 & 3) == 1
    half8 = (row8 < 4) == (lane8 < LANES // 2)
    ones_half = jnp.where(half8, 1.0, 0.0)
    row_sum = lax.broadcasted_iota(jnp.int32, (2 * LANES, 2 * LANES), 0)
    col_sum = lax.broadcasted_iota(jnp.int32, (2 * LANES, 2 * LANES), 1)
    halves = jnp.where(
        ((row_sum & (LANES - 1)) >= LANES // 2) == (col_sum >= LANES), 1.0, 0.0
    ).astype(jnp.bfloat16)
    row16 = lax.broadcasted_iota(jnp.int32, (16, LANES), 0)
    keeps = [jnp.where((row16 & 7) == sub, 1.0, 0.0).astype(jnp.bfloat16) for sub in range(8)]

    def fetch(first):
        row = first >> 7
        base = first & (LANES - 1)
        for index in range(CHUNK):
            near = words[row, base + index]
            far = words[slot_rows + row, base + index]
            gathered[pl.ds(index, 1), :] = table[pl.ds(near, 1), :]
            gathered[pl.ds(CHUNK + index, 1), :] = table[pl.ds(far, 1), :]

    def arrange(first):
        def keep_part(slot, value):
            parts[pl.ds(pl.multiple_of(slot * slots + first, 8), CHUNK), :] = value

        packed = gathered[...]

        def spread(column):
            return jnp.take_along_axis(
                packed, column_of + column, axis=1, mode="promise_in_bounds"
            )

        kind_low = jnp.take_along_axis(
            packed, jnp.where(pick_low, 9, PARAMS + 9), axis=1, mode="promise_in_bounds"
        )
        pick = jnp.where(pick_all & (kind_low == lane_f), 1.0, 0.0).astype(jnp.bfloat16)
        offsets = jnp.dot(pick, off_ref[...], preferred_element_type=jnp.float32)
        turns = [spread(3 + entry) for entry in range(6)]
        for mode in range(3):
            after, last = (mode + 1) % 3, (mode + 2) % 3
            turns.append(turns[after] * turns[3 + last] - turns[last] * turns[3 + after])
        where_at = []
        for axis in range(3):
            value = spread(axis)
            for mode in range(3):
                value = value + turns[3 * axis + mode] * offsets[:, mode * LANES : (mode + 1) * LANES]
            where_at.append(value)
        near = [value[:CHUNK] for value in where_at]
        far = [value[CHUNK:] for value in where_at]
        near_sq = near[0] * near[0] + near[1] * near[1] + near[2] * near[2]
        far_sq = far[0] * far[0] + far[1] * far[1] + far[2] * far[2]
        for axis, value in enumerate(near + [REACH_SQUARED - near_sq]):
            for part, piece in enumerate(split3(value)):
                keep_part(4 * part + axis, piece)
        for axis, value in enumerate([2.0 * value for value in far] + [-far_sq]):
            for part, piece in enumerate(split3(value)):
                keep_part(12 + 4 * part + axis, piece)
        for axis in range(3):
            keep_part(24 + axis, far[axis])

    one8 = jnp.ones((8, LANES), jnp.float32)

    def choose(first, second, third):
        return jnp.where(row_first, first, jnp.where(row_second, second, third))

    def prepare(base):
        def part(slot):
            return parts[pl.ds(slot * slots + base, 8), :]

        near = [[part(4 * which + axis) for axis in range(4)] for which in range(3)]
        far = [[part(12 + 4 * which + axis) for axis in range(4)] for which in range(3)]
        rows_a, rows_b = [], []
        for a, b, a_last, b_last in (
            (0, 0, near[0][3], one8),
            (0, 1, one8, far[1][3]),
            (1, 0, near[1][3], one8),
            (1, 1, one8, far[0][3]),
            (0, 2, one8, far[2][3]),
            (2, 0, near[2][3], one8),
        ):
            rows_a += near[a][:3] + [a_last]
            rows_b += far[b][:3] + [b_last]
        all_a = jnp.concatenate(rows_a, 0).astype(jnp.bfloat16)
        tiles_b = [
            jnp.concatenate(rows_b[2 * tile : 2 * tile + 2], 0).astype(jnp.bfloat16)
            for tile in range(12)
        ]
        return all_a, tiles_b

    def reach_of(all_a, tiles_b, pair):
        side_b = jnp.concatenate(
            [jnp.concatenate([tile * keeps[sub] for tile in tiles_b], 0) for sub in pair], 1
        )
        return lax.dot_general(
            all_a, side_b, (((0,), (0,)), ((), ())), preferred_element_type=jnp.float32
        )

    def sums_of(reach, base, pair):
        weight = jnp.maximum(reach, 0.0)
        weight_high = weight.astype(jnp.bfloat16)
        weight_low = (weight - weight_high.astype(jnp.float32)).astype(jnp.bfloat16)
        side_c = []
        for sub in pair:
            for which in range(3):
                row = choose(
                    *[
                        parts[pl.ds((4 * which + axis) * slots + base + sub, 8, stride=0), :]
                        for axis in range(3)
                    ]
                )
                side_c.append(jnp.where(half8, row, 0.0))
            side_c.append(ones_half)
        side_c = jnp.concatenate(side_c, 0).astype(jnp.bfloat16)
        return jnp.dot(
            jnp.concatenate([side_c, side_c], 1),
            jnp.concatenate([weight_high, weight_low], 0),
            preferred_element_type=jnp.float32,
        )

    def terms_of(sums, base, pair):
        terms = []
        for place, sub in enumerate(pair):
            mine = sums[32 * place : 32 * place + 32, LANES * place : LANES * place + LANES]
            axes = [
                parts[pl.ds((24 + axis) * slots + base + sub, 8, stride=0), :] for axis in range(3)
            ]
            force = mine[24:32] * choose(*axes) - (mine[0:8] + mine[8:16] + mine[16:24])
            terms += [
                force,
                force * choose(axes[1], axes[2], axes[0]),
                force * choose(axes[2], axes[0], axes[1]),
            ]
        terms = jnp.concatenate(terms, 0)
        terms_high = terms.astype(jnp.bfloat16)
        terms_low = (terms - terms_high.astype(jnp.float32)).astype(jnp.bfloat16)
        return jnp.concatenate([terms_high, terms_low], 1)

    def scatter(group):
        base = jnp.clip(group, 0, groups - 1) * 8
        row = base >> 7
        spot = base & (LANES - 1)
        for sub in range(8):
            lower = folded_ref[pl.ds(24 * sub, 24), :LANES]
            upper = folded_ref[pl.ds(24 * sub, 24), LANES:]
            live = (group >= 0) & (group * 8 + sub < number)
            block = words[row, spot + sub]
            here = lane24 == jnp.where(live, block & (LANES - 1), -1)
            at = pl.ds(pl.multiple_of((block >> 7) * 24, 8), 24)
            acc_near[at, :] += jnp.where(here, lower + upper, 0.0)
            block = words[slot_rows + row, spot + sub]
            here = lane24 == jnp.where(live, block & (LANES - 1), -1)
            at = pl.ds(pl.multiple_of((block >> 7) * 48, 8), 48)
            acc_far[at, :] += jnp.concatenate(
                [jnp.where(here, lower, 0.0), jnp.where(here, upper, 0.0)], 0
            )

    def chunk(turn, carry):
        arrange(pl.multiple_of(turn * CHUNK, CHUNK))
        fetch(jnp.minimum((turn + 1) * CHUNK, slots - CHUNK))
        return carry

    fetch(jnp.int32(0))
    lax.fori_loop(0, (number + CHUNK - 1) // CHUNK, chunk, 0)

    groups = (number + 7) // 8
    pairs = [(2 * couple, 2 * couple + 1) for couple in range(4)]

    def octet(turn, slot):
        fresh = 4 * LANES * slot
        stale = 4 * LANES * (1 - slot)
        ready = prepare(pl.multiple_of(jnp.minimum(turn, groups - 1) * 8, 8))
        for couple, pair in enumerate(pairs):
            reach_ref[pl.ds(fresh + LANES * couple, LANES), :] = reach_of(*ready, pair)
        scatter(turn - 3)
        base = jnp.clip(turn - 2, 0, groups - 1) * 8
        terms = [
            terms_of(sums_ref[pl.ds(64 * couple, 64), :], base, pair)
            for couple, pair in enumerate(pairs)
        ]
        folded_ref[...] = jnp.dot(
            jnp.concatenate(terms, 0), halves, preferred_element_type=jnp.float32
        )
        base = jnp.clip(turn - 1, 0, groups - 1) * 8
        for couple, pair in enumerate(pairs):
            sums_ref[pl.ds(64 * couple, 64), :] = sums_of(
                reach_ref[pl.ds(stale + LANES * couple, LANES), :], base, pair
            )

    def octets(turn, carry):
        for sub in range(DEPTH):
            octet(DEPTH * turn + sub, sub % 2)
        return carry

    lax.fori_loop(0, (groups + 2 + DEPTH) // DEPTH, octets, 0)

    def total_of(row, half, tiles, start):
        line = (row // 3) * 8 + row % 3
        mine = acc_near[pl.ds(start * 24 + line + 4 * half, tiles, stride=24), :]
        line += 24 * half
        other = (
            acc_far[pl.ds(start * 48 + line, tiles, stride=48), :]
            + acc_far[pl.ds(start * 48 + line + 4, tiles, stride=48), :]
        )
        return (other - mine) * STIFFNESS

    def results_of(half, tiles, start):
        rows = [total_of(row, half, tiles, start) for row in range(9)]
        return rows[0:3] + [
            rows[6 + (axis + 2) % 3] - rows[3 + (axis + 1) % 3] for axis in range(3)
        ]

    own_tiles = own_blocks // LANES
    own_rows = own_tiles * COMPS
    edges = [results_of(half, 2, inner_blocks // LANES) for half in range(2)]
    for k, out in zip(clique_order(piece_count), outs):
        place = jnp.bitwise_xor(clique, k)
        for side in range(2):
            start = (side * piece_count + place) * own_tiles
            for half in range(2):
                for axis, value in enumerate(results_of(half, own_tiles, start)):
                    at = pl.ds(side * own_rows + 6 * half + axis, own_tiles, stride=COMPS)
                    out[at, :] = value
        out[pl.ds(2 * own_rows, RIM_ROWS), :] = jnp.zeros((RIM_ROWS, LANES), jnp.float32)
        for half in range(2):
            for axis, value in enumerate(edges[half]):
                rim = jnp.where(place == 0, value[1:2], value[0:1])
                rim = jnp.where((place == 0) | (place == piece_count - 1), rim, 0.0)
                out[pl.ds(2 * own_rows + 6 * half + axis, 1), :] = rim


def shards(positions, rotations, clump_kind, sub_offsets, pair_blocks, pair_count):
    members = lax.axis_size("dev")
    groups = lax.axis_size("grp")
    group = lax.axis_index("grp")
    me = lax.axis_index("dev")
    rings = members // 2
    clique, far = me % rings, me // rings
    clumps = positions.shape[1]
    slots = pair_blocks.shape[1]
    own_blocks = clumps // 2
    kinds, _, subs = sub_offsets.shape
    vmem = pl.BlockSpec(memory_space=pltpu.VMEM)
    smem = pl.BlockSpec(memory_space=pltpu.SMEM)

    payload, end = pl.pallas_call(
        functools.partial(payload_kernel, slots, members),
        out_shape=(
            jax.ShapeDtypeStruct((ROWS, own_blocks), jnp.float32),
            jax.ShapeDtypeStruct((ROWS, RIM), jnp.float32),
        ),
        in_specs=[pl.BlockSpec(memory_space=pltpu.HBM)] * 4 + [smem],
        out_specs=(vmem, vmem),
        scratch_shapes=[
            pltpu.VMEM((3, clumps), jnp.float32),
            pltpu.VMEM((9, clumps), jnp.float32),
            pltpu.VMEM((clumps // LANES, LANES), jnp.int32),
            pltpu.VMEM((2, slots), jnp.int32),
            pltpu.SemaphoreType.DMA((4,)),
        ],
        name="payload_kernel",
    )(positions, rotations, clump_kind.reshape(-1, LANES), pair_blocks, pair_count)

    def trade(value, k):
        return lax.ppermute(value, "dev", [(i, i ^ k) for i in range(members)])

    def cross(value, step, flip):
        steps = [
            (
                g * members + d,
                (g + (step if d < rings else -step)) % groups * members + (d ^ flip),
            )
            for g in range(groups)
            for d in range(members)
        ]
        return lax.ppermute(value, ("grp", "dev"), steps)

    rim_a, rim_b = cross(end, -1, 0), cross(end, -1, rings)
    far_payload = trade(payload, rings)
    rim = jnp.where((clique == 0) == (far == 0), rim_a, rim_b)
    both = jnp.concatenate([payload, far_payload, rim], 1)
    order = clique_order(rings)
    pieces = [both] + [trade(both, k) for k in order[1:]]

    offset_table = sub_offsets.astype(jnp.float32) * OFFSET_UNIT
    blank = jnp.zeros_like(offset_table)
    offset_rows = jnp.concatenate(
        [
            jnp.concatenate([offset_table, blank], 2).reshape(kinds, -1),
            jnp.concatenate([blank, offset_table], 2).reshape(kinds, -1),
        ],
        0,
    )
    offset_rows = jnp.concatenate(
        [offset_rows, jnp.zeros((LANES - 2 * kinds, offset_rows.shape[1]), jnp.float32)], 0
    ).astype(jnp.bfloat16)

    inner_blocks = own_blocks * members
    tiles = inner_blocks // LANES
    own_rows = own_blocks // LANES * COMPS
    outs = pl.pallas_call(
        functools.partial(pair_kernel, members, slots),
        out_shape=(jax.ShapeDtypeStruct((2 * own_rows + RIM_ROWS, LANES), jnp.float32),) * rings,
        in_specs=[vmem] * (rings + 1),
        out_specs=(vmem,) * rings,
        scratch_shapes=[
            pltpu.VMEM((inner_blocks + 3 * RIM, LANES), jnp.float32),
            pltpu.VMEM((members * 2 * slots // LANES, LANES), jnp.float32),
            pltpu.VMEM((2 * slots // LANES, LANES), jnp.int32),
            pltpu.SMEM((2 * slots // LANES, LANES), jnp.int32),
            pltpu.VMEM((2 * CHUNK, LANES), jnp.float32),
            pltpu.VMEM((27 * slots, LANES), jnp.float32),
            pltpu.VMEM((8 * LANES, 2 * LANES), jnp.float32),
            pltpu.VMEM((4 * 64, 2 * LANES), jnp.float32),
            pltpu.VMEM((192, 2 * LANES), jnp.float32),
            pltpu.VMEM(((tiles + 2) * 24, LANES), jnp.float32),
            pltpu.VMEM(((tiles + 2) * 48, LANES), jnp.float32),
            pltpu.SemaphoreType.DMA,
        ],
        compiler_params=pltpu.CompilerParams(vmem_limit_bytes=32 << 20),
        name="pair_kernel",
    )(*pieces, offset_rows)

    column = outs[0]
    for k, out in list(zip(order, outs))[:0:-1]:
        column = column + trade(out, k)
    in_low = far == 0
    low, high = column[:own_rows], column[own_rows : 2 * own_rows]
    rim = column[2 * own_rows :]
    rim_a, rim_b = cross(rim, 1, 0), cross(rim, -1, rings)
    other = trade(jnp.where(in_low, high, low), rings)
    shares = [jnp.where(in_low, low, high), other, rim_a, rim_b]
    clump_force, clump_torque = pl.pallas_call(
        functools.partial(finish_kernel, members, groups),
        out_shape=(jax.ShapeDtypeStruct((3, clumps), jnp.float32),) * 2,
        in_specs=[vmem] * 5,
        out_specs=(vmem, vmem),
        scratch_shapes=[pltpu.VMEM((own_rows, LANES), jnp.float32)],
        compiler_params=pltpu.CompilerParams(vmem_limit_bytes=4 << 20),
        name="finish_kernel",
    )(*shares, positions)
    return (clump_force, clump_torque)


def solution(mesh):
    placed = (
        P(None, ("grp", "dev")),
        P(None, ("grp", "dev")),
        P(("grp", "dev")),
        P(),
        P(None, ("grp", "dev")),
        P(("grp", "dev")),
    )
    return jax.shard_map(
        shards,
        mesh=mesh,
        in_specs=placed,
        out_specs=(P(None, ("grp", "dev")), P(None, ("grp", "dev"))),
        check_vma=False,
    )
```

```python
import functools

import jax
import jax.numpy as jnp
from jax import lax
from jax.experimental import pallas as pl
from jax.experimental.pallas import tpu as pltpu
from jax.sharding import PartitionSpec as P


RIM = 128
LANES = 128
OFFSET_UNIT = 0.125
REACH_SQUARED = 4.0
STIFFNESS = 1.0 / 256.0
CHUNK = 64
COMPS = 12
PARAMS = 10
ROWS = 24
RIM_ROWS = 16
DEPTH = 4


def split3(value):
    high = value.astype(jnp.bfloat16).astype(jnp.float32)
    rest = value - high
    middle = rest.astype(jnp.bfloat16).astype(jnp.float32)
    return high, middle, rest - middle


def clique_order(count):
    return [0, count - 1] + list(range(1, count - 1))


def payload_kernel(slots, members, *refs):
    sources, (count_ref, out_ref, end_ref), landed, sems = refs[:4], refs[4:7], refs[7:11], refs[11]
    copies = [
        pltpu.make_async_copy(source, target, sems.at[turn])
        for turn, (source, target) in enumerate(zip(sources, landed))
    ]
    for copy in copies:
        copy.start()
    for copy in copies:
        copy.wait()
    position_ref, rotation_ref, kind_ref, pair_ref = landed
    clumps = position_ref.shape[1]
    blocks = clumps // 2
    inner_blocks = blocks * members
    wide = 2 * LANES
    row = lax.broadcasted_iota(jnp.int32, (wide, wide), 0)
    column = lax.broadcasted_iota(jnp.int32, (wide, wide), 1)
    source = jnp.where(column < LANES, 2 * column, 2 * column - (wide - 1))
    picked = jnp.where(row == source, 1.0, 0.0).astype(jnp.bfloat16)
    parts = []
    for turn in range(clumps // wide):
        at = slice(turn * wide, (turn + 1) * wide)
        kinds = kind_ref[2 * turn : 2 * turn + 2, :].astype(jnp.float32)
        value = jnp.concatenate(
            [
                position_ref[:, at],
                rotation_ref[0:6, at],
                jnp.concatenate([kinds[0:1], kinds[1:2]], 1),
                jnp.zeros((16 - PARAMS, wide), jnp.float32),
            ],
            0,
        )
        parts += [piece.astype(jnp.bfloat16) for piece in split3(value)]
    sorted_parts = jnp.dot(
        jnp.concatenate(parts, 0), picked, preferred_element_type=jnp.float32
    )
    for turn in range(clumps // wide):
        high, middle, low = (sorted_parts[16 * (3 * turn + part) : 16 * (3 * turn + part) + 16] for part in range(3))
        value = (high + middle) + low
        at = slice(turn * LANES, (turn + 1) * LANES)
        out_ref[0:PARAMS, at] = value[0:PARAMS, :LANES]
        out_ref[PARAMS : 2 * PARAMS, at] = value[0:PARAMS, LANES:]
    pairs = pair_ref[...] - lax.axis_index("grp") * inner_blocks
    pairs = jnp.where(
        pairs < 0,
        pairs + inner_blocks + RIM,
        jnp.where(pairs >= inner_blocks, pairs + RIM, pairs),
    )
    live = lax.broadcasted_iota(jnp.int32, pairs.shape, 1) < count_ref[0]
    pairs = jnp.where(live, pairs, -1).astype(jnp.float32)
    lists = slots // blocks
    for which in range(2):
        for part in range(lists):
            out_ref[pl.ds(2 * PARAMS + which * lists + part, 1), :] = pairs[
                which : which + 1, part * blocks : (part + 1) * blocks
            ]
    in_low = lax.axis_index("dev") < members // 2
    end_ref[...] = jnp.where(in_low, out_ref[:, :RIM], out_ref[:, blocks - RIM :])


def finish_kernel(members, groups, own_ref, *refs):
    other_ref, rim_a_ref, rim_b_ref, position_ref, force_ref, torque_ref, total_ref = refs
    me, group = lax.axis_index("dev"), lax.axis_index("grp")
    total_ref[...] = own_ref[...] + other_ref[...]
    rim = rim_a_ref[0:COMPS] + rim_b_ref[0:COMPS]
    first = (me == 0) & (group > 0)
    final = (me == members - 1) & (group < groups - 1)
    total_ref[0:COMPS] += jnp.where(first, rim, 0.0)
    total_ref[own_ref.shape[0] - COMPS :] += jnp.where(final, rim, 0.0)
    tiles = own_ref.shape[0] // COMPS
    wide = 2 * LANES
    row = lax.broadcasted_iota(jnp.int32, (wide, wide), 0)
    column = lax.broadcasted_iota(jnp.int32, (wide, wide), 1)
    target = jnp.where(row < LANES, 2 * row, 2 * row - (wide - 1))
    placed = jnp.where(column == target, 1.0, 0.0).astype(jnp.bfloat16)
    halves = [
        jnp.concatenate(
            [total_ref[pl.ds(6 * half + comp, tiles, stride=COMPS), :] for comp in range(6)], 0
        )
        for half in range(2)
    ]
    value = jnp.concatenate(halves, 1)
    rows = value.shape[0]
    joined = jnp.dot(
        jnp.concatenate([part.astype(jnp.bfloat16) for part in split3(value)], 0),
        placed,
        preferred_element_type=jnp.float32,
    )
    value = (joined[0:rows] + joined[rows : 2 * rows]) + joined[2 * rows : 3 * rows]
    comps = [value[comp * tiles : (comp + 1) * tiles] for comp in range(6)]
    centre = [
        jnp.concatenate(
            [position_ref[axis : axis + 1, tile * wide : (tile + 1) * wide] for tile in range(tiles)], 0
        )
        for axis in range(3)
    ]
    for axis in range(3):
        after, last = (axis + 1) % 3, (axis + 2) % 3
        torque = comps[3 + axis] - (centre[after] * comps[last] - centre[last] * comps[after])
        for tile in range(tiles):
            at = slice(tile * wide, (tile + 1) * wide)
            force_ref[axis : axis + 1, at] = comps[axis][tile : tile + 1]
            torque_ref[axis : axis + 1, at] = torque[tile : tile + 1]


def pair_kernel(members, slots, *refs):
    piece_count = members // 2
    pieces = refs[:piece_count]
    off_ref = refs[piece_count]
    outs = refs[piece_count + 1 : 2 * piece_count + 1]
    (table, list_ref, word_ref, words, gathered, parts, reach_ref, sums_ref, folded_ref, acc_near,
     acc_far, sem) = refs[2 * piece_count + 1 :]
    me = lax.axis_index("dev")
    clique = lax.rem(me, piece_count)
    own_blocks = (pieces[0].shape[1] - RIM) // 2
    inner_blocks = members * own_blocks
    slot_rows = slots // LANES

    owners = []
    counts = []
    for k in range(piece_count):
        for side in range(2):
            owners.append(jnp.bitwise_xor(me, clique_order(piece_count)[k] + side * piece_count))
            base = (2 * k + side) * 2 * slot_rows
            for part in range(2 * slot_rows):
                line, spot = part // (own_blocks // LANES), part % (own_blocks // LANES)
                at = side * own_blocks + spot * LANES
                list_ref[pl.ds(base + part, 1), :] = pieces[k][
                    pl.ds(2 * PARAMS + line, 1), at : at + LANES
                ]
            found = jnp.where(list_ref[pl.ds(base, slot_rows), :] >= 0.0, 1.0, 0.0)
            counts.append(jnp.sum(found).astype(jnp.int32))
    starts = []
    total = jnp.int32(0)
    for index in range(members):
        start = jnp.int32(0)
        for other in range(members):
            if other != index:
                start = start + jnp.where(owners[other] < owners[index], counts[other], 0)
        starts.append(start)
        total = total + counts[index]
    begin = (total * me) // members
    finish = (total * (me + 1)) // members
    number = finish - begin

    flat = lax.broadcasted_iota(jnp.int32, (slot_rows, LANES), 0) * LANES
    column = lax.broadcasted_iota(jnp.int32, (slot_rows, LANES), 1)
    flat = flat + column
    near_list = jnp.zeros((slot_rows, LANES), jnp.float32)
    far_list = jnp.zeros((slot_rows, LANES), jnp.float32)
    for index in range(members):
        start = starts[index]
        low = jnp.maximum(start, begin) - begin
        high = jnp.minimum(start + counts[index], finish) - begin
        shift = jnp.bitwise_and(start - begin, slots - 1)
        wanted = (flat >= low) & (flat < high)

        def moved(rows, shift=shift):
            turned = pltpu.roll(rows, shift & (LANES - 1), axis=1)
            same = pltpu.roll(turned, shift >> 7, axis=0)
            following = pltpu.roll(turned, (shift >> 7) + 1, axis=0)
            return jnp.where(column < (shift & (LANES - 1)), following, same)

        base = index * 2 * slot_rows
        near_list = jnp.where(wanted, moved(list_ref[pl.ds(base, slot_rows), :]), near_list)
        far_list = jnp.where(wanted, moved(list_ref[pl.ds(base + slot_rows, slot_rows), :]), far_list)
    word_ref[pl.ds(0, slot_rows), :] = near_list.astype(jnp.int32)
    word_ref[pl.ds(slot_rows, slot_rows), :] = far_list.astype(jnp.int32)
    copy = pltpu.make_async_copy(word_ref, words, sem)
    copy.start()

    for k in range(piece_count):
        for side in range(2):
            base = pl.multiple_of(owners[2 * k + side] * own_blocks, LANES)
            for tile in range(own_blocks // LANES):
                at = side * own_blocks + tile * LANES
                table[pl.ds(base + tile * LANES, LANES), 0:ROWS] = pieces[k][:, at : at + LANES].T
        place = jnp.bitwise_xor(clique, clique_order(piece_count)[k])
        base = jnp.where(place == 0, RIM, jnp.where(place == piece_count - 1, 0, 2 * RIM))
        table[pl.ds(pl.multiple_of(inner_blocks + base, RIM), RIM), 0:ROWS] = pieces[k][
            :, 2 * own_blocks :
        ].T

    def clear(turn, carry):
        acc_near[pl.ds(pl.multiple_of(turn * 48, 8), 48), :] = jnp.zeros((48, LANES), jnp.float32)
        acc_far[pl.ds(pl.multiple_of(turn * 96, 8), 96), :] = jnp.zeros((96, LANES), jnp.float32)
        return carry

    lax.fori_loop(0, acc_near.shape[0] // 48, clear, 0)

    copy.wait()

    lane = lax.broadcasted_iota(jnp.int32, (2 * CHUNK, LANES), 1)
    column_of = jnp.where(lane < LANES // 2, 0, PARAMS)
    lane_f = (lane & 7).astype(jnp.float32)
    pick_low = lane < 8
    pick_all = lane < 16
    lane24 = lax.broadcasted_iota(jnp.int32, (24, LANES), 1)
    row8 = lax.broadcasted_iota(jnp.int32, (8, LANES), 0)
    lane8 = lax.broadcasted_iota(jnp.int32, (8, LANES), 1)
    row_first = (row8 & 3) == 0
    row_second = (row8 & 3) == 1
    half8 = (row8 < 4) == (lane8 < LANES // 2)
    ones_half = jnp.where(half8, 1.0, 0.0)
    row_sum = lax.broadcasted_iota(jnp.int32, (2 * LANES, 2 * LANES), 0)
    col_sum = lax.broadcasted_iota(jnp.int32, (2 * LANES, 2 * LANES), 1)
    halves = jnp.where(
        ((row_sum & (LANES - 1)) >= LANES // 2) == (col_sum >= LANES), 1.0, 0.0
    ).astype(jnp.bfloat16)
    row16 = lax.broadcasted_iota(jnp.int32, (16, LANES), 0)
    keeps = [jnp.where((row16 & 7) == sub, 1.0, 0.0).astype(jnp.bfloat16) for sub in range(8)]

    def fetch(first):
        row = first >> 7
        base = first & (LANES - 1)
        for index in range(CHUNK):
            near = words[row, base + index]
            far = words[slot_rows + row, base + index]
            gathered[pl.ds(index, 1), :] = table[pl.ds(near, 1), :]
            gathered[pl.ds(CHUNK + index, 1), :] = table[pl.ds(far, 1), :]

    def arrange(first):
        def keep_part(slot, value):
            parts[pl.ds(pl.multiple_of(slot * slots + first, 8), CHUNK), :] = value

        packed = gathered[...]

        def spread(column):
            return jnp.take_along_axis(
                packed, column_of + column, axis=1, mode="promise_in_bounds"
            )

        kind_low = jnp.take_along_axis(
            packed, jnp.where(pick_low, 9, PARAMS + 9), axis=1, mode="promise_in_bounds"
        )
        pick = jnp.where(pick_all & (kind_low == lane_f), 1.0, 0.0).astype(jnp.bfloat16)
        offsets = jnp.dot(pick, off_ref[...], preferred_element_type=jnp.float32)
        turns = [spread(3 + entry) for entry in range(6)]
        for mode in range(3):
            after, last = (mode + 1) % 3, (mode + 2) % 3
            turns.append(turns[after] * turns[3 + last] - turns[last] * turns[3 + after])
        where_at = []
        for axis in range(3):
            value = spread(axis)
            for mode in range(3):
                value = value + turns[3 * axis + mode] * offsets[:, mode * LANES : (mode + 1) * LANES]
            where_at.append(value)
        near = [value[:CHUNK] for value in where_at]
        far = [value[CHUNK:] for value in where_at]
        near_sq = near[0] * near[0] + near[1] * near[1] + near[2] * near[2]
        far_sq = far[0] * far[0] + far[1] * far[1] + far[2] * far[2]
        for axis, value in enumerate(near + [REACH_SQUARED - near_sq]):
            for part, piece in enumerate(split3(value)):
                keep_part(4 * part + axis, piece)
        for axis, value in enumerate([2.0 * value for value in far] + [-far_sq]):
            for part, piece in enumerate(split3(value)):
                keep_part(12 + 4 * part + axis, piece)
        for axis in range(3):
            keep_part(24 + axis, far[axis])

    one8 = jnp.ones((8, LANES), jnp.float32)

    def choose(first, second, third):
        return jnp.where(row_first, first, jnp.where(row_second, second, third))

    def prepare(base):
        def part(slot):
            return parts[pl.ds(slot * slots + base, 8), :]

        near = [[part(4 * which + axis) for axis in range(4)] for which in range(3)]
        far = [[part(12 + 4 * which + axis) for axis in range(4)] for which in range(3)]
        rows_a, rows_b = [], []
        for a, b, a_last, b_last in (
            (0, 0, near[0][3], one8),
            (0, 1, one8, far[1][3]),
            (1, 0, near[1][3], one8),
            (1, 1, one8, far[0][3]),
            (0, 2, one8, far[2][3]),
            (2, 0, near[2][3], one8),
        ):
            rows_a += near[a][:3] + [a_last]
            rows_b += far[b][:3] + [b_last]
        all_a = jnp.concatenate(rows_a, 0).astype(jnp.bfloat16)
        tiles_b = [
            jnp.concatenate(rows_b[2 * tile : 2 * tile + 2], 0).astype(jnp.bfloat16)
            for tile in range(12)
        ]
        return all_a, tiles_b

    def reach_of(all_a, tiles_b, pair):
        side_b = jnp.concatenate(
            [jnp.concatenate([tile * keeps[sub] for tile in tiles_b], 0) for sub in pair], 1
        )
        return lax.dot_general(
            all_a, side_b, (((0,), (0,)), ((), ())), preferred_element_type=jnp.float32
        )

    def sums_of(reach, base, pair):
        weight = jnp.maximum(reach, 0.0)
        weight_high = weight.astype(jnp.bfloat16)
        weight_low = (weight - weight_high.astype(jnp.float32)).astype(jnp.bfloat16)
        side_c = []
        for sub in pair:
            for which in range(3):
                row = choose(
                    *[
                        parts[pl.ds((4 * which + axis) * slots + base + sub, 8, stride=0), :]
                        for axis in range(3)
                    ]
                )
                side_c.append(jnp.where(half8, row, 0.0))
            side_c.append(ones_half)
        side_c = jnp.concatenate(side_c, 0).astype(jnp.bfloat16)
        return jnp.dot(
            jnp.concatenate([side_c, side_c], 1),
            jnp.concatenate([weight_high, weight_low], 0),
            preferred_element_type=jnp.float32,
        )

    def terms_of(sums, base, pair):
        terms = []
        for place, sub in enumerate(pair):
            mine = sums[32 * place : 32 * place + 32, LANES * place : LANES * place + LANES]
            axes = [
                parts[pl.ds((24 + axis) * slots + base + sub, 8, stride=0), :] for axis in range(3)
            ]
            force = mine[24:32] * choose(*axes) - (mine[0:8] + mine[8:16] + mine[16:24])
            terms += [
                force,
                force * choose(axes[1], axes[2], axes[0]),
                force * choose(axes[2], axes[0], axes[1]),
            ]
        terms = jnp.concatenate(terms, 0)
        terms_high = terms.astype(jnp.bfloat16)
        terms_low = (terms - terms_high.astype(jnp.float32)).astype(jnp.bfloat16)
        return jnp.concatenate([terms_high, terms_low], 1)

    def scatter(group):
        base = jnp.clip(group, 0, groups - 1) * 8
        row = base >> 7
        spot = base & (LANES - 1)
        for sub in range(8):
            lower = folded_ref[pl.ds(24 * sub, 24), :LANES]
            upper = folded_ref[pl.ds(24 * sub, 24), LANES:]
            live = (group >= 0) & (group * 8 + sub < number)
            block = words[row, spot + sub]
            here = lane24 == jnp.where(live, block & (LANES - 1), -1)
            at = pl.ds(pl.multiple_of((block >> 7) * 24, 8), 24)
            acc_near[at, :] += jnp.where(here, lower + upper, 0.0)
            block = words[slot_rows + row, spot + sub]
            here = lane24 == jnp.where(live, block & (LANES - 1), -1)
            at = pl.ds(pl.multiple_of((block >> 7) * 48, 8), 48)
            acc_far[at, :] += jnp.concatenate(
                [jnp.where(here, lower, 0.0), jnp.where(here, upper, 0.0)], 0
            )

    def chunk(turn, carry):
        arrange(pl.multiple_of(turn * CHUNK, CHUNK))
        fetch(jnp.minimum((turn + 1) * CHUNK, slots - CHUNK))
        return carry

    fetch(jnp.int32(0))
    lax.fori_loop(0, (number + CHUNK - 1) // CHUNK, chunk, 0)

    groups = (number + 7) // 8
    pairs = [(2 * couple, 2 * couple + 1) for couple in range(4)]

    def octet(turn, slot):
        fresh = 4 * LANES * slot
        stale = 4 * LANES * (1 - slot)
        ready = prepare(pl.multiple_of(jnp.minimum(turn, groups - 1) * 8, 8))
        for couple, pair in enumerate(pairs):
            reach_ref[pl.ds(fresh + LANES * couple, LANES), :] = reach_of(*ready, pair)
        scatter(turn - 3)
        base = jnp.clip(turn - 2, 0, groups - 1) * 8
        terms = [
            terms_of(sums_ref[pl.ds(64 * couple, 64), :], base, pair)
            for couple, pair in enumerate(pairs)
        ]
        folded_ref[...] = jnp.dot(
            jnp.concatenate(terms, 0), halves, preferred_element_type=jnp.float32
        )
        base = jnp.clip(turn - 1, 0, groups - 1) * 8
        for couple, pair in enumerate(pairs):
            sums_ref[pl.ds(64 * couple, 64), :] = sums_of(
                reach_ref[pl.ds(stale + LANES * couple, LANES), :], base, pair
            )

    def octets(turn, carry):
        for sub in range(DEPTH):
            octet(DEPTH * turn + sub, sub % 2)
        return carry

    lax.fori_loop(0, (groups + 2 + DEPTH) // DEPTH, octets, 0)

    def total_of(row, half, tiles, start):
        line = (row // 3) * 8 + row % 3
        mine = acc_near[pl.ds(start * 24 + line + 4 * half, tiles, stride=24), :]
        line += 24 * half
        other = (
            acc_far[pl.ds(start * 48 + line, tiles, stride=48), :]
            + acc_far[pl.ds(start * 48 + line + 4, tiles, stride=48), :]
        )
        return (other - mine) * STIFFNESS

    def results_of(half, tiles, start):
        rows = [total_of(row, half, tiles, start) for row in range(9)]
        return rows[0:3] + [
            rows[6 + (axis + 2) % 3] - rows[3 + (axis + 1) % 3] for axis in range(3)
        ]

    own_tiles = own_blocks // LANES
    own_rows = own_tiles * COMPS
    edges = [results_of(half, 2, inner_blocks // LANES) for half in range(2)]
    for k, out in zip(clique_order(piece_count), outs):
        place = jnp.bitwise_xor(clique, k)
        for side in range(2):
            start = (side * piece_count + place) * own_tiles
            for half in range(2):
                for axis, value in enumerate(results_of(half, own_tiles, start)):
                    at = pl.ds(side * own_rows + 6 * half + axis, own_tiles, stride=COMPS)
                    out[at, :] = value
        out[pl.ds(2 * own_rows, RIM_ROWS), :] = jnp.zeros((RIM_ROWS, LANES), jnp.float32)
        for half in range(2):
            for axis, value in enumerate(edges[half]):
                rim = jnp.where(place == 0, value[1:2], value[0:1])
                rim = jnp.where((place == 0) | (place == piece_count - 1), rim, 0.0)
                out[pl.ds(2 * own_rows + 6 * half + axis, 1), :] = rim


def whole_step(positions, rotations, clump_kind, sub_offsets, pair_blocks, pair_count):
    members = lax.axis_size("dev")
    groups = lax.axis_size("grp")
    me = lax.axis_index("dev")
    rings = members // 2
    clique, far = me % rings, me // rings
    clumps = positions.shape[1]
    slots = pair_blocks.shape[1]
    own_blocks = clumps // 2
    kinds, _, _ = sub_offsets.shape
    vmem = pl.BlockSpec(memory_space=pltpu.VMEM)
    smem = pl.BlockSpec(memory_space=pltpu.SMEM)

    payload, end = pl.pallas_call(
        functools.partial(payload_kernel, slots, members),
        out_shape=(
            jax.ShapeDtypeStruct((ROWS, own_blocks), jnp.float32),
            jax.ShapeDtypeStruct((ROWS, RIM), jnp.float32),
        ),
        in_specs=[pl.BlockSpec(memory_space=pltpu.HBM)] * 4 + [smem],
        out_specs=(vmem, vmem),
        scratch_shapes=[
            pltpu.VMEM((3, clumps), jnp.float32),
            pltpu.VMEM((9, clumps), jnp.float32),
            pltpu.VMEM((clumps // LANES, LANES), jnp.int32),
            pltpu.VMEM((2, slots), jnp.int32),
            pltpu.SemaphoreType.DMA((4,)),
        ],
        name="payload_kernel",
    )(positions, rotations, clump_kind.reshape(-1, LANES), pair_blocks, pair_count)

    def trade(value, k):
        return lax.ppermute(value, "dev", [(i, i ^ k) for i in range(members)])

    def cross(value, step, flip):
        steps = [
            (
                g * members + d,
                (g + (step if d < rings else -step)) % groups * members + (d ^ flip),
            )
            for g in range(groups)
            for d in range(members)
        ]
        return lax.ppermute(value, ("grp", "dev"), steps)

    far_payload = trade(payload, rings)
    rim_a = cross(end, -1, 0)
    rim_b = cross(end, -1, rings)
    rim = jnp.where((clique == 0) == (far == 0), rim_a, rim_b)
    both = jnp.concatenate([payload, far_payload, rim], 1)
    order = clique_order(rings)
    pieces = [both] + [trade(both, k) for k in order[1:]]

    offset_table = sub_offsets.astype(jnp.float32) * OFFSET_UNIT
    blank = jnp.zeros_like(offset_table)
    offset_rows = jnp.concatenate(
        [
            jnp.concatenate([offset_table, blank], 2).reshape(kinds, -1),
            jnp.concatenate([blank, offset_table], 2).reshape(kinds, -1),
        ],
        0,
    )
    offset_rows = jnp.concatenate(
        [offset_rows, jnp.zeros((LANES - 2 * kinds, offset_rows.shape[1]), jnp.float32)], 0
    ).astype(jnp.bfloat16)

    inner_blocks = own_blocks * members
    tiles = inner_blocks // LANES
    own_rows = own_blocks // LANES * COMPS
    outs = pl.pallas_call(
        functools.partial(pair_kernel, members, slots),
        out_shape=(jax.ShapeDtypeStruct((2 * own_rows + RIM_ROWS, LANES), jnp.float32),) * rings,
        in_specs=[vmem] * (rings + 1),
        out_specs=(vmem,) * rings,
        scratch_shapes=[
            pltpu.VMEM((inner_blocks + 3 * RIM, LANES), jnp.float32),
            pltpu.VMEM((members * 2 * slots // LANES, LANES), jnp.float32),
            pltpu.VMEM((2 * slots // LANES, LANES), jnp.int32),
            pltpu.SMEM((2 * slots // LANES, LANES), jnp.int32),
            pltpu.VMEM((2 * CHUNK, LANES), jnp.float32),
            pltpu.VMEM((27 * slots, LANES), jnp.float32),
            pltpu.VMEM((8 * LANES, 2 * LANES), jnp.float32),
            pltpu.VMEM((4 * 64, 2 * LANES), jnp.float32),
            pltpu.VMEM((192, 2 * LANES), jnp.float32),
            pltpu.VMEM(((tiles + 2) * 24, LANES), jnp.float32),
            pltpu.VMEM(((tiles + 2) * 48, LANES), jnp.float32),
            pltpu.SemaphoreType.DMA,
        ],
        compiler_params=pltpu.CompilerParams(vmem_limit_bytes=32 << 20),
        name="pair_kernel",
    )(*pieces, offset_rows)

    column = outs[0]
    for k, out in list(zip(order, outs))[:0:-1]:
        column = column + trade(out, k)
    in_low = far == 0
    low, high = column[:own_rows], column[own_rows : 2 * own_rows]
    rim = column[2 * own_rows :]
    other = trade(jnp.where(in_low, high, low), rings)
    rim_a = cross(rim, 1, 0)
    rim_b = cross(rim, -1, rings)
    shares = [jnp.where(in_low, low, high), other, rim_a, rim_b]
    clump_force, clump_torque = pl.pallas_call(
        functools.partial(finish_kernel, members, groups),
        out_shape=(jax.ShapeDtypeStruct((3, clumps), jnp.float32),) * 2,
        in_specs=[vmem] * 5,
        out_specs=(vmem, vmem),
        scratch_shapes=[pltpu.VMEM((own_rows, LANES), jnp.float32)],
        compiler_params=pltpu.CompilerParams(vmem_limit_bytes=4 << 20),
        name="finish_kernel",
    )(*shares, positions)
    return (clump_force, clump_torque)


def solution(mesh):
    placed = (
        P(None, ("grp", "dev")),
        P(None, ("grp", "dev")),
        P(("grp", "dev")),
        P(),
        P(None, ("grp", "dev")),
        P(("grp", "dev")),
    )
    return jax.shard_map(
        whole_step,
        mesh=mesh,
        in_specs=placed,
        out_specs=(P(None, ("grp", "dev")), P(None, ("grp", "dev"))),
        check_vma=False,
    )
```

```python
import functools

import jax
import jax.numpy as jnp
from jax import lax
from jax.experimental import pallas as pl
from jax.experimental.pallas import tpu as pltpu
from jax.sharding import PartitionSpec as P


RIM = 128
LANES = 128
OFFSET_UNIT = 0.125
REACH_SQUARED = 4.0
STIFFNESS = 1.0 / 256.0
CHUNK = 64
COMPS = 12
PARAMS = 10
ROWS = 24
RIM_ROWS = 16
DEPTH = 6


def split3(value):
    high = value.astype(jnp.bfloat16).astype(jnp.float32)
    rest = value - high
    middle = rest.astype(jnp.bfloat16).astype(jnp.float32)
    return high, middle, rest - middle


def clique_order(count):
    return [0, count - 1] + list(range(1, count - 1))


def payload_kernel(slots, members, *refs):
    sources, (count_ref, out_ref, end_ref), landed, sems = refs[:4], refs[4:7], refs[7:11], refs[11]
    copies = [
        pltpu.make_async_copy(source, target, sems.at[turn])
        for turn, (source, target) in enumerate(zip(sources, landed))
    ]
    for copy in copies:
        copy.start()
    for copy in copies:
        copy.wait()
    position_ref, rotation_ref, kind_ref, pair_ref = landed
    clumps = position_ref.shape[1]
    blocks = clumps // 2
    inner_blocks = blocks * members
    wide = 2 * LANES
    row = lax.broadcasted_iota(jnp.int32, (wide, wide), 0)
    column = lax.broadcasted_iota(jnp.int32, (wide, wide), 1)
    source = jnp.where(column < LANES, 2 * column, 2 * column - (wide - 1))
    picked = jnp.where(row == source, 1.0, 0.0).astype(jnp.bfloat16)
    parts = []
    for turn in range(clumps // wide):
        at = slice(turn * wide, (turn + 1) * wide)
        kinds = kind_ref[2 * turn : 2 * turn + 2, :].astype(jnp.float32)
        value = jnp.concatenate(
            [
                position_ref[:, at],
                rotation_ref[0:6, at],
                jnp.concatenate([kinds[0:1], kinds[1:2]], 1),
                jnp.zeros((16 - PARAMS, wide), jnp.float32),
            ],
            0,
        )
        parts += [piece.astype(jnp.bfloat16) for piece in split3(value)]
    sorted_parts = jnp.dot(
        jnp.concatenate(parts, 0), picked, preferred_element_type=jnp.float32
    )
    for turn in range(clumps // wide):
        high, middle, low = (sorted_parts[16 * (3 * turn + part) : 16 * (3 * turn + part) + 16] for part in range(3))
        value = (high + middle) + low
        at = slice(turn * LANES, (turn + 1) * LANES)
        out_ref[0:PARAMS, at] = value[0:PARAMS, :LANES]
        out_ref[PARAMS : 2 * PARAMS, at] = value[0:PARAMS, LANES:]
    pairs = pair_ref[...] - lax.axis_index("grp") * inner_blocks
    pairs = jnp.where(
        pairs < 0,
        pairs + inner_blocks + RIM,
        jnp.where(pairs >= inner_blocks, pairs + RIM, pairs),
    )
    live = lax.broadcasted_iota(jnp.int32, pairs.shape, 1) < count_ref[0]
    pairs = jnp.where(live, pairs, -1).astype(jnp.float32)
    lists = slots // blocks
    for which in range(2):
        for part in range(lists):
            out_ref[pl.ds(2 * PARAMS + which * lists + part, 1), :] = pairs[
                which : which + 1, part * blocks : (part + 1) * blocks
            ]
    in_low = lax.axis_index("dev") < members // 2
    end_ref[...] = jnp.where(in_low, out_ref[:, :RIM], out_ref[:, blocks - RIM :])


def finish_kernel(members, groups, own_ref, *refs):
    other_ref, rim_a_ref, rim_b_ref, position_ref, force_ref, torque_ref, total_ref = refs
    me, group = lax.axis_index("dev"), lax.axis_index("grp")
    total_ref[...] = own_ref[...] + other_ref[...]
    rim = rim_a_ref[0:COMPS] + rim_b_ref[0:COMPS]
    first = (me == 0) & (group > 0)
    final = (me == members - 1) & (group < groups - 1)
    total_ref[0:COMPS] += jnp.where(first, rim, 0.0)
    total_ref[own_ref.shape[0] - COMPS :] += jnp.where(final, rim, 0.0)
    tiles = own_ref.shape[0] // COMPS
    wide = 2 * LANES
    row = lax.broadcasted_iota(jnp.int32, (wide, wide), 0)
    column = lax.broadcasted_iota(jnp.int32, (wide, wide), 1)
    target = jnp.where(row < LANES, 2 * row, 2 * row - (wide - 1))
    placed = jnp.where(column == target, 1.0, 0.0).astype(jnp.bfloat16)
    halves = [
        jnp.concatenate(
            [total_ref[pl.ds(6 * half + comp, tiles, stride=COMPS), :] for comp in range(6)], 0
        )
        for half in range(2)
    ]
    value = jnp.concatenate(halves, 1)
    rows = value.shape[0]
    joined = jnp.dot(
        jnp.concatenate([part.astype(jnp.bfloat16) for part in split3(value)], 0),
        placed,
        preferred_element_type=jnp.float32,
    )
    value = (joined[0:rows] + joined[rows : 2 * rows]) + joined[2 * rows : 3 * rows]
    comps = [value[comp * tiles : (comp + 1) * tiles] for comp in range(6)]
    centre = [
        jnp.concatenate(
            [position_ref[axis : axis + 1, tile * wide : (tile + 1) * wide] for tile in range(tiles)], 0
        )
        for axis in range(3)
    ]
    for axis in range(3):
        after, last = (axis + 1) % 3, (axis + 2) % 3
        torque = comps[3 + axis] - (centre[after] * comps[last] - centre[last] * comps[after])
        for tile in range(tiles):
            at = slice(tile * wide, (tile + 1) * wide)
            force_ref[axis : axis + 1, at] = comps[axis][tile : tile + 1]
            torque_ref[axis : axis + 1, at] = torque[tile : tile + 1]


def pair_kernel(members, slots, *refs):
    piece_count = members // 2
    pieces = refs[:piece_count]
    off_ref = refs[piece_count]
    outs = refs[piece_count + 1 : 2 * piece_count + 1]
    (table, list_ref, word_ref, words, gathered, parts, reach_ref, sums_ref, folded_ref, acc_near,
     acc_far, sem) = refs[2 * piece_count + 1 :]
    me = lax.axis_index("dev")
    clique = lax.rem(me, piece_count)
    own_blocks = (pieces[0].shape[1] - RIM) // 2
    inner_blocks = members * own_blocks
    slot_rows = slots // LANES

    owners = []
    counts = []
    for k in range(piece_count):
        for side in range(2):
            owners.append(jnp.bitwise_xor(me, clique_order(piece_count)[k] + side * piece_count))
            base = (2 * k + side) * 2 * slot_rows
            for part in range(2 * slot_rows):
                line, spot = part // (own_blocks // LANES), part % (own_blocks // LANES)
                at = side * own_blocks + spot * LANES
                list_ref[pl.ds(base + part, 1), :] = pieces[k][
                    pl.ds(2 * PARAMS + line, 1), at : at + LANES
                ]
            found = jnp.where(list_ref[pl.ds(base, slot_rows), :] >= 0.0, 1.0, 0.0)
            counts.append(jnp.sum(found).astype(jnp.int32))
    starts = []
    total = jnp.int32(0)
    for index in range(members):
        start = jnp.int32(0)
        for other in range(members):
            if other != index:
                start = start + jnp.where(owners[other] < owners[index], counts[other], 0)
        starts.append(start)
        total = total + counts[index]
    begin = (total * me) // members
    finish = (total * (me + 1)) // members
    number = finish - begin

    flat = lax.broadcasted_iota(jnp.int32, (slot_rows, LANES), 0) * LANES
    column = lax.broadcasted_iota(jnp.int32, (slot_rows, LANES), 1)
    flat = flat + column
    near_list = jnp.zeros((slot_rows, LANES), jnp.float32)
    far_list = jnp.zeros((slot_rows, LANES), jnp.float32)
    for index in range(members):
        start = starts[index]
        low = jnp.maximum(start, begin) - begin
        high = jnp.minimum(start + counts[index], finish) - begin
        shift = jnp.bitwise_and(start - begin, slots - 1)
        wanted = (flat >= low) & (flat < high)

        def moved(rows, shift=shift):
            turned = pltpu.roll(rows, shift & (LANES - 1), axis=1)
            same = pltpu.roll(turned, shift >> 7, axis=0)
            following = pltpu.roll(turned, (shift >> 7) + 1, axis=0)
            return jnp.where(column < (shift & (LANES - 1)), following, same)

        base = index * 2 * slot_rows
        near_list = jnp.where(wanted, moved(list_ref[pl.ds(base, slot_rows), :]), near_list)
        far_list = jnp.where(wanted, moved(list_ref[pl.ds(base + slot_rows, slot_rows), :]), far_list)
    for start, found in ((0, near_list), (2 * slot_rows, far_list)):
        value = found.astype(jnp.int32)
        word_ref[pl.ds(start, slot_rows, stride=2), :] = value
        word_ref[pl.ds(start + 1, slot_rows, stride=2), :] = pltpu.roll(value, CHUNK, axis=1)
    copy = pltpu.make_async_copy(word_ref, words, sem)
    copy.start()

    for k in range(piece_count):
        for side in range(2):
            base = pl.multiple_of(owners[2 * k + side] * own_blocks, LANES)
            for tile in range(own_blocks // LANES):
                at = side * own_blocks + tile * LANES
                table[pl.ds(base + tile * LANES, LANES), 0:ROWS] = pieces[k][:, at : at + LANES].T
        place = jnp.bitwise_xor(clique, clique_order(piece_count)[k])
        base = jnp.where(place == 0, RIM, jnp.where(place == piece_count - 1, 0, 2 * RIM))
        table[pl.ds(pl.multiple_of(inner_blocks + base, RIM), RIM), 0:ROWS] = pieces[k][
            :, 2 * own_blocks :
        ].T

    def clear(turn, carry):
        acc_near[pl.ds(pl.multiple_of(turn * 48, 8), 48), :] = jnp.zeros((48, LANES), jnp.float32)
        acc_far[pl.ds(pl.multiple_of(turn * 96, 8), 96), :] = jnp.zeros((96, LANES), jnp.float32)
        return carry

    lax.fori_loop(0, acc_near.shape[0] // 48, clear, 0)

    copy.wait()

    lane = lax.broadcasted_iota(jnp.int32, (2 * CHUNK, LANES), 1)
    column_of = jnp.where(lane < LANES // 2, 0, PARAMS)
    lane_f = (lane & 7).astype(jnp.float32)
    pick_low = lane < 8
    pick_all = lane < 16
    lane24 = lax.broadcasted_iota(jnp.int32, (24, LANES), 1)
    row8 = lax.broadcasted_iota(jnp.int32, (8, LANES), 0)
    lane8 = lax.broadcasted_iota(jnp.int32, (8, LANES), 1)
    row_first = (row8 & 3) == 0
    row_second = (row8 & 3) == 1
    half8 = (row8 < 4) == (lane8 < LANES // 2)
    ones_half = jnp.where(half8, 1.0, 0.0)
    row_sum = lax.broadcasted_iota(jnp.int32, (2 * LANES, 2 * LANES), 0)
    col_sum = lax.broadcasted_iota(jnp.int32, (2 * LANES, 2 * LANES), 1)
    halves = jnp.where(
        ((row_sum & (LANES - 1)) >= LANES // 2) == (col_sum >= LANES), 1.0, 0.0
    ).astype(jnp.bfloat16)
    row16 = lax.broadcasted_iota(jnp.int32, (16, LANES), 0)
    keeps = [jnp.where((row16 & 7) == sub, 1.0, 0.0).astype(jnp.bfloat16) for sub in range(8)]

    def fetch(turn):
        for index in range(CHUNK):
            near = words[turn, index]
            far = words[2 * slot_rows + turn, index]
            gathered[pl.ds(index, 1), :] = table[pl.ds(near, 1), :]
            gathered[pl.ds(CHUNK + index, 1), :] = table[pl.ds(far, 1), :]

    def arrange(first):
        def keep_part(slot, value):
            parts[pl.ds(pl.multiple_of(slot * slots + first, 8), CHUNK), :] = value

        packed = gathered[...]

        def spread(column):
            return jnp.take_along_axis(
                packed, column_of + column, axis=1, mode="promise_in_bounds"
            )

        kind_low = jnp.take_along_axis(
            packed, jnp.where(pick_low, 9, PARAMS + 9), axis=1, mode="promise_in_bounds"
        )
        pick = jnp.where(pick_all & (kind_low == lane_f), 1.0, 0.0).astype(jnp.bfloat16)
        offsets = jnp.dot(pick, off_ref[...], preferred_element_type=jnp.float32)
        turns = [spread(3 + entry) for entry in range(6)]
        for mode in range(3):
            after, last = (mode + 1) % 3, (mode + 2) % 3
            turns.append(turns[after] * turns[3 + last] - turns[last] * turns[3 + after])
        where_at = []
        for axis in range(3):
            value = spread(axis)
            for mode in range(3):
                value = value + turns[3 * axis + mode] * offsets[:, mode * LANES : (mode + 1) * LANES]
            where_at.append(value)
        near = [value[:CHUNK] for value in where_at]
        far = [value[CHUNK:] for value in where_at]
        near_sq = near[0] * near[0] + near[1] * near[1] + near[2] * near[2]
        far_sq = far[0] * far[0] + far[1] * far[1] + far[2] * far[2]
        for axis, value in enumerate(near + [REACH_SQUARED - near_sq]):
            for part, piece in enumerate(split3(value)):
                keep_part(4 * part + axis, piece)
        for axis, value in enumerate([2.0 * value for value in far] + [-far_sq]):
            for part, piece in enumerate(split3(value)):
                keep_part(12 + 4 * part + axis, piece)
        for axis in range(3):
            keep_part(24 + axis, far[axis])

    one8 = jnp.ones((8, LANES), jnp.float32)

    def choose(first, second, third):
        return jnp.where(row_first, first, jnp.where(row_second, second, third))

    def prepare(base):
        def part(slot):
            return parts[pl.ds(slot * slots + base, 8), :]

        near = [[part(4 * which + axis) for axis in range(4)] for which in range(3)]
        far = [[part(12 + 4 * which + axis) for axis in range(4)] for which in range(3)]
        rows_a, rows_b = [], []
        for a, b, a_last, b_last in (
            (0, 0, near[0][3], one8),
            (0, 1, one8, far[1][3]),
            (1, 0, near[1][3], one8),
            (1, 1, one8, far[0][3]),
            (0, 2, one8, far[2][3]),
            (2, 0, near[2][3], one8),
        ):
            rows_a += near[a][:3] + [a_last]
            rows_b += far[b][:3] + [b_last]
        all_a = jnp.concatenate(rows_a, 0).astype(jnp.bfloat16)
        tiles_b = [
            jnp.concatenate(rows_b[2 * tile : 2 * tile + 2], 0).astype(jnp.bfloat16)
            for tile in range(12)
        ]
        return all_a, tiles_b

    def reach_of(all_a, tiles_b, pair):
        side_b = jnp.concatenate(
            [jnp.concatenate([tile * keeps[sub] for tile in tiles_b], 0) for sub in pair], 1
        )
        return lax.dot_general(
            all_a, side_b, (((0,), (0,)), ((), ())), preferred_element_type=jnp.float32
        )

    def sums_of(reach, base, pair):
        weight = jnp.maximum(reach, 0.0)
        weight_high = weight.astype(jnp.bfloat16)
        weight_low = (weight - weight_high.astype(jnp.float32)).astype(jnp.bfloat16)
        side_c = []
        for sub in pair:
            for which in range(3):
                row = choose(
                    *[
                        parts[pl.ds((4 * which + axis) * slots + base + sub, 8, stride=0), :]
                        for axis in range(3)
                    ]
                )
                side_c.append(jnp.where(half8, row, 0.0))
            side_c.append(ones_half)
        side_c = jnp.concatenate(side_c, 0).astype(jnp.bfloat16)
        return jnp.dot(
            jnp.concatenate([side_c, side_c], 1),
            jnp.concatenate([weight_high, weight_low], 0),
            preferred_element_type=jnp.float32,
        )

    def terms_of(sums, base, pair):
        terms = []
        for place, sub in enumerate(pair):
            mine = sums[32 * place : 32 * place + 32, LANES * place : LANES * place + LANES]
            axes = [
                parts[pl.ds((24 + axis) * slots + base + sub, 8, stride=0), :] for axis in range(3)
            ]
            force = mine[24:32] * choose(*axes) - (mine[0:8] + mine[8:16] + mine[16:24])
            terms += [
                force,
                force * choose(axes[1], axes[2], axes[0]),
                force * choose(axes[2], axes[0], axes[1]),
            ]
        terms = jnp.concatenate(terms, 0)
        terms_high = terms.astype(jnp.bfloat16)
        terms_low = (terms - terms_high.astype(jnp.float32)).astype(jnp.bfloat16)
        return jnp.concatenate([terms_high, terms_low], 1)

    def scatter(group):
        base = jnp.clip(group, 0, groups - 1) * 8
        row = base // CHUNK
        spot = lax.rem(base, CHUNK)
        for sub in range(8):
            lower = folded_ref[pl.ds(24 * sub, 24), :LANES]
            upper = folded_ref[pl.ds(24 * sub, 24), LANES:]
            live = (group >= 0) & (group * 8 + sub < number)
            block = words[row, spot + sub]
            here = lane24 == jnp.where(live, block & (LANES - 1), -1)
            at = pl.ds(pl.multiple_of((block >> 7) * 24, 8), 24)
            acc_near[at, :] += jnp.where(here, lower + upper, 0.0)
            block = words[2 * slot_rows + row, spot + sub]
            here = lane24 == jnp.where(live, block & (LANES - 1), -1)
            at = pl.ds(pl.multiple_of((block >> 7) * 48, 8), 48)
            acc_far[at, :] += jnp.concatenate(
                [jnp.where(here, lower, 0.0), jnp.where(here, upper, 0.0)], 0
            )

    def chunk(turn, carry):
        arrange(pl.multiple_of(turn * CHUNK, CHUNK))
        fetch(jnp.minimum(turn + 1, slots // CHUNK - 1))
        return carry

    fetch(jnp.int32(0))
    lax.fori_loop(0, (number + CHUNK - 1) // CHUNK, chunk, 0)

    groups = (number + 7) // 8
    pairs = [(2 * couple, 2 * couple + 1) for couple in range(4)]

    def octet(turn, slot):
        fresh = 4 * LANES * slot
        stale = 4 * LANES * (1 - slot)
        ready = prepare(pl.multiple_of(jnp.minimum(turn, groups - 1) * 8, 8))
        for couple, pair in enumerate(pairs):
            reach_ref[pl.ds(fresh + LANES * couple, LANES), :] = reach_of(*ready, pair)
        scatter(turn - 3)
        base = jnp.clip(turn - 2, 0, groups - 1) * 8
        terms = [
            terms_of(sums_ref[pl.ds(64 * couple, 64), :], base, pair)
            for couple, pair in enumerate(pairs)
        ]
        folded_ref[...] = jnp.dot(
            jnp.concatenate(terms, 0), halves, preferred_element_type=jnp.float32
        )
        base = jnp.clip(turn - 1, 0, groups - 1) * 8
        for couple, pair in enumerate(pairs):
            sums_ref[pl.ds(64 * couple, 64), :] = sums_of(
                reach_ref[pl.ds(stale + LANES * couple, LANES), :], base, pair
            )

    def octets(turn, carry):
        for sub in range(DEPTH):
            octet(DEPTH * turn + sub, sub % 2)
        return carry

    lax.fori_loop(0, (groups + 2 + DEPTH) // DEPTH, octets, 0)

    def total_of(row, half, tiles, start):
        line = (row // 3) * 8 + row % 3
        mine = acc_near[pl.ds(start * 24 + line + 4 * half, tiles, stride=24), :]
        line += 24 * half
        other = (
            acc_far[pl.ds(start * 48 + line, tiles, stride=48), :]
            + acc_far[pl.ds(start * 48 + line + 4, tiles, stride=48), :]
        )
        return (other - mine) * STIFFNESS

    def results_of(half, tiles, start):
        rows = [total_of(row, half, tiles, start) for row in range(9)]
        return rows[0:3] + [
            rows[6 + (axis + 2) % 3] - rows[3 + (axis + 1) % 3] for axis in range(3)
        ]

    own_tiles = own_blocks // LANES
    own_rows = own_tiles * COMPS
    edges = [results_of(half, 2, inner_blocks // LANES) for half in range(2)]
    for k, out in zip(clique_order(piece_count), outs):
        place = jnp.bitwise_xor(clique, k)
        for side in range(2):
            start = (side * piece_count + place) * own_tiles
            for half in range(2):
                for axis, value in enumerate(results_of(half, own_tiles, start)):
                    at = pl.ds(side * own_rows + 6 * half + axis, own_tiles, stride=COMPS)
                    out[at, :] = value
        out[pl.ds(2 * own_rows, RIM_ROWS), :] = jnp.zeros((RIM_ROWS, LANES), jnp.float32)
        for half in range(2):
            for axis, value in enumerate(edges[half]):
                rim = jnp.where(place == 0, value[1:2], value[0:1])
                rim = jnp.where((place == 0) | (place == piece_count - 1), rim, 0.0)
                out[pl.ds(2 * own_rows + 6 * half + axis, 1), :] = rim


def whole_step(positions, rotations, clump_kind, sub_offsets, pair_blocks, pair_count):
    members = lax.axis_size("dev")
    groups = lax.axis_size("grp")
    me = lax.axis_index("dev")
    rings = members // 2
    clique, far = me % rings, me // rings
    clumps = positions.shape[1]
    slots = pair_blocks.shape[1]
    own_blocks = clumps // 2
    kinds, _, _ = sub_offsets.shape
    vmem = pl.BlockSpec(memory_space=pltpu.VMEM)
    smem = pl.BlockSpec(memory_space=pltpu.SMEM)

    payload, end = pl.pallas_call(
        functools.partial(payload_kernel, slots, members),
        out_shape=(
            jax.ShapeDtypeStruct((ROWS, own_blocks), jnp.float32),
            jax.ShapeDtypeStruct((ROWS, RIM), jnp.float32),
        ),
        in_specs=[pl.BlockSpec(memory_space=pltpu.HBM)] * 4 + [smem],
        out_specs=(vmem, vmem),
        scratch_shapes=[
            pltpu.VMEM((3, clumps), jnp.float32),
            pltpu.VMEM((9, clumps), jnp.float32),
            pltpu.VMEM((clumps // LANES, LANES), jnp.int32),
            pltpu.VMEM((2, slots), jnp.int32),
            pltpu.SemaphoreType.DMA((4,)),
        ],
        name="payload_kernel",
    )(positions, rotations, clump_kind.reshape(-1, LANES), pair_blocks, pair_count)

    def trade(value, k):
        return lax.ppermute(value, "dev", [(i, i ^ k) for i in range(members)])

    def cross(value, step, flip):
        steps = [
            (
                g * members + d,
                (g + (step if d < rings else -step)) % groups * members + (d ^ flip),
            )
            for g in range(groups)
            for d in range(members)
        ]
        return lax.ppermute(value, ("grp", "dev"), steps)

    far_payload = trade(payload, rings)
    rim_a = cross(end, -1, 0)
    rim_b = cross(end, -1, rings)
    rim = jnp.where((clique == 0) == (far == 0), rim_a, rim_b)
    both = jnp.concatenate([payload, far_payload, rim], 1)
    order = clique_order(rings)
    pieces = [both] + [trade(both, k) for k in order[1:]]

    offset_table = sub_offsets.astype(jnp.float32) * OFFSET_UNIT
    blank = jnp.zeros_like(offset_table)
    offset_rows = jnp.concatenate(
        [
            jnp.concatenate([offset_table, blank], 2).reshape(kinds, -1),
            jnp.concatenate([blank, offset_table], 2).reshape(kinds, -1),
        ],
        0,
    )
    offset_rows = jnp.concatenate(
        [offset_rows, jnp.zeros((LANES - 2 * kinds, offset_rows.shape[1]), jnp.float32)], 0
    ).astype(jnp.bfloat16)

    inner_blocks = own_blocks * members
    tiles = inner_blocks // LANES
    own_rows = own_blocks // LANES * COMPS
    outs = pl.pallas_call(
        functools.partial(pair_kernel, members, slots),
        out_shape=(jax.ShapeDtypeStruct((2 * own_rows + RIM_ROWS, LANES), jnp.float32),) * rings,
        in_specs=[vmem] * (rings + 1),
        out_specs=(vmem,) * rings,
        scratch_shapes=[
            pltpu.VMEM((inner_blocks + 3 * RIM, LANES), jnp.float32),
            pltpu.VMEM((members * 2 * slots // LANES, LANES), jnp.float32),
            pltpu.VMEM((2 * slots // CHUNK, LANES), jnp.int32),
            pltpu.SMEM((2 * slots // CHUNK, LANES), jnp.int32),
            pltpu.VMEM((2 * CHUNK, LANES), jnp.float32),
            pltpu.VMEM((27 * slots, LANES), jnp.float32),
            pltpu.VMEM((8 * LANES, 2 * LANES), jnp.float32),
            pltpu.VMEM((4 * 64, 2 * LANES), jnp.float32),
            pltpu.VMEM((192, 2 * LANES), jnp.float32),
            pltpu.VMEM(((tiles + 2) * 24, LANES), jnp.float32),
            pltpu.VMEM(((tiles + 2) * 48, LANES), jnp.float32),
            pltpu.SemaphoreType.DMA,
        ],
        compiler_params=pltpu.CompilerParams(vmem_limit_bytes=32 << 20),
        name="pair_kernel",
    )(*pieces, offset_rows)

    column = outs[0]
    for k, out in list(zip(order, outs))[:0:-1]:
        column = column + trade(out, k)
    in_low = far == 0
    low, high = column[:own_rows], column[own_rows : 2 * own_rows]
    rim = column[2 * own_rows :]
    other = trade(jnp.where(in_low, high, low), rings)
    rim_a = cross(rim, 1, 0)
    rim_b = cross(rim, -1, rings)
    shares = [jnp.where(in_low, low, high), other, rim_a, rim_b]
    clump_force, clump_torque = pl.pallas_call(
        functools.partial(finish_kernel, members, groups),
        out_shape=(jax.ShapeDtypeStruct((3, clumps), jnp.float32),) * 2,
        in_specs=[vmem] * 5,
        out_specs=(vmem, vmem),
        scratch_shapes=[pltpu.VMEM((own_rows, LANES), jnp.float32)],
        compiler_params=pltpu.CompilerParams(vmem_limit_bytes=4 << 20),
        name="finish_kernel",
    )(*shares, positions)
    return (clump_force, clump_torque)


def solution(mesh):
    placed = (
        P(None, ("grp", "dev")),
        P(None, ("grp", "dev")),
        P(("grp", "dev")),
        P(),
        P(None, ("grp", "dev")),
        P(("grp", "dev")),
    )
    return jax.shard_map(
        whole_step,
        mesh=mesh,
        in_specs=placed,
        out_specs=(P(None, ("grp", "dev")), P(None, ("grp", "dev"))),
        check_vma=False,
    )
```

```python
import functools

import jax
import jax.numpy as jnp
from jax import lax
from jax.experimental import pallas as pl
from jax.experimental.pallas import tpu as pltpu
from jax.sharding import PartitionSpec as P


RIM = 128
LANES = 128
OFFSET_UNIT = 0.125
REACH_SQUARED = 4.0
STIFFNESS = 1.0 / 256.0
CHUNK = 64
COMPS = 12
PARAMS = 8
ROWS = 16
RIM_ROWS = 16
DEPTH = 6


def split3(value):
    high = value.astype(jnp.bfloat16).astype(jnp.float32)
    rest = value - high
    middle = rest.astype(jnp.bfloat16).astype(jnp.float32)
    return high, middle, rest - middle


def quaternion(entries):
    (xx, xy, xz), (yx, yy, yz), (zx, zy, zz) = entries[0:3], entries[3:6], entries[6:9]
    squares = [1.0 + xx + yy + zz, 1.0 + xx - yy - zz, 1.0 - xx + yy - zz, 1.0 - xx - yy + zz]
    forms = [
        [squares[0], zy - yz, xz - zx, yx - xy],
        [zy - yz, squares[1], yx + xy, xz + zx],
        [xz - zx, yx + xy, squares[2], zy + yz],
        [yx - xy, xz + zx, zy + yz, squares[3]],
    ]
    largest, form = squares[0], forms[0]
    for square, other in zip(squares[1:], forms[1:]):
        better = square > largest
        largest = jnp.where(better, square, largest)
        form = [jnp.where(better, new, old) for new, old in zip(other, form)]
    scale = 0.5 / jnp.sqrt(largest)
    return [entry * scale for entry in form]


def rotation(real, first, second, third):
    length = real * real + first * first + second * second + third * third
    double = 4.0 - 2.0 * length
    along = [double * first, double * second, double * third]
    xx, yy, zz = along[0] * first, along[1] * second, along[2] * third
    xy, xz, yz = along[0] * second, along[0] * third, along[1] * third
    wx, wy, wz = along[0] * real, along[1] * real, along[2] * real
    return [
        1.0 - (yy + zz), xy - wz, xz + wy,
        xy + wz, 1.0 - (xx + zz), yz - wx,
        xz - wy, yz + wx, 1.0 - (xx + yy),
    ]


def clique_order(count):
    return [0, count - 1] + list(range(1, count - 1))


def payload_kernel(slots, members, *refs):
    sources, (count_ref, out_ref, end_ref), landed, sems = refs[:4], refs[4:7], refs[7:11], refs[11]
    copies = [
        pltpu.make_async_copy(source, target, sems.at[turn])
        for turn, (source, target) in enumerate(zip(sources, landed))
    ]
    for copy in copies:
        copy.start()
    for copy in copies:
        copy.wait()
    position_ref, rotation_ref, kind_ref, pair_ref = landed
    clumps = position_ref.shape[1]
    blocks = clumps // 2
    inner_blocks = blocks * members
    wide = 2 * LANES
    row = lax.broadcasted_iota(jnp.int32, (wide, wide), 0)
    column = lax.broadcasted_iota(jnp.int32, (wide, wide), 1)
    source = jnp.where(column < LANES, 2 * column, 2 * column - (wide - 1))
    picked = jnp.where(row == source, 1.0, 0.0).astype(jnp.bfloat16)
    turned = quaternion([rotation_ref[entry : entry + 1, :] for entry in range(9)])
    parts = []
    for turn in range(clumps // wide):
        at = slice(turn * wide, (turn + 1) * wide)
        kinds = kind_ref[2 * turn : 2 * turn + 2, :].astype(jnp.float32)
        value = jnp.concatenate(
            [position_ref[:, at]]
            + [entry[:, at] for entry in turned]
            + [jnp.concatenate([kinds[0:1], kinds[1:2]], 1)],
            0,
        )
        parts += [piece.astype(jnp.bfloat16) for piece in split3(value)]
    sorted_parts = jnp.dot(
        jnp.concatenate(parts, 0), picked, preferred_element_type=jnp.float32
    )
    for turn in range(clumps // wide):
        high, middle, low = (
            sorted_parts[PARAMS * (3 * turn + part) : PARAMS * (3 * turn + part + 1)]
            for part in range(3)
        )
        value = (high + middle) + low
        at = slice(turn * LANES, (turn + 1) * LANES)
        out_ref[0:PARAMS, at] = value[:, :LANES]
        out_ref[PARAMS : 2 * PARAMS, at] = value[:, LANES:]
    pairs = pair_ref[...] - lax.axis_index("grp") * inner_blocks
    pairs = jnp.where(
        pairs < 0,
        pairs + inner_blocks + RIM,
        jnp.where(pairs >= inner_blocks, pairs + RIM, pairs),
    )
    live = lax.broadcasted_iota(jnp.int32, pairs.shape, 1) < count_ref[0]
    pairs = jnp.where(live, pairs, -1).astype(jnp.float32)
    slot_rows = slots // LANES
    for which in range(2):
        for part in range(slot_rows):
            out_ref[pl.ds(which * slot_rows + part, 1), blocks:] = pairs[
                which : which + 1, part * LANES : (part + 1) * LANES
            ]
    in_low = lax.axis_index("dev") < members // 2
    end_ref[...] = jnp.where(in_low, out_ref[:, :RIM], out_ref[:, blocks - RIM : blocks])


def finish_kernel(members, groups, own_ref, *refs):
    other_ref, rim_a_ref, rim_b_ref, position_ref, force_ref, torque_ref, total_ref = refs
    me, group = lax.axis_index("dev"), lax.axis_index("grp")
    total_ref[...] = own_ref[...] + other_ref[...]
    rim = rim_a_ref[0:COMPS] + rim_b_ref[0:COMPS]
    first = (me == 0) & (group > 0)
    final = (me == members - 1) & (group < groups - 1)
    total_ref[0:COMPS] += jnp.where(first, rim, 0.0)
    total_ref[own_ref.shape[0] - COMPS :] += jnp.where(final, rim, 0.0)
    tiles = own_ref.shape[0] // COMPS
    wide = 2 * LANES
    row = lax.broadcasted_iota(jnp.int32, (wide, wide), 0)
    column = lax.broadcasted_iota(jnp.int32, (wide, wide), 1)
    target = jnp.where(row < LANES, 2 * row, 2 * row - (wide - 1))
    placed = jnp.where(column == target, 1.0, 0.0).astype(jnp.bfloat16)
    halves = [
        jnp.concatenate(
            [total_ref[pl.ds(6 * half + comp, tiles, stride=COMPS), :] for comp in range(6)], 0
        )
        for half in range(2)
    ]
    value = jnp.concatenate(halves, 1)
    rows = value.shape[0]
    joined = jnp.dot(
        jnp.concatenate([part.astype(jnp.bfloat16) for part in split3(value)], 0),
        placed,
        preferred_element_type=jnp.float32,
    )
    value = (joined[0:rows] + joined[rows : 2 * rows]) + joined[2 * rows : 3 * rows]
    comps = [value[comp * tiles : (comp + 1) * tiles] for comp in range(6)]
    centre = [
        jnp.concatenate(
            [position_ref[axis : axis + 1, tile * wide : (tile + 1) * wide] for tile in range(tiles)], 0
        )
        for axis in range(3)
    ]
    for axis in range(3):
        after, last = (axis + 1) % 3, (axis + 2) % 3
        torque = comps[3 + axis] - (centre[after] * comps[last] - centre[last] * comps[after])
        for tile in range(tiles):
            at = slice(tile * wide, (tile + 1) * wide)
            force_ref[axis : axis + 1, at] = comps[axis][tile : tile + 1]
            torque_ref[axis : axis + 1, at] = torque[tile : tile + 1]


def pair_kernel(members, slots, *refs):
    piece_count = members // 2
    pieces = refs[:piece_count]
    off_ref = refs[piece_count]
    outs = refs[piece_count + 1 : 2 * piece_count + 1]
    (table, word_ref, words, gathered, parts, reach_ref, sums_ref, folded_ref, acc_near,
     acc_far, sem) = refs[2 * piece_count + 1 :]
    me = lax.axis_index("dev")
    clique = lax.rem(me, piece_count)
    own_columns = (pieces[0].shape[1] - RIM) // 2
    own_blocks = own_columns - LANES
    inner_blocks = members * own_blocks
    slot_rows = slots // LANES

    owners = []
    counts = []
    slot_lists = []
    for k in range(piece_count):
        for side in range(2):
            owners.append(jnp.bitwise_xor(me, clique_order(piece_count)[k] + side * piece_count))
            at = side * own_columns + own_blocks
            both_lists = pieces[k][:, at : at + LANES]
            slot_lists.append((both_lists[0:slot_rows], both_lists[slot_rows : 2 * slot_rows]))
            found = jnp.where(slot_lists[-1][0] >= 0.0, 1.0, 0.0)
            counts.append(jnp.sum(found).astype(jnp.int32))
    starts = []
    total = jnp.int32(0)
    for index in range(members):
        start = jnp.int32(0)
        for other in range(members):
            if other != index:
                start = start + jnp.where(owners[other] < owners[index], counts[other], 0)
        starts.append(start)
        total = total + counts[index]
    begin = (total * me) // members
    finish = (total * (me + 1)) // members
    number = finish - begin

    flat = lax.broadcasted_iota(jnp.int32, (slot_rows, LANES), 0) * LANES
    column = lax.broadcasted_iota(jnp.int32, (slot_rows, LANES), 1)
    flat = flat + column
    near_list = jnp.zeros((slot_rows, LANES), jnp.float32)
    far_list = jnp.zeros((slot_rows, LANES), jnp.float32)
    for index in range(members):
        start = starts[index]
        low = jnp.maximum(start, begin) - begin
        high = jnp.minimum(start + counts[index], finish) - begin
        shift = jnp.bitwise_and(start - begin, slots - 1)
        wanted = (flat >= low) & (flat < high)

        def moved(rows, shift=shift):
            turned = pltpu.roll(rows, shift & (LANES - 1), axis=1)
            same = pltpu.roll(turned, shift >> 7, axis=0)
            following = pltpu.roll(turned, (shift >> 7) + 1, axis=0)
            return jnp.where(column < (shift & (LANES - 1)), following, same)

        near_list = jnp.where(wanted, moved(slot_lists[index][0]), near_list)
        far_list = jnp.where(wanted, moved(slot_lists[index][1]), far_list)
    for start, found in ((0, near_list), (2 * slot_rows, far_list)):
        value = found.astype(jnp.int32)
        word_ref[pl.ds(start, slot_rows, stride=2), :] = value
        word_ref[pl.ds(start + 1, slot_rows, stride=2), :] = pltpu.roll(value, CHUNK, axis=1)
    copy = pltpu.make_async_copy(word_ref, words, sem)
    copy.start()

    for k in range(piece_count):
        for side in range(2):
            base = pl.multiple_of(owners[2 * k + side] * own_blocks, LANES)
            for tile in range(own_blocks // LANES):
                at = side * own_columns + tile * LANES
                table[pl.ds(base + tile * LANES, LANES), 0:ROWS] = pieces[k][:, at : at + LANES].T
        place = jnp.bitwise_xor(clique, clique_order(piece_count)[k])
        base = jnp.where(place == 0, RIM, jnp.where(place == piece_count - 1, 0, 2 * RIM))
        table[pl.ds(pl.multiple_of(inner_blocks + base, RIM), RIM), 0:ROWS] = pieces[k][
            :, 2 * own_columns :
        ].T

    def clear(turn, carry):
        acc_near[pl.ds(pl.multiple_of(turn * 48, 8), 48), :] = jnp.zeros((48, LANES), jnp.float32)
        acc_far[pl.ds(pl.multiple_of(turn * 96, 8), 96), :] = jnp.zeros((96, LANES), jnp.float32)
        return carry

    lax.fori_loop(0, acc_near.shape[0] // 48, clear, 0)

    copy.wait()

    lane = lax.broadcasted_iota(jnp.int32, (2 * CHUNK, LANES), 1)
    column_of = jnp.where(lane < LANES // 2, 0, PARAMS)
    lane_f = (lane & 7).astype(jnp.float32)
    pick_low = lane < 8
    pick_all = lane < 16
    lane24 = lax.broadcasted_iota(jnp.int32, (24, LANES), 1)
    row8 = lax.broadcasted_iota(jnp.int32, (8, LANES), 0)
    lane8 = lax.broadcasted_iota(jnp.int32, (8, LANES), 1)
    row_first = (row8 & 3) == 0
    row_second = (row8 & 3) == 1
    half8 = (row8 < 4) == (lane8 < LANES // 2)
    ones_half = jnp.where(half8, 1.0, 0.0)
    row_sum = lax.broadcasted_iota(jnp.int32, (2 * LANES, 2 * LANES), 0)
    col_sum = lax.broadcasted_iota(jnp.int32, (2 * LANES, 2 * LANES), 1)
    halves = jnp.where(
        ((row_sum & (LANES - 1)) >= LANES // 2) == (col_sum >= LANES), 1.0, 0.0
    ).astype(jnp.bfloat16)
    row16 = lax.broadcasted_iota(jnp.int32, (16, LANES), 0)
    keeps = [jnp.where((row16 & 7) == sub, 1.0, 0.0).astype(jnp.bfloat16) for sub in range(8)]

    def fetch(turn):
        for index in range(CHUNK):
            near = words[turn, index]
            far = words[2 * slot_rows + turn, index]
            gathered[pl.ds(index, 1), :] = table[pl.ds(near, 1), :]
            gathered[pl.ds(CHUNK + index, 1), :] = table[pl.ds(far, 1), :]

    def arrange(first):
        def keep_part(slot, value):
            parts[pl.ds(pl.multiple_of(slot * slots + first, 8), CHUNK), :] = value

        packed = gathered[...]

        def spread(column):
            return jnp.take_along_axis(
                packed, column_of + column, axis=1, mode="promise_in_bounds"
            )

        kind_low = jnp.take_along_axis(
            packed, jnp.where(pick_low, PARAMS - 1, 2 * PARAMS - 1), axis=1, mode="promise_in_bounds"
        )
        pick = jnp.where(pick_all & (kind_low == lane_f), 1.0, 0.0).astype(jnp.bfloat16)
        offsets = jnp.dot(pick, off_ref[...], preferred_element_type=jnp.float32)
        turns = rotation(*[spread(3 + entry) for entry in range(4)])
        where_at = []
        for axis in range(3):
            value = spread(axis)
            for mode in range(3):
                value = value + turns[3 * axis + mode] * offsets[:, mode * LANES : (mode + 1) * LANES]
            where_at.append(value)
        near = [value[:CHUNK] for value in where_at]
        far = [value[CHUNK:] for value in where_at]
        near_sq = near[0] * near[0] + near[1] * near[1] + near[2] * near[2]
        far_sq = far[0] * far[0] + far[1] * far[1] + far[2] * far[2]
        for axis, value in enumerate(near + [REACH_SQUARED - near_sq]):
            for part, piece in enumerate(split3(value)):
                keep_part(4 * part + axis, piece)
        for axis, value in enumerate([2.0 * value for value in far] + [-far_sq]):
            for part, piece in enumerate(split3(value)):
                keep_part(12 + 4 * part + axis, piece)
        for axis in range(3):
            keep_part(24 + axis, far[axis])

    one8 = jnp.ones((8, LANES), jnp.float32)

    def choose(first, second, third):
        return jnp.where(row_first, first, jnp.where(row_second, second, third))

    def prepare(base):
        def part(slot):
            return parts[pl.ds(slot * slots + base, 8), :]

        near = [[part(4 * which + axis) for axis in range(4)] for which in range(3)]
        far = [[part(12 + 4 * which + axis) for axis in range(4)] for which in range(3)]
        rows_a, rows_b = [], []
        for a, b, a_last, b_last in (
            (0, 0, near[0][3], one8),
            (0, 1, one8, far[1][3]),
            (1, 0, near[1][3], one8),
            (1, 1, one8, far[0][3]),
            (0, 2, one8, far[2][3]),
            (2, 0, near[2][3], one8),
        ):
            rows_a += near[a][:3] + [a_last]
            rows_b += far[b][:3] + [b_last]
        all_a = jnp.concatenate(rows_a, 0).astype(jnp.bfloat16)
        tiles_b = [
            jnp.concatenate(rows_b[2 * tile : 2 * tile + 2], 0).astype(jnp.bfloat16)
            for tile in range(12)
        ]
        return all_a, tiles_b

    def reach_of(all_a, tiles_b, pair):
        side_b = jnp.concatenate(
            [jnp.concatenate([tile * keeps[sub] for tile in tiles_b], 0) for sub in pair], 1
        )
        return lax.dot_general(
            all_a, side_b, (((0,), (0,)), ((), ())), preferred_element_type=jnp.float32
        )

    def sums_of(reach, base, pair):
        weight = jnp.maximum(reach, 0.0)
        weight_high = weight.astype(jnp.bfloat16)
        weight_low = (weight - weight_high.astype(jnp.float32)).astype(jnp.bfloat16)
        side_c = []
        for sub in pair:
            for which in range(3):
                row = choose(
                    *[
                        parts[pl.ds((4 * which + axis) * slots + base + sub, 8, stride=0), :]
                        for axis in range(3)
                    ]
                )
                side_c.append(jnp.where(half8, row, 0.0))
            side_c.append(ones_half)
        side_c = jnp.concatenate(side_c, 0).astype(jnp.bfloat16)
        return jnp.dot(
            jnp.concatenate([side_c, side_c], 1),
            jnp.concatenate([weight_high, weight_low], 0),
            preferred_element_type=jnp.float32,
        )

    def terms_of(sums, base, pair):
        terms = []
        for place, sub in enumerate(pair):
            mine = sums[32 * place : 32 * place + 32, LANES * place : LANES * place + LANES]
            axes = [
                parts[pl.ds((24 + axis) * slots + base + sub, 8, stride=0), :] for axis in range(3)
            ]
            force = mine[24:32] * choose(*axes) - (mine[0:8] + mine[8:16] + mine[16:24])
            terms += [
                force,
                force * choose(axes[1], axes[2], axes[0]),
                force * choose(axes[2], axes[0], axes[1]),
            ]
        terms = jnp.concatenate(terms, 0)
        terms_high = terms.astype(jnp.bfloat16)
        terms_low = (terms - terms_high.astype(jnp.float32)).astype(jnp.bfloat16)
        return jnp.concatenate([terms_high, terms_low], 1)

    def scatter(group):
        base = jnp.clip(group, 0, groups - 1) * 8
        row = base // CHUNK
        spot = lax.rem(base, CHUNK)
        for sub in range(8):
            lower = folded_ref[pl.ds(24 * sub, 24), :LANES]
            upper = folded_ref[pl.ds(24 * sub, 24), LANES:]
            live = (group >= 0) & (group * 8 + sub < number)
            block = words[row, spot + sub]
            here = lane24 == jnp.where(live, block & (LANES - 1), -1)
            target = acc_near.at[pl.ds(pl.multiple_of((block >> 7) * 24, 8), 24), :]
            pltpu.store(target, target[...] + (lower + upper), mask=here)
            block = words[2 * slot_rows + row, spot + sub]
            here = lane24 == jnp.where(live, block & (LANES - 1), -1)
            for half, value in enumerate((lower, upper)):
                at = pl.multiple_of((block >> 7) * 48 + 24 * half, 8)
                target = acc_far.at[pl.ds(at, 24), :]
                pltpu.store(target, target[...] + value, mask=here)

    def chunk(turn, carry):
        arrange(pl.multiple_of(turn * CHUNK, CHUNK))
        fetch(jnp.minimum(turn + 1, slots // CHUNK - 1))
        return carry

    fetch(jnp.int32(0))
    lax.fori_loop(0, (number + CHUNK - 1) // CHUNK, chunk, 0)

    groups = (number + 7) // 8
    pairs = [(2 * couple, 2 * couple + 1) for couple in range(4)]

    def octet(turn, slot):
        fresh = 4 * LANES * slot
        stale = 4 * LANES * (1 - slot)
        ready = prepare(pl.multiple_of(jnp.minimum(turn, groups - 1) * 8, 8))
        for couple, pair in enumerate(pairs):
            reach_ref[pl.ds(fresh + LANES * couple, LANES), :] = reach_of(*ready, pair)
        scatter(turn - 3)
        base = jnp.clip(turn - 2, 0, groups - 1) * 8
        terms = [
            terms_of(sums_ref[pl.ds(64 * couple, 64), :], base, pair)
            for couple, pair in enumerate(pairs)
        ]
        folded_ref[...] = jnp.dot(
            jnp.concatenate(terms, 0), halves, preferred_element_type=jnp.float32
        )
        base = jnp.clip(turn - 1, 0, groups - 1) * 8
        for couple, pair in enumerate(pairs):
            sums_ref[pl.ds(64 * couple, 64), :] = sums_of(
                reach_ref[pl.ds(stale + LANES * couple, LANES), :], base, pair
            )

    def octets(turn, carry):
        for sub in range(DEPTH):
            octet(DEPTH * turn + sub, sub % 2)
        return carry

    lax.fori_loop(0, (groups + 2 + DEPTH) // DEPTH, octets, 0)

    def total_of(row, half, tiles, start):
        line = (row // 3) * 8 + row % 3
        mine = acc_near[pl.ds(start * 24 + line + 4 * half, tiles, stride=24), :]
        line += 24 * half
        other = (
            acc_far[pl.ds(start * 48 + line, tiles, stride=48), :]
            + acc_far[pl.ds(start * 48 + line + 4, tiles, stride=48), :]
        )
        return (other - mine) * STIFFNESS

    def results_of(half, tiles, start):
        rows = [total_of(row, half, tiles, start) for row in range(9)]
        return rows[0:3] + [
            rows[6 + (axis + 2) % 3] - rows[3 + (axis + 1) % 3] for axis in range(3)
        ]

    own_tiles = own_blocks // LANES
    own_rows = own_tiles * COMPS
    edges = [results_of(half, 2, inner_blocks // LANES) for half in range(2)]
    for k, out in zip(clique_order(piece_count), outs):
        place = jnp.bitwise_xor(clique, k)
        for side in range(2):
            start = (side * piece_count + place) * own_tiles
            for half in range(2):
                for axis, value in enumerate(results_of(half, own_tiles, start)):
                    at = pl.ds(side * own_rows + 6 * half + axis, own_tiles, stride=COMPS)
                    out[at, :] = value
        out[pl.ds(2 * own_rows, RIM_ROWS), :] = jnp.zeros((RIM_ROWS, LANES), jnp.float32)
        for half in range(2):
            for axis, value in enumerate(edges[half]):
                rim = jnp.where(place == 0, value[1:2], value[0:1])
                rim = jnp.where((place == 0) | (place == piece_count - 1), rim, 0.0)
                out[pl.ds(2 * own_rows + 6 * half + axis, 1), :] = rim


def whole_step(positions, rotations, clump_kind, sub_offsets, pair_blocks, pair_count):
    members = lax.axis_size("dev")
    groups = lax.axis_size("grp")
    me = lax.axis_index("dev")
    rings = members // 2
    clique, far = me % rings, me // rings
    clumps = positions.shape[1]
    slots = pair_blocks.shape[1]
    own_blocks = clumps // 2
    kinds, _, _ = sub_offsets.shape
    vmem = pl.BlockSpec(memory_space=pltpu.VMEM)
    smem = pl.BlockSpec(memory_space=pltpu.SMEM)

    payload, end = pl.pallas_call(
        functools.partial(payload_kernel, slots, members),
        out_shape=(
            jax.ShapeDtypeStruct((ROWS, own_blocks + LANES), jnp.float32),
            jax.ShapeDtypeStruct((ROWS, RIM), jnp.float32),
        ),
        in_specs=[pl.BlockSpec(memory_space=pltpu.HBM)] * 4 + [smem],
        out_specs=(vmem, vmem),
        scratch_shapes=[
            pltpu.VMEM((3, clumps), jnp.float32),
            pltpu.VMEM((9, clumps), jnp.float32),
            pltpu.VMEM((clumps // LANES, LANES), jnp.int32),
            pltpu.VMEM((2, slots), jnp.int32),
            pltpu.SemaphoreType.DMA((4,)),
        ],
        name="payload_kernel",
    )(positions, rotations, clump_kind.reshape(-1, LANES), pair_blocks, pair_count)

    def trade(value, k):
        return lax.ppermute(value, "dev", [(i, i ^ k) for i in range(members)])

    def cross(value, step, flip):
        steps = [
            (
                g * members + d,
                (g + (step if d < rings else -step)) % groups * members + (d ^ flip),
            )
            for g in range(groups)
            for d in range(members)
        ]
        return lax.ppermute(value, ("grp", "dev"), steps)

    far_payload = trade(payload, rings)
    rim_a = cross(end, -1, 0)
    rim_b = cross(end, -1, rings)
    rim = jnp.where((clique == 0) == (far == 0), rim_a, rim_b)
    both = jnp.concatenate([payload, far_payload, rim], 1)
    order = clique_order(rings)
    pieces = [both] + [trade(both, k) for k in order[1:]]

    offset_table = sub_offsets.astype(jnp.float32) * OFFSET_UNIT
    blank = jnp.zeros_like(offset_table)
    offset_rows = jnp.concatenate(
        [
            jnp.concatenate([offset_table, blank], 2).reshape(kinds, -1),
            jnp.concatenate([blank, offset_table], 2).reshape(kinds, -1),
        ],
        0,
    )
    offset_rows = jnp.concatenate(
        [offset_rows, jnp.zeros((LANES - 2 * kinds, offset_rows.shape[1]), jnp.float32)], 0
    ).astype(jnp.bfloat16)

    inner_blocks = own_blocks * members
    tiles = inner_blocks // LANES
    own_rows = own_blocks // LANES * COMPS
    outs = pl.pallas_call(
        functools.partial(pair_kernel, members, slots),
        out_shape=(jax.ShapeDtypeStruct((2 * own_rows + RIM_ROWS, LANES), jnp.float32),) * rings,
        in_specs=[vmem] * (rings + 1),
        out_specs=(vmem,) * rings,
        scratch_shapes=[
            pltpu.VMEM((inner_blocks + 3 * RIM, LANES), jnp.float32),
            pltpu.VMEM((2 * slots // CHUNK, LANES), jnp.int32),
            pltpu.SMEM((2 * slots // CHUNK, LANES), jnp.int32),
            pltpu.VMEM((2 * CHUNK, LANES), jnp.float32),
            pltpu.VMEM((27 * slots, LANES), jnp.float32),
            pltpu.VMEM((8 * LANES, 2 * LANES), jnp.float32),
            pltpu.VMEM((4 * 64, 2 * LANES), jnp.float32),
            pltpu.VMEM((192, 2 * LANES), jnp.float32),
            pltpu.VMEM(((tiles + 2) * 24, LANES), jnp.float32),
            pltpu.VMEM(((tiles + 2) * 48, LANES), jnp.float32),
            pltpu.SemaphoreType.DMA,
        ],
        compiler_params=pltpu.CompilerParams(vmem_limit_bytes=32 << 20),
        name="pair_kernel",
    )(*pieces, offset_rows)

    column = outs[0]
    for k, out in list(zip(order, outs))[:0:-1]:
        column = column + trade(out, k)
    in_low = far == 0
    low, high = column[:own_rows], column[own_rows : 2 * own_rows]
    rim = column[2 * own_rows :]
    other = trade(jnp.where(in_low, high, low), rings)
    rim_a = cross(rim, 1, 0)
    rim_b = cross(rim, -1, rings)
    shares = [jnp.where(in_low, low, high), other, rim_a, rim_b]
    clump_force, clump_torque = pl.pallas_call(
        functools.partial(finish_kernel, members, groups),
        out_shape=(jax.ShapeDtypeStruct((3, clumps), jnp.float32),) * 2,
        in_specs=[vmem] * 5,
        out_specs=(vmem, vmem),
        scratch_shapes=[pltpu.VMEM((own_rows, LANES), jnp.float32)],
        compiler_params=pltpu.CompilerParams(vmem_limit_bytes=4 << 20),
        name="finish_kernel",
    )(*shares, positions)
    return (clump_force, clump_torque)


def solution(mesh):
    placed = (
        P(None, ("grp", "dev")),
        P(None, ("grp", "dev")),
        P(("grp", "dev")),
        P(),
        P(None, ("grp", "dev")),
        P(("grp", "dev")),
    )
    return jax.shard_map(
        whole_step,
        mesh=mesh,
        in_specs=placed,
        out_specs=(P(None, ("grp", "dev")), P(None, ("grp", "dev"))),
        check_vma=False,
    )
```

```python
import functools

import jax
import jax.numpy as jnp
from jax import lax
from jax.experimental import pallas as pl
from jax.experimental.pallas import tpu as pltpu
from jax.sharding import PartitionSpec as P


RIM = 128
LANES = 128
OFFSET_UNIT = 0.125
REACH_SQUARED = 4.0
STIFFNESS = 1.0 / 256.0
CHUNK = 64
COMPS = 12
PARAMS = 8
ROWS = 16
RIM_ROWS = 16
DEPTH = 6


def split3(value):
    high = value.astype(jnp.bfloat16).astype(jnp.float32)
    rest = value - high
    middle = rest.astype(jnp.bfloat16).astype(jnp.float32)
    return high, middle, rest - middle


def quaternion(entries):
    (xx, xy, xz), (yx, yy, yz), (zx, zy, zz) = entries[0:3], entries[3:6], entries[6:9]
    squares = [1.0 + xx + yy + zz, 1.0 + xx - yy - zz, 1.0 - xx + yy - zz, 1.0 - xx - yy + zz]
    forms = [
        [squares[0], zy - yz, xz - zx, yx - xy],
        [zy - yz, squares[1], yx + xy, xz + zx],
        [xz - zx, yx + xy, squares[2], zy + yz],
        [yx - xy, xz + zx, zy + yz, squares[3]],
    ]
    largest, form = squares[0], forms[0]
    for square, other in zip(squares[1:], forms[1:]):
        better = square > largest
        largest = jnp.where(better, square, largest)
        form = [jnp.where(better, new, old) for new, old in zip(other, form)]
    scale = 0.5 / jnp.sqrt(largest)
    return [entry * scale for entry in form]


def rotation(real, first, second, third):
    length = real * real + first * first + second * second + third * third
    double = 4.0 - 2.0 * length
    along = [double * first, double * second, double * third]
    xx, yy, zz = along[0] * first, along[1] * second, along[2] * third
    xy, xz, yz = along[0] * second, along[0] * third, along[1] * third
    wx, wy, wz = along[0] * real, along[1] * real, along[2] * real
    return [
        1.0 - (yy + zz), xy - wz, xz + wy,
        xy + wz, 1.0 - (xx + zz), yz - wx,
        xz - wy, yz + wx, 1.0 - (xx + yy),
    ]


def clique_order(count):
    return list(range(count))


def payload_kernel(slots, members, *refs):
    sources, (count_ref, out_ref, end_ref), landed, sems = refs[:4], refs[4:7], refs[7:11], refs[11]
    copies = [
        pltpu.make_async_copy(source, target, sems.at[turn])
        for turn, (source, target) in enumerate(zip(sources, landed))
    ]
    for copy in copies:
        copy.start()
    for copy in copies:
        copy.wait()
    position_ref, rotation_ref, kind_ref, pair_ref = landed
    clumps = position_ref.shape[1]
    blocks = clumps // 2
    inner_blocks = blocks * members
    wide = 2 * LANES
    row = lax.broadcasted_iota(jnp.int32, (wide, wide), 0)
    column = lax.broadcasted_iota(jnp.int32, (wide, wide), 1)
    source = jnp.where(column < LANES, 2 * column, 2 * column - (wide - 1))
    picked = jnp.where(row == source, 1.0, 0.0).astype(jnp.bfloat16)
    turned = quaternion([rotation_ref[entry : entry + 1, :] for entry in range(9)])
    parts = []
    for turn in range(clumps // wide):
        at = slice(turn * wide, (turn + 1) * wide)
        kinds = kind_ref[2 * turn : 2 * turn + 2, :].astype(jnp.float32)
        value = jnp.concatenate(
            [position_ref[:, at]]
            + [entry[:, at] for entry in turned]
            + [jnp.concatenate([kinds[0:1], kinds[1:2]], 1)],
            0,
        )
        parts += [piece.astype(jnp.bfloat16) for piece in split3(value)]
    sorted_parts = jnp.dot(
        jnp.concatenate(parts, 0), picked, preferred_element_type=jnp.float32
    )
    for turn in range(clumps // wide):
        high, middle, low = (
            sorted_parts[PARAMS * (3 * turn + part) : PARAMS * (3 * turn + part + 1)]
            for part in range(3)
        )
        value = (high + middle) + low
        at = slice(turn * LANES, (turn + 1) * LANES)
        out_ref[0:PARAMS, at] = value[:, :LANES]
        out_ref[PARAMS : 2 * PARAMS, at] = value[:, LANES:]
    pairs = pair_ref[...] - lax.axis_index("grp") * inner_blocks
    pairs = jnp.where(
        pairs < 0,
        pairs + inner_blocks + RIM,
        jnp.where(pairs >= inner_blocks, pairs + RIM, pairs),
    )
    live = lax.broadcasted_iota(jnp.int32, pairs.shape, 1) < count_ref[0]
    pairs = jnp.where(live, pairs, -1).astype(jnp.float32)
    slot_rows = slots // LANES
    for which in range(2):
        for part in range(slot_rows):
            out_ref[pl.ds(which * slot_rows + part, 1), blocks:] = pairs[
                which : which + 1, part * LANES : (part + 1) * LANES
            ]
    in_low = lax.axis_index("dev") < members // 2
    end_ref[...] = jnp.where(in_low, out_ref[:, :RIM], out_ref[:, blocks - RIM : blocks])


def finish_kernel(members, groups, own_ref, *refs):
    other_ref, rim_a_ref, rim_b_ref, position_ref, force_ref, torque_ref, total_ref = refs
    me, group = lax.axis_index("dev"), lax.axis_index("grp")
    total_ref[...] = own_ref[...] + other_ref[...]
    rim = rim_a_ref[0:COMPS] + rim_b_ref[0:COMPS]
    first = (me == 0) & (group > 0)
    final = (me == members - 1) & (group < groups - 1)
    total_ref[0:COMPS] += jnp.where(first, rim, 0.0)
    total_ref[own_ref.shape[0] - COMPS :] += jnp.where(final, rim, 0.0)
    tiles = own_ref.shape[0] // COMPS
    wide = 2 * LANES
    row = lax.broadcasted_iota(jnp.int32, (wide, wide), 0)
    column = lax.broadcasted_iota(jnp.int32, (wide, wide), 1)
    target = jnp.where(row < LANES, 2 * row, 2 * row - (wide - 1))
    placed = jnp.where(column == target, 1.0, 0.0).astype(jnp.bfloat16)
    halves = [
        jnp.concatenate(
            [total_ref[pl.ds(6 * half + comp, tiles, stride=COMPS), :] for comp in range(6)], 0
        )
        for half in range(2)
    ]
    value = jnp.concatenate(halves, 1)
    rows = value.shape[0]
    joined = jnp.dot(
        jnp.concatenate([part.astype(jnp.bfloat16) for part in split3(value)], 0),
        placed,
        preferred_element_type=jnp.float32,
    )
    value = (joined[0:rows] + joined[rows : 2 * rows]) + joined[2 * rows : 3 * rows]
    comps = [value[comp * tiles : (comp + 1) * tiles] for comp in range(6)]
    centre = [
        jnp.concatenate(
            [position_ref[axis : axis + 1, tile * wide : (tile + 1) * wide] for tile in range(tiles)], 0
        )
        for axis in range(3)
    ]
    for axis in range(3):
        after, last = (axis + 1) % 3, (axis + 2) % 3
        torque = comps[3 + axis] - (centre[after] * comps[last] - centre[last] * comps[after])
        for tile in range(tiles):
            at = slice(tile * wide, (tile + 1) * wide)
            force_ref[axis : axis + 1, at] = comps[axis][tile : tile + 1]
            torque_ref[axis : axis + 1, at] = torque[tile : tile + 1]


def pair_kernel(members, slots, *refs):
    piece_count = members // 2
    pieces = refs[:piece_count]
    off_ref = refs[piece_count]
    outs = refs[piece_count + 1 : 2 * piece_count + 1]
    (table, word_ref, words, gathered, parts, reach_ref, sums_ref, folded_ref, acc_near,
     acc_far, sem) = refs[2 * piece_count + 1 :]
    me = lax.axis_index("dev")
    clique = lax.rem(me, piece_count)
    own_columns = (pieces[0].shape[1] - RIM) // 2
    own_blocks = own_columns - LANES
    inner_blocks = members * own_blocks
    slot_rows = slots // LANES

    owners = []
    counts = []
    slot_lists = []
    for k in range(piece_count):
        for side in range(2):
            owners.append(jnp.bitwise_xor(me, clique_order(piece_count)[k] + side * piece_count))
            at = side * own_columns + own_blocks
            both_lists = pieces[k][:, at : at + LANES]
            slot_lists.append((both_lists[0:slot_rows], both_lists[slot_rows : 2 * slot_rows]))
            found = jnp.where(slot_lists[-1][0] >= 0.0, 1.0, 0.0)
            counts.append(jnp.sum(found).astype(jnp.int32))
    starts = []
    total = jnp.int32(0)
    for index in range(members):
        start = jnp.int32(0)
        for other in range(members):
            if other != index:
                start = start + jnp.where(owners[other] < owners[index], counts[other], 0)
        starts.append(start)
        total = total + counts[index]
    begin = (total * me) // members
    finish = (total * (me + 1)) // members
    number = finish - begin

    flat = lax.broadcasted_iota(jnp.int32, (slot_rows, LANES), 0) * LANES
    column = lax.broadcasted_iota(jnp.int32, (slot_rows, LANES), 1)
    flat = flat + column
    near_list = jnp.zeros((slot_rows, LANES), jnp.float32)
    far_list = jnp.zeros((slot_rows, LANES), jnp.float32)
    for index in range(members):
        start = starts[index]
        low = jnp.maximum(start, begin) - begin
        high = jnp.minimum(start + counts[index], finish) - begin
        shift = jnp.bitwise_and(start - begin, slots - 1)
        wanted = (flat >= low) & (flat < high)

        def moved(rows, shift=shift):
            turned = pltpu.roll(rows, shift & (LANES - 1), axis=1)
            same = pltpu.roll(turned, shift >> 7, axis=0)
            following = pltpu.roll(turned, (shift >> 7) + 1, axis=0)
            return jnp.where(column < (shift & (LANES - 1)), following, same)

        near_list = jnp.where(wanted, moved(slot_lists[index][0]), near_list)
        far_list = jnp.where(wanted, moved(slot_lists[index][1]), far_list)
    for start, found in ((0, near_list), (2 * slot_rows, far_list)):
        value = found.astype(jnp.int32)
        word_ref[pl.ds(start, slot_rows, stride=2), :] = value
        word_ref[pl.ds(start + 1, slot_rows, stride=2), :] = pltpu.roll(value, CHUNK, axis=1)
    copy = pltpu.make_async_copy(word_ref, words, sem)
    copy.start()

    for k in range(piece_count):
        for side in range(2):
            base = pl.multiple_of(owners[2 * k + side] * own_blocks, LANES)
            for tile in range(own_blocks // LANES):
                at = side * own_columns + tile * LANES
                table[pl.ds(base + tile * LANES, LANES), 0:ROWS] = pieces[k][:, at : at + LANES].T
        place = jnp.bitwise_xor(clique, clique_order(piece_count)[k])
        base = jnp.where(place == 0, RIM, jnp.where(place == piece_count - 1, 0, 2 * RIM))
        table[pl.ds(pl.multiple_of(inner_blocks + base, RIM), RIM), 0:ROWS] = pieces[k][
            :, 2 * own_columns :
        ].T

    def clear(turn, carry):
        acc_near[pl.ds(pl.multiple_of(turn * 48, 8), 48), :] = jnp.zeros((48, LANES), jnp.float32)
        acc_far[pl.ds(pl.multiple_of(turn * 96, 8), 96), :] = jnp.zeros((96, LANES), jnp.float32)
        return carry

    lax.fori_loop(0, acc_near.shape[0] // 48, clear, 0)

    copy.wait()

    lane = lax.broadcasted_iota(jnp.int32, (2 * CHUNK, LANES), 1)
    column_of = jnp.where(lane < LANES // 2, 0, PARAMS)
    lane_f = (lane & 7).astype(jnp.float32)
    pick_low = lane < 8
    pick_all = lane < 16
    lane24 = lax.broadcasted_iota(jnp.int32, (24, LANES), 1)
    row8 = lax.broadcasted_iota(jnp.int32, (8, LANES), 0)
    lane8 = lax.broadcasted_iota(jnp.int32, (8, LANES), 1)
    row_first = (row8 & 3) == 0
    row_second = (row8 & 3) == 1
    half8 = (row8 < 4) == (lane8 < LANES // 2)
    ones_half = jnp.where(half8, 1.0, 0.0)
    row_sum = lax.broadcasted_iota(jnp.int32, (2 * LANES, 2 * LANES), 0)
    col_sum = lax.broadcasted_iota(jnp.int32, (2 * LANES, 2 * LANES), 1)
    halves = jnp.where(
        ((row_sum & (LANES - 1)) >= LANES // 2) == (col_sum >= LANES), 1.0, 0.0
    ).astype(jnp.bfloat16)
    row16 = lax.broadcasted_iota(jnp.int32, (16, LANES), 0)
    keeps = [jnp.where((row16 & 7) == sub, 1.0, 0.0).astype(jnp.bfloat16) for sub in range(8)]

    def fetch(turn):
        for index in range(CHUNK):
            near = words[turn, index]
            far = words[2 * slot_rows + turn, index]
            gathered[pl.ds(index, 1), :] = table[pl.ds(near, 1), :]
            gathered[pl.ds(CHUNK + index, 1), :] = table[pl.ds(far, 1), :]

    def arrange(first):
        def keep_part(slot, value):
            parts[pl.ds(pl.multiple_of(slot * slots + first, 8), CHUNK), :] = value

        packed = gathered[...]

        def spread(column):
            return jnp.take_along_axis(
                packed, column_of + column, axis=1, mode="promise_in_bounds"
            )

        kind_low = jnp.take_along_axis(
            packed, jnp.where(pick_low, PARAMS - 1, 2 * PARAMS - 1), axis=1, mode="promise_in_bounds"
        )
        pick = jnp.where(pick_all & (kind_low == lane_f), 1.0, 0.0).astype(jnp.bfloat16)
        offsets = jnp.dot(pick, off_ref[...], preferred_element_type=jnp.float32)
        turns = rotation(*[spread(3 + entry) for entry in range(4)])
        where_at = []
        for axis in range(3):
            value = spread(axis)
            for mode in range(3):
                value = value + turns[3 * axis + mode] * offsets[:, mode * LANES : (mode + 1) * LANES]
            where_at.append(value)
        near = [value[:CHUNK] for value in where_at]
        far = [value[CHUNK:] for value in where_at]
        near_sq = near[0] * near[0] + near[1] * near[1] + near[2] * near[2]
        far_sq = far[0] * far[0] + far[1] * far[1] + far[2] * far[2]
        for axis, value in enumerate(near + [REACH_SQUARED - near_sq]):
            for part, piece in enumerate(split3(value)):
                keep_part(4 * part + axis, piece)
        for axis, value in enumerate([2.0 * value for value in far] + [-far_sq]):
            for part, piece in enumerate(split3(value)):
                keep_part(12 + 4 * part + axis, piece)
        for axis in range(3):
            keep_part(24 + axis, far[axis])

    one8 = jnp.ones((8, LANES), jnp.float32)

    def choose(first, second, third):
        return jnp.where(row_first, first, jnp.where(row_second, second, third))

    def prepare(base):
        def part(slot):
            return parts[pl.ds(slot * slots + base, 8), :]

        near = [[part(4 * which + axis) for axis in range(4)] for which in range(3)]
        far = [[part(12 + 4 * which + axis) for axis in range(4)] for which in range(3)]
        rows_a, rows_b = [], []
        for a, b, a_last, b_last in (
            (0, 0, near[0][3], one8),
            (0, 1, one8, far[1][3]),
            (1, 0, near[1][3], one8),
            (1, 1, one8, far[0][3]),
            (0, 2, one8, far[2][3]),
            (2, 0, near[2][3], one8),
        ):
            rows_a += near[a][:3] + [a_last]
            rows_b += far[b][:3] + [b_last]
        all_a = jnp.concatenate(rows_a, 0).astype(jnp.bfloat16)
        tiles_b = [
            jnp.concatenate(rows_b[2 * tile : 2 * tile + 2], 0).astype(jnp.bfloat16)
            for tile in range(12)
        ]
        return all_a, tiles_b

    def reach_of(all_a, tiles_b, pair):
        side_b = jnp.concatenate(
            [jnp.concatenate([tile * keeps[sub] for tile in tiles_b], 0) for sub in pair], 1
        )
        return lax.dot_general(
            all_a, side_b, (((0,), (0,)), ((), ())), preferred_element_type=jnp.float32
        )

    def sums_of(reach, base, pair):
        weight = jnp.maximum(reach, 0.0)
        weight_high = weight.astype(jnp.bfloat16)
        weight_low = (weight - weight_high.astype(jnp.float32)).astype(jnp.bfloat16)
        side_c = []
        for sub in pair:
            for which in range(3):
                row = choose(
                    *[
                        parts[pl.ds((4 * which + axis) * slots + base + sub, 8, stride=0), :]
                        for axis in range(3)
                    ]
                )
                side_c.append(jnp.where(half8, row, 0.0))
            side_c.append(ones_half)
        side_c = jnp.concatenate(side_c, 0).astype(jnp.bfloat16)
        return jnp.dot(
            jnp.concatenate([side_c, side_c], 1),
            jnp.concatenate([weight_high, weight_low], 0),
            preferred_element_type=jnp.float32,
        )

    def terms_of(sums, base, pair):
        terms = []
        for place, sub in enumerate(pair):
            mine = sums[32 * place : 32 * place + 32, LANES * place : LANES * place + LANES]
            axes = [
                parts[pl.ds((24 + axis) * slots + base + sub, 8, stride=0), :] for axis in range(3)
            ]
            force = mine[24:32] * choose(*axes) - (mine[0:8] + mine[8:16] + mine[16:24])
            terms += [
                force,
                force * choose(axes[1], axes[2], axes[0]),
                force * choose(axes[2], axes[0], axes[1]),
            ]
        terms = jnp.concatenate(terms, 0)
        terms_high = terms.astype(jnp.bfloat16)
        terms_low = (terms - terms_high.astype(jnp.float32)).astype(jnp.bfloat16)
        return jnp.concatenate([terms_high, terms_low], 1)

    def scatter(group):
        base = jnp.clip(group, 0, groups - 1) * 8
        row = base // CHUNK
        spot = lax.rem(base, CHUNK)
        for sub in range(8):
            lower = folded_ref[pl.ds(24 * sub, 24), :LANES]
            upper = folded_ref[pl.ds(24 * sub, 24), LANES:]
            live = (group >= 0) & (group * 8 + sub < number)
            block = words[row, spot + sub]
            here = lane24 == jnp.where(live, block & (LANES - 1), -1)
            target = acc_near.at[pl.ds(pl.multiple_of((block >> 7) * 24, 8), 24), :]
            pltpu.store(target, target[...] + (lower + upper), mask=here)
            block = words[2 * slot_rows + row, spot + sub]
            here = lane24 == jnp.where(live, block & (LANES - 1), -1)
            for half, value in enumerate((lower, upper)):
                at = pl.multiple_of((block >> 7) * 48 + 24 * half, 8)
                target = acc_far.at[pl.ds(at, 24), :]
                pltpu.store(target, target[...] + value, mask=here)

    def chunk(turn, carry):
        arrange(pl.multiple_of(turn * CHUNK, CHUNK))
        fetch(jnp.minimum(turn + 1, slots // CHUNK - 1))
        return carry

    fetch(jnp.int32(0))
    lax.fori_loop(0, (number + CHUNK - 1) // CHUNK, chunk, 0)

    groups = (number + 7) // 8
    pairs = [(2 * couple, 2 * couple + 1) for couple in range(4)]

    def octet(turn, slot):
        fresh = 4 * LANES * slot
        stale = 4 * LANES * (1 - slot)
        ready = prepare(pl.multiple_of(jnp.minimum(turn, groups - 1) * 8, 8))
        for couple, pair in enumerate(pairs):
            reach_ref[pl.ds(fresh + LANES * couple, LANES), :] = reach_of(*ready, pair)
        scatter(turn - 3)
        base = jnp.clip(turn - 2, 0, groups - 1) * 8
        terms = [
            terms_of(sums_ref[pl.ds(64 * couple, 64), :], base, pair)
            for couple, pair in enumerate(pairs)
        ]
        folded_ref[...] = jnp.dot(
            jnp.concatenate(terms, 0), halves, preferred_element_type=jnp.float32
        )
        base = jnp.clip(turn - 1, 0, groups - 1) * 8
        for couple, pair in enumerate(pairs):
            sums_ref[pl.ds(64 * couple, 64), :] = sums_of(
                reach_ref[pl.ds(stale + LANES * couple, LANES), :], base, pair
            )

    def octets(depth, start):
        def turn_of(turn, carry):
            for sub in range(depth):
                octet(start + depth * turn + sub, sub % 2)
            return carry

        return turn_of

    turns = groups + 3
    whole = turns // DEPTH
    lax.fori_loop(0, whole, octets(DEPTH, 0), 0)
    lax.fori_loop(0, (turns - whole * DEPTH + 1) // 2, octets(2, whole * DEPTH), 0)

    def total_of(row, half, tiles, start):
        line = (row // 3) * 8 + row % 3
        mine = acc_near[pl.ds(start * 24 + line + 4 * half, tiles, stride=24), :]
        line += 24 * half
        other = (
            acc_far[pl.ds(start * 48 + line, tiles, stride=48), :]
            + acc_far[pl.ds(start * 48 + line + 4, tiles, stride=48), :]
        )
        return (other - mine) * STIFFNESS

    def results_of(half, tiles, start):
        rows = [total_of(row, half, tiles, start) for row in range(9)]
        return rows[0:3] + [
            rows[6 + (axis + 2) % 3] - rows[3 + (axis + 1) % 3] for axis in range(3)
        ]

    own_tiles = own_blocks // LANES
    own_rows = own_tiles * COMPS
    edges = [results_of(half, 2, inner_blocks // LANES) for half in range(2)]
    for k, out in zip(clique_order(piece_count), outs):
        place = jnp.bitwise_xor(clique, k)
        for side in range(2):
            start = (side * piece_count + place) * own_tiles
            for half in range(2):
                for axis, value in enumerate(results_of(half, own_tiles, start)):
                    at = pl.ds(side * own_rows + 6 * half + axis, own_tiles, stride=COMPS)
                    out[at, :] = value
        out[pl.ds(2 * own_rows, RIM_ROWS), :] = jnp.zeros((RIM_ROWS, LANES), jnp.float32)
        for half in range(2):
            for axis, value in enumerate(edges[half]):
                rim = jnp.where(place == 0, value[1:2], value[0:1])
                rim = jnp.where((place == 0) | (place == piece_count - 1), rim, 0.0)
                out[pl.ds(2 * own_rows + 6 * half + axis, 1), :] = rim


def whole_step(positions, rotations, clump_kind, sub_offsets, pair_blocks, pair_count):
    members = lax.axis_size("dev")
    groups = lax.axis_size("grp")
    me = lax.axis_index("dev")
    rings = members // 2
    clique, far = me % rings, me // rings
    clumps = positions.shape[1]
    slots = pair_blocks.shape[1]
    own_blocks = clumps // 2
    kinds, _, _ = sub_offsets.shape
    vmem = pl.BlockSpec(memory_space=pltpu.VMEM)
    smem = pl.BlockSpec(memory_space=pltpu.SMEM)

    payload, end = pl.pallas_call(
        functools.partial(payload_kernel, slots, members),
        out_shape=(
            jax.ShapeDtypeStruct((ROWS, own_blocks + LANES), jnp.float32),
            jax.ShapeDtypeStruct((ROWS, RIM), jnp.float32),
        ),
        in_specs=[pl.BlockSpec(memory_space=pltpu.HBM)] * 4 + [smem],
        out_specs=(vmem, vmem),
        scratch_shapes=[
            pltpu.VMEM((3, clumps), jnp.float32),
            pltpu.VMEM((9, clumps), jnp.float32),
            pltpu.VMEM((clumps // LANES, LANES), jnp.int32),
            pltpu.VMEM((2, slots), jnp.int32),
            pltpu.SemaphoreType.DMA((4,)),
        ],
        name="payload_kernel",
    )(positions, rotations, clump_kind.reshape(-1, LANES), pair_blocks, pair_count)

    def trade(value, k):
        return lax.ppermute(value, "dev", [(i, i ^ k) for i in range(members)])

    def cross(value, step, flip):
        steps = [
            (
                g * members + d,
                (g + (step if d < rings else -step)) % groups * members + (d ^ flip),
            )
            for g in range(groups)
            for d in range(members)
        ]
        return lax.ppermute(value, ("grp", "dev"), steps)

    far_payload = trade(payload, rings)
    rim_a = cross(end, -1, 0)
    rim_b = cross(end, -1, rings)
    rim = jnp.where((clique == 0) == (far == 0), rim_a, rim_b)
    both = jnp.concatenate([payload, far_payload, rim], 1)
    order = clique_order(rings)
    pieces = [both] + [trade(both, k) for k in order[1:]]

    offset_table = sub_offsets.astype(jnp.float32) * OFFSET_UNIT
    blank = jnp.zeros_like(offset_table)
    offset_rows = jnp.concatenate(
        [
            jnp.concatenate([offset_table, blank], 2).reshape(kinds, -1),
            jnp.concatenate([blank, offset_table], 2).reshape(kinds, -1),
        ],
        0,
    )
    offset_rows = jnp.concatenate(
        [offset_rows, jnp.zeros((LANES - 2 * kinds, offset_rows.shape[1]), jnp.float32)], 0
    ).astype(jnp.bfloat16)

    inner_blocks = own_blocks * members
    tiles = inner_blocks // LANES
    own_rows = own_blocks // LANES * COMPS
    outs = pl.pallas_call(
        functools.partial(pair_kernel, members, slots),
        out_shape=(jax.ShapeDtypeStruct((2 * own_rows + RIM_ROWS, LANES), jnp.float32),) * rings,
        in_specs=[vmem] * (rings + 1),
        out_specs=(vmem,) * rings,
        scratch_shapes=[
            pltpu.VMEM((inner_blocks + 3 * RIM, LANES), jnp.float32),
            pltpu.VMEM((2 * slots // CHUNK, LANES), jnp.int32),
            pltpu.SMEM((2 * slots // CHUNK, LANES), jnp.int32),
            pltpu.VMEM((2 * CHUNK, LANES), jnp.float32),
            pltpu.VMEM((27 * slots, LANES), jnp.float32),
            pltpu.VMEM((8 * LANES, 2 * LANES), jnp.float32),
            pltpu.VMEM((4 * 64, 2 * LANES), jnp.float32),
            pltpu.VMEM((192, 2 * LANES), jnp.float32),
            pltpu.VMEM(((tiles + 2) * 24, LANES), jnp.float32),
            pltpu.VMEM(((tiles + 2) * 48, LANES), jnp.float32),
            pltpu.SemaphoreType.DMA,
        ],
        compiler_params=pltpu.CompilerParams(vmem_limit_bytes=32 << 20),
        name="pair_kernel",
    )(*pieces, offset_rows)

    column = outs[0]
    for k, out in list(zip(order, outs))[:0:-1]:
        column = column + trade(out, k)
    in_low = far == 0
    low, high = column[:own_rows], column[own_rows : 2 * own_rows]
    rim = column[2 * own_rows :]
    other = trade(jnp.where(in_low, high, low), rings)
    rim_a = cross(rim, 1, 0)
    rim_b = cross(rim, -1, rings)
    shares = [jnp.where(in_low, low, high), other, rim_a, rim_b]
    clump_force, clump_torque = pl.pallas_call(
        functools.partial(finish_kernel, members, groups),
        out_shape=(jax.ShapeDtypeStruct((3, clumps), jnp.float32),) * 2,
        in_specs=[vmem] * 5,
        out_specs=(vmem, vmem),
        scratch_shapes=[pltpu.VMEM((own_rows, LANES), jnp.float32)],
        compiler_params=pltpu.CompilerParams(vmem_limit_bytes=4 << 20),
        name="finish_kernel",
    )(*shares, positions)
    return (clump_force, clump_torque)


def solution(mesh):
    placed = (
        P(None, ("grp", "dev")),
        P(None, ("grp", "dev")),
        P(("grp", "dev")),
        P(),
        P(None, ("grp", "dev")),
        P(("grp", "dev")),
    )
    return jax.shard_map(
        whole_step,
        mesh=mesh,
        in_specs=placed,
        out_specs=(P(None, ("grp", "dev")), P(None, ("grp", "dev"))),
        check_vma=False,
    )
```

```python
import functools

import jax
import jax.numpy as jnp
from jax import lax
from jax.experimental import pallas as pl
from jax.experimental.pallas import tpu as pltpu
from jax.sharding import PartitionSpec as P


RIM = 128
LANES = 128
OFFSET_UNIT = 0.125
REACH_SQUARED = 4.0
STIFFNESS = 1.0 / 256.0
CHUNK = 64
COMPS = 12
PARAMS = 8
ROWS = 16
RIM_ROWS = 16
DEPTH = 8


def split3(value):
    high = value.astype(jnp.bfloat16).astype(jnp.float32)
    rest = value - high
    middle = rest.astype(jnp.bfloat16).astype(jnp.float32)
    return high, middle, rest - middle


def quaternion(entries):
    (xx, xy, xz), (yx, yy, yz), (zx, zy, zz) = entries[0:3], entries[3:6], entries[6:9]
    squares = [1.0 + xx + yy + zz, 1.0 + xx - yy - zz, 1.0 - xx + yy - zz, 1.0 - xx - yy + zz]
    forms = [
        [squares[0], zy - yz, xz - zx, yx - xy],
        [zy - yz, squares[1], yx + xy, xz + zx],
        [xz - zx, yx + xy, squares[2], zy + yz],
        [yx - xy, xz + zx, zy + yz, squares[3]],
    ]
    largest, form = squares[0], forms[0]
    for square, other in zip(squares[1:], forms[1:]):
        better = square > largest
        largest = jnp.where(better, square, largest)
        form = [jnp.where(better, new, old) for new, old in zip(other, form)]
    scale = 0.5 / jnp.sqrt(largest)
    return [entry * scale for entry in form]


def rotation(real, first, second, third):
    length = real * real + first * first + second * second + third * third
    double = 4.0 - 2.0 * length
    along = [double * first, double * second, double * third]
    xx, yy, zz = along[0] * first, along[1] * second, along[2] * third
    xy, xz, yz = along[0] * second, along[0] * third, along[1] * third
    wx, wy, wz = along[0] * real, along[1] * real, along[2] * real
    return [
        1.0 - (yy + zz), xy - wz, xz + wy,
        xy + wz, 1.0 - (xx + zz), yz - wx,
        xz - wy, yz + wx, 1.0 - (xx + yy),
    ]


def clique_order(count):
    return list(range(count))


def payload_kernel(slots, members, *refs):
    sources, (count_ref, out_ref, end_ref), landed, sems = refs[:4], refs[4:7], refs[7:11], refs[11]
    copies = [
        pltpu.make_async_copy(source, target, sems.at[turn])
        for turn, (source, target) in enumerate(zip(sources, landed))
    ]
    for copy in copies:
        copy.start()
    for copy in copies:
        copy.wait()
    position_ref, rotation_ref, kind_ref, pair_ref = landed
    clumps = position_ref.shape[1]
    blocks = clumps // 2
    inner_blocks = blocks * members
    wide = 2 * LANES
    row = lax.broadcasted_iota(jnp.int32, (wide, wide), 0)
    column = lax.broadcasted_iota(jnp.int32, (wide, wide), 1)
    source = jnp.where(column < LANES, 2 * column, 2 * column - (wide - 1))
    picked = jnp.where(row == source, 1.0, 0.0).astype(jnp.bfloat16)
    turned = quaternion([rotation_ref[entry : entry + 1, :] for entry in range(9)])
    parts = []
    for turn in range(clumps // wide):
        at = slice(turn * wide, (turn + 1) * wide)
        kinds = kind_ref[2 * turn : 2 * turn + 2, :].astype(jnp.float32)
        value = jnp.concatenate(
            [position_ref[:, at]]
            + [entry[:, at] for entry in turned]
            + [jnp.concatenate([kinds[0:1], kinds[1:2]], 1)],
            0,
        )
        parts += [piece.astype(jnp.bfloat16) for piece in split3(value)]
    sorted_parts = jnp.dot(
        jnp.concatenate(parts, 0), picked, preferred_element_type=jnp.float32
    )
    for turn in range(clumps // wide):
        high, middle, low = (
            sorted_parts[PARAMS * (3 * turn + part) : PARAMS * (3 * turn + part + 1)]
            for part in range(3)
        )
        value = (high + middle) + low
        at = slice(turn * LANES, (turn + 1) * LANES)
        out_ref[0:PARAMS, at] = value[:, :LANES]
        out_ref[PARAMS : 2 * PARAMS, at] = value[:, LANES:]
    pairs = pair_ref[...] - lax.axis_index("grp") * inner_blocks
    pairs = jnp.where(
        pairs < 0,
        pairs + inner_blocks + RIM,
        jnp.where(pairs >= inner_blocks, pairs + RIM, pairs),
    )
    live = lax.broadcasted_iota(jnp.int32, pairs.shape, 1) < count_ref[0]
    pairs = jnp.where(live, pairs, -1).astype(jnp.float32)
    slot_rows = slots // LANES
    for which in range(2):
        for part in range(slot_rows):
            out_ref[pl.ds(which * slot_rows + part, 1), blocks:] = pairs[
                which : which + 1, part * LANES : (part + 1) * LANES
            ]
    in_low = lax.axis_index("dev") < members // 2
    end_ref[...] = jnp.where(in_low, out_ref[:, :RIM], out_ref[:, blocks - RIM : blocks])


def finish_kernel(members, groups, own_ref, *refs):
    other_ref, rim_a_ref, rim_b_ref, position_ref, force_ref, torque_ref, total_ref = refs
    me, group = lax.axis_index("dev"), lax.axis_index("grp")
    total_ref[...] = own_ref[...] + other_ref[...]
    rim = rim_a_ref[0:COMPS] + rim_b_ref[0:COMPS]
    first = (me == 0) & (group > 0)
    final = (me == members - 1) & (group < groups - 1)
    total_ref[0:COMPS] += jnp.where(first, rim, 0.0)
    total_ref[own_ref.shape[0] - COMPS :] += jnp.where(final, rim, 0.0)
    tiles = own_ref.shape[0] // COMPS
    wide = 2 * LANES
    row = lax.broadcasted_iota(jnp.int32, (wide, wide), 0)
    column = lax.broadcasted_iota(jnp.int32, (wide, wide), 1)
    target = jnp.where(row < LANES, 2 * row, 2 * row - (wide - 1))
    placed = jnp.where(column == target, 1.0, 0.0).astype(jnp.bfloat16)
    halves = [
        jnp.concatenate(
            [total_ref[pl.ds(6 * half + comp, tiles, stride=COMPS), :] for comp in range(6)], 0
        )
        for half in range(2)
    ]
    value = jnp.concatenate(halves, 1)
    rows = value.shape[0]
    joined = jnp.dot(
        jnp.concatenate([part.astype(jnp.bfloat16) for part in split3(value)], 0),
        placed,
        preferred_element_type=jnp.float32,
    )
    value = (joined[0:rows] + joined[rows : 2 * rows]) + joined[2 * rows : 3 * rows]
    comps = [value[comp * tiles : (comp + 1) * tiles] for comp in range(6)]
    centre = [
        jnp.concatenate(
            [position_ref[axis : axis + 1, tile * wide : (tile + 1) * wide] for tile in range(tiles)], 0
        )
        for axis in range(3)
    ]
    for axis in range(3):
        after, last = (axis + 1) % 3, (axis + 2) % 3
        torque = comps[3 + axis] - (centre[after] * comps[last] - centre[last] * comps[after])
        for tile in range(tiles):
            at = slice(tile * wide, (tile + 1) * wide)
            force_ref[axis : axis + 1, at] = comps[axis][tile : tile + 1]
            torque_ref[axis : axis + 1, at] = torque[tile : tile + 1]


def pair_kernel(members, slots, *refs):
    piece_count = members // 2
    pieces = refs[:piece_count]
    off_ref = refs[piece_count]
    outs = refs[piece_count + 1 : 2 * piece_count + 1]
    (table, word_ref, words, gathered, parts, reach_ref, sums_ref, folded_ref, acc_near,
     acc_far, sem) = refs[2 * piece_count + 1 :]
    me = lax.axis_index("dev")
    clique = lax.rem(me, piece_count)
    own_columns = (pieces[0].shape[1] - RIM) // 2
    own_blocks = own_columns - LANES
    inner_blocks = members * own_blocks
    slot_rows = slots // LANES

    owners = []
    counts = []
    slot_lists = []
    for k in range(piece_count):
        for side in range(2):
            owners.append(jnp.bitwise_xor(me, clique_order(piece_count)[k] + side * piece_count))
            at = side * own_columns + own_blocks
            both_lists = pieces[k][:, at : at + LANES]
            slot_lists.append((both_lists[0:slot_rows], both_lists[slot_rows : 2 * slot_rows]))
            found = jnp.where(slot_lists[-1][0] >= 0.0, 1.0, 0.0)
            counts.append(jnp.sum(found).astype(jnp.int32))
    starts = []
    total = jnp.int32(0)
    for index in range(members):
        start = jnp.int32(0)
        for other in range(members):
            if other != index:
                start = start + jnp.where(owners[other] < owners[index], counts[other], 0)
        starts.append(start)
        total = total + counts[index]
    begin = (total * me) // members
    finish = (total * (me + 1)) // members
    number = finish - begin

    flat = lax.broadcasted_iota(jnp.int32, (slot_rows, LANES), 0) * LANES
    column = lax.broadcasted_iota(jnp.int32, (slot_rows, LANES), 1)
    flat = flat + column
    near_list = jnp.zeros((slot_rows, LANES), jnp.float32)
    far_list = jnp.zeros((slot_rows, LANES), jnp.float32)
    for index in range(members):
        start = starts[index]
        low = jnp.maximum(start, begin) - begin
        high = jnp.minimum(start + counts[index], finish) - begin
        shift = jnp.bitwise_and(start - begin, slots - 1)
        wanted = (flat >= low) & (flat < high)

        def moved(rows, shift=shift):
            turned = pltpu.roll(rows, shift & (LANES - 1), axis=1)
            same = pltpu.roll(turned, shift >> 7, axis=0)
            following = pltpu.roll(turned, ((shift >> 7) + 1) & (slot_rows - 1), axis=0)
            return jnp.where(column < (shift & (LANES - 1)), following, same)

        near_list = jnp.where(wanted, moved(slot_lists[index][0]), near_list)
        far_list = jnp.where(wanted, moved(slot_lists[index][1]), far_list)
    for start, found in ((0, near_list), (2 * slot_rows, far_list)):
        value = found.astype(jnp.int32)
        word_ref[pl.ds(start, slot_rows, stride=2), :] = value
        word_ref[pl.ds(start + 1, slot_rows, stride=2), :] = pltpu.roll(value, CHUNK, axis=1)
    copy = pltpu.make_async_copy(word_ref, words, sem)
    copy.start()

    for k in range(piece_count):
        for side in range(2):
            base = pl.multiple_of(owners[2 * k + side] * own_blocks, LANES)
            for tile in range(own_blocks // LANES):
                at = side * own_columns + tile * LANES
                table[pl.ds(base + tile * LANES, LANES), 0:ROWS] = pieces[k][:, at : at + LANES].T
        place = jnp.bitwise_xor(clique, clique_order(piece_count)[k])
        base = jnp.where(place == 0, RIM, jnp.where(place == piece_count - 1, 0, 2 * RIM))
        table[pl.ds(pl.multiple_of(inner_blocks + base, RIM), RIM), 0:ROWS] = pieces[k][
            :, 2 * own_columns :
        ].T

    def clear(turn, carry):
        acc_near[pl.ds(pl.multiple_of(turn * 48, 8), 48), :] = jnp.zeros((48, LANES), jnp.float32)
        acc_far[pl.ds(pl.multiple_of(turn * 96, 8), 96), :] = jnp.zeros((96, LANES), jnp.float32)
        return carry

    lax.fori_loop(0, acc_near.shape[0] // 48, clear, 0)

    copy.wait()

    lane = lax.broadcasted_iota(jnp.int32, (2 * CHUNK, LANES), 1)
    column_of = jnp.where(lane < LANES // 2, 0, PARAMS)
    lane_f = (lane & 7).astype(jnp.float32)
    pick_low = lane < 8
    pick_all = lane < 16
    lane24 = lax.broadcasted_iota(jnp.int32, (24, LANES), 1)
    row8 = lax.broadcasted_iota(jnp.int32, (8, LANES), 0)
    lane8 = lax.broadcasted_iota(jnp.int32, (8, LANES), 1)
    row_first = (row8 & 3) == 0
    row_second = (row8 & 3) == 1
    half8 = (row8 < 4) == (lane8 < LANES // 2)
    ones_half = jnp.where(half8, 1.0, 0.0)
    row_sum = lax.broadcasted_iota(jnp.int32, (2 * LANES, 2 * LANES), 0)
    col_sum = lax.broadcasted_iota(jnp.int32, (2 * LANES, 2 * LANES), 1)
    halves = jnp.where(
        ((row_sum & (LANES - 1)) >= LANES // 2) == (col_sum >= LANES), 1.0, 0.0
    ).astype(jnp.bfloat16)
    row16 = lax.broadcasted_iota(jnp.int32, (16, LANES), 0)
    keeps = [jnp.where((row16 & 7) == sub, 1.0, 0.0).astype(jnp.bfloat16) for sub in range(8)]

    def fetch(turn):
        for index in range(CHUNK):
            near = words[turn, index]
            far = words[2 * slot_rows + turn, index]
            gathered[pl.ds(index, 1), :] = table[pl.ds(near, 1), :]
            gathered[pl.ds(CHUNK + index, 1), :] = table[pl.ds(far, 1), :]

    def arrange(first):
        def keep_part(slot, value):
            parts[pl.ds(pl.multiple_of(slot * slots + first, 8), CHUNK), :] = value

        packed = gathered[...]

        def spread(column):
            return jnp.take_along_axis(
                packed, column_of + column, axis=1, mode="promise_in_bounds"
            )

        kind_low = jnp.take_along_axis(
            packed, jnp.where(pick_low, PARAMS - 1, 2 * PARAMS - 1), axis=1, mode="promise_in_bounds"
        )
        pick = jnp.where(pick_all & (kind_low == lane_f), 1.0, 0.0).astype(jnp.bfloat16)
        offsets = jnp.dot(pick, off_ref[...], preferred_element_type=jnp.float32)
        turns = rotation(*[spread(3 + entry) for entry in range(4)])
        where_at = []
        for axis in range(3):
            value = spread(axis)
            for mode in range(3):
                value = value + turns[3 * axis + mode] * offsets[:, mode * LANES : (mode + 1) * LANES]
            where_at.append(value)
        near = [value[:CHUNK] for value in where_at]
        far = [value[CHUNK:] for value in where_at]
        near_sq = near[0] * near[0] + near[1] * near[1] + near[2] * near[2]
        far_sq = far[0] * far[0] + far[1] * far[1] + far[2] * far[2]
        for axis, value in enumerate(near + [REACH_SQUARED - near_sq]):
            for part, piece in enumerate(split3(value)):
                keep_part(4 * part + axis, piece)
        for axis, value in enumerate([2.0 * value for value in far] + [-far_sq]):
            for part, piece in enumerate(split3(value)):
                keep_part(12 + 4 * part + axis, piece)
        for axis in range(3):
            keep_part(24 + axis, far[axis])

    one8 = jnp.ones((8, LANES), jnp.float32)

    def choose(first, second, third):
        return jnp.where(row_first, first, jnp.where(row_second, second, third))

    def prepare(base):
        def part(slot):
            return parts[pl.ds(slot * slots + base, 8), :]

        near = [[part(4 * which + axis) for axis in range(4)] for which in range(3)]
        far = [[part(12 + 4 * which + axis) for axis in range(4)] for which in range(3)]
        rows_a, rows_b = [], []
        for a, b, a_last, b_last in (
            (0, 0, near[0][3], one8),
            (0, 1, one8, far[1][3]),
            (1, 0, near[1][3], one8),
            (1, 1, one8, far[0][3]),
            (0, 2, one8, far[2][3]),
            (2, 0, near[2][3], one8),
        ):
            rows_a += near[a][:3] + [a_last]
            rows_b += far[b][:3] + [b_last]
        all_a = jnp.concatenate(rows_a, 0).astype(jnp.bfloat16)
        tiles_b = [
            jnp.concatenate(rows_b[2 * tile : 2 * tile + 2], 0).astype(jnp.bfloat16)
            for tile in range(12)
        ]
        return all_a, tiles_b

    def reach_of(all_a, tiles_b, pair):
        side_b = jnp.concatenate(
            [jnp.concatenate([tile * keeps[sub] for tile in tiles_b], 0) for sub in pair], 1
        )
        return lax.dot_general(
            all_a, side_b, (((0,), (0,)), ((), ())), preferred_element_type=jnp.float32
        )

    def sums_of(reach, base, pair):
        weight = jnp.maximum(reach, 0.0)
        weight_high = weight.astype(jnp.bfloat16)
        weight_low = (weight - weight_high.astype(jnp.float32)).astype(jnp.bfloat16)
        side_c = []
        for sub in pair:
            for which in range(3):
                row = choose(
                    *[
                        parts[pl.ds((4 * which + axis) * slots + base + sub, 8, stride=0), :]
                        for axis in range(3)
                    ]
                )
                side_c.append(jnp.where(half8, row, 0.0))
            side_c.append(ones_half)
        side_c = jnp.concatenate(side_c, 0).astype(jnp.bfloat16)
        return jnp.dot(
            jnp.concatenate([side_c, side_c], 1),
            jnp.concatenate([weight_high, weight_low], 0),
            preferred_element_type=jnp.float32,
        )

    def terms_of(sums, base, pair):
        terms = []
        for place, sub in enumerate(pair):
            mine = sums[32 * place : 32 * place + 32, LANES * place : LANES * place + LANES]
            axes = [
                parts[pl.ds((24 + axis) * slots + base + sub, 8, stride=0), :] for axis in range(3)
            ]
            force = mine[24:32] * choose(*axes) - (mine[0:8] + mine[8:16] + mine[16:24])
            terms += [
                force,
                force * choose(axes[1], axes[2], axes[0]),
                force * choose(axes[2], axes[0], axes[1]),
            ]
        terms = jnp.concatenate(terms, 0)
        terms_high = terms.astype(jnp.bfloat16)
        terms_low = (terms - terms_high.astype(jnp.float32)).astype(jnp.bfloat16)
        return jnp.concatenate([terms_high, terms_low], 1)

    def scatter(group):
        base = jnp.clip(group, 0, groups - 1) * 8
        row = base // CHUNK
        spot = lax.rem(base, CHUNK)
        for sub in range(8):
            lower = folded_ref[pl.ds(24 * sub, 24), :LANES]
            upper = folded_ref[pl.ds(24 * sub, 24), LANES:]
            live = (group >= 0) & (group * 8 + sub < number)
            block = words[row, spot + sub]
            here = lane24 == jnp.where(live, block & (LANES - 1), -1)
            target = acc_near.at[pl.ds(pl.multiple_of((block >> 7) * 24, 8), 24), :]
            pltpu.store(target, target[...] + (lower + upper), mask=here)
            block = words[2 * slot_rows + row, spot + sub]
            here = lane24 == jnp.where(live, block & (LANES - 1), -1)
            for half, value in enumerate((lower, upper)):
                at = pl.multiple_of((block >> 7) * 48 + 24 * half, 8)
                target = acc_far.at[pl.ds(at, 24), :]
                pltpu.store(target, target[...] + value, mask=here)

    def chunk(turn, carry):
        arrange(pl.multiple_of(turn * CHUNK, CHUNK))
        fetch(jnp.minimum(turn + 1, slots // CHUNK - 1))
        return carry

    fetch(jnp.int32(0))
    lax.fori_loop(0, (number + CHUNK - 1) // CHUNK, chunk, 0)

    groups = (number + 7) // 8
    pairs = [(2 * couple, 2 * couple + 1) for couple in range(4)]

    def octet(turn, slot):
        fresh = 4 * LANES * slot
        stale = 4 * LANES * (1 - slot)
        ready = prepare(pl.multiple_of(jnp.minimum(turn, groups - 1) * 8, 8))
        for couple, pair in enumerate(pairs):
            reach_ref[pl.ds(fresh + LANES * couple, LANES), :] = reach_of(*ready, pair)
        scatter(turn - 3)
        base = jnp.clip(turn - 2, 0, groups - 1) * 8
        terms = [
            terms_of(sums_ref[pl.ds(64 * couple, 64), :], base, pair)
            for couple, pair in enumerate(pairs)
        ]
        folded_ref[...] = jnp.dot(
            jnp.concatenate(terms, 0), halves, preferred_element_type=jnp.float32
        )
        base = jnp.clip(turn - 1, 0, groups - 1) * 8
        for couple, pair in enumerate(pairs):
            sums_ref[pl.ds(64 * couple, 64), :] = sums_of(
                reach_ref[pl.ds(stale + LANES * couple, LANES), :], base, pair
            )

    def octets(depth, start):
        def turn_of(turn, carry):
            for sub in range(depth):
                octet(start + depth * turn + sub, sub % 2)
            return carry

        return turn_of

    turns = groups + 3
    whole = turns // DEPTH
    lax.fori_loop(0, whole, octets(DEPTH, 0), 0)
    lax.fori_loop(0, (turns - whole * DEPTH + 1) // 2, octets(2, whole * DEPTH), 0)

    def total_of(row, half, tiles, start):
        line = (row // 3) * 8 + row % 3
        mine = acc_near[pl.ds(start * 24 + line + 4 * half, tiles, stride=24), :]
        line += 24 * half
        other = (
            acc_far[pl.ds(start * 48 + line, tiles, stride=48), :]
            + acc_far[pl.ds(start * 48 + line + 4, tiles, stride=48), :]
        )
        return (other - mine) * STIFFNESS

    def results_of(half, tiles, start):
        rows = [total_of(row, half, tiles, start) for row in range(9)]
        return rows[0:3] + [
            rows[6 + (axis + 2) % 3] - rows[3 + (axis + 1) % 3] for axis in range(3)
        ]

    own_tiles = own_blocks // LANES
    own_rows = own_tiles * COMPS
    edges = [results_of(half, 2, inner_blocks // LANES) for half in range(2)]
    for k, out in zip(clique_order(piece_count), outs):
        place = jnp.bitwise_xor(clique, k)
        for side in range(2):
            start = (side * piece_count + place) * own_tiles
            for half in range(2):
                for axis, value in enumerate(results_of(half, own_tiles, start)):
                    at = pl.ds(side * own_rows + 6 * half + axis, own_tiles, stride=COMPS)
                    out[at, :] = value
        out[pl.ds(2 * own_rows, RIM_ROWS), :] = jnp.zeros((RIM_ROWS, LANES), jnp.float32)
        for half in range(2):
            for axis, value in enumerate(edges[half]):
                rim = jnp.where(place == 0, value[1:2], value[0:1])
                rim = jnp.where((place == 0) | (place == piece_count - 1), rim, 0.0)
                out[pl.ds(2 * own_rows + 6 * half + axis, 1), :] = rim


def whole_step(positions, rotations, clump_kind, sub_offsets, pair_blocks, pair_count):
    members = lax.axis_size("dev")
    groups = lax.axis_size("grp")
    me = lax.axis_index("dev")
    rings = members // 2
    clique, far = me % rings, me // rings
    clumps = positions.shape[1]
    slots = pair_blocks.shape[1]
    own_blocks = clumps // 2
    kinds, _, _ = sub_offsets.shape
    vmem = pl.BlockSpec(memory_space=pltpu.VMEM)
    smem = pl.BlockSpec(memory_space=pltpu.SMEM)

    payload, end = pl.pallas_call(
        functools.partial(payload_kernel, slots, members),
        out_shape=(
            jax.ShapeDtypeStruct((ROWS, own_blocks + LANES), jnp.float32),
            jax.ShapeDtypeStruct((ROWS, RIM), jnp.float32),
        ),
        in_specs=[pl.BlockSpec(memory_space=pltpu.HBM)] * 4 + [smem],
        out_specs=(vmem, vmem),
        scratch_shapes=[
            pltpu.VMEM((3, clumps), jnp.float32),
            pltpu.VMEM((9, clumps), jnp.float32),
            pltpu.VMEM((clumps // LANES, LANES), jnp.int32),
            pltpu.VMEM((2, slots), jnp.int32),
            pltpu.SemaphoreType.DMA((4,)),
        ],
        name="payload_kernel",
    )(positions, rotations, clump_kind.reshape(-1, LANES), pair_blocks, pair_count)

    def trade(value, k):
        return lax.ppermute(value, "dev", [(i, i ^ k) for i in range(members)])

    def cross(value, step, flip):
        steps = [
            (
                g * members + d,
                (g + (step if d < rings else -step)) % groups * members + (d ^ flip),
            )
            for g in range(groups)
            for d in range(members)
        ]
        return lax.ppermute(value, ("grp", "dev"), steps)

    far_payload = trade(payload, rings)
    rim_a = cross(end, -1, 0)
    rim_b = cross(end, -1, rings)
    rim = jnp.where((clique == 0) == (far == 0), rim_a, rim_b)
    both = jnp.concatenate([payload, far_payload, rim], 1)
    order = clique_order(rings)
    pieces = [both] + [trade(both, k) for k in order[1:]]

    offset_table = sub_offsets.astype(jnp.float32) * OFFSET_UNIT
    blank = jnp.zeros_like(offset_table)
    offset_rows = jnp.concatenate(
        [
            jnp.concatenate([offset_table, blank], 2).reshape(kinds, -1),
            jnp.concatenate([blank, offset_table], 2).reshape(kinds, -1),
        ],
        0,
    )
    offset_rows = jnp.concatenate(
        [offset_rows, jnp.zeros((LANES - 2 * kinds, offset_rows.shape[1]), jnp.float32)], 0
    ).astype(jnp.bfloat16)

    inner_blocks = own_blocks * members
    tiles = inner_blocks // LANES
    own_rows = own_blocks // LANES * COMPS
    outs = pl.pallas_call(
        functools.partial(pair_kernel, members, slots),
        out_shape=(jax.ShapeDtypeStruct((2 * own_rows + RIM_ROWS, LANES), jnp.float32),) * rings,
        in_specs=[vmem] * (rings + 1),
        out_specs=(vmem,) * rings,
        scratch_shapes=[
            pltpu.VMEM((inner_blocks + 3 * RIM, LANES), jnp.float32),
            pltpu.VMEM((2 * slots // CHUNK, LANES), jnp.int32),
            pltpu.SMEM((2 * slots // CHUNK, LANES), jnp.int32),
            pltpu.VMEM((2 * CHUNK, LANES), jnp.float32),
            pltpu.VMEM((27 * slots + 8, LANES), jnp.float32),
            pltpu.VMEM((8 * LANES, 2 * LANES), jnp.float32),
            pltpu.VMEM((4 * 64, 2 * LANES), jnp.float32),
            pltpu.VMEM((192, 2 * LANES), jnp.float32),
            pltpu.VMEM(((tiles + 3) * 24, LANES), jnp.float32),
            pltpu.VMEM(((tiles + 3) * 48, LANES), jnp.float32),
            pltpu.SemaphoreType.DMA,
        ],
        compiler_params=pltpu.CompilerParams(vmem_limit_bytes=32 << 20),
        name="pair_kernel",
    )(*pieces, offset_rows)

    column = outs[0]
    for k, out in list(zip(order, outs))[:0:-1]:
        column = column + trade(out, k)
    in_low = far == 0
    low, high = column[:own_rows], column[own_rows : 2 * own_rows]
    rim = column[2 * own_rows :]
    other = trade(jnp.where(in_low, high, low), rings)
    rim_a = cross(rim, 1, 0)
    rim_b = cross(rim, -1, rings)
    shares = [jnp.where(in_low, low, high), other, rim_a, rim_b]
    clump_force, clump_torque = pl.pallas_call(
        functools.partial(finish_kernel, members, groups),
        out_shape=(jax.ShapeDtypeStruct((3, clumps), jnp.float32),) * 2,
        in_specs=[vmem] * 5,
        out_specs=(vmem, vmem),
        scratch_shapes=[pltpu.VMEM((own_rows, LANES), jnp.float32)],
        compiler_params=pltpu.CompilerParams(vmem_limit_bytes=4 << 20),
        name="finish_kernel",
    )(*shares, positions)
    return (clump_force, clump_torque)


def solution(mesh):
    placed = (
        P(None, ("grp", "dev")),
        P(None, ("grp", "dev")),
        P(("grp", "dev")),
        P(),
        P(None, ("grp", "dev")),
        P(("grp", "dev")),
    )
    return jax.shard_map(
        whole_step,
        mesh=mesh,
        in_specs=placed,
        out_specs=(P(None, ("grp", "dev")), P(None, ("grp", "dev"))),
        check_vma=False,
    )
```
